32 devices in a mesh: prow: 4 (over x, core), pcol: 8 (over z, y).
Axes of the slice: x: 2, y: 2, z: 4, core: 2. Of those that a mesh axis runs over, the one named last changes fastest.
Arguments:
- coords: int32 [3, 8192], P(None, ('prow', 'pcol')), may hold values from 0 to 1023
- block_map: int32 [64], replicated, may hold values from 0 to 63, each once
- pattern: int32 [2, 64], replicated, may hold values 0 or 1
Outputs:
- factor: float32 [16, 4, 128, 8, 8, 128], P(None, 'prow', None, None, 'pcol')
The draws below stay inside these ranges and needn't reach their ends.
Inputs may be any that keep to these rules, and one draw needn't show every extreme that they name: `block_map`: every block number appears once.
All inputs are finite; a program needn't handle non-finite values.
Results may differ from the reference program's by a relative error of at most 0.0001.
Values sent between devices are 32-bit elements; how exact they have to be, the bound alone decides.
No kernel may reach another device: no remote copies, remote signals or barrier semaphores. Data moves between devices by JAX's collectives and lax.ppermute only.
A program may use at most 128 MiB of HBM per device.

```python
import jax
import jax.numpy as jnp
from jax import lax

BLOCK = 128
SNODE_BLOCKS = 4
PANELS = 2
LR = 16
NB = 64
LC = 8
FRONT = 8192
N_PROW = 4
N_PCOL = 8


def set_ends(array, rng, smallest, top_value):
    index_at = [jax.random.randint(jax.random.fold_in(rng, axis), (), 0, length) for axis, length in enumerate(array.shape)]
    main_axis = array.shape.index(max(array.shape))
    next_to = index_at[:main_axis] + [(index_at[main_axis] + 1) % array.shape[main_axis]] + index_at[main_axis + 1:]
    return array.at[tuple(index_at)].set(smallest).at[tuple(next_to)].set(top_value)


def setup_inputs(seed: int = 0) -> dict:
    seeds = jax.random.split(jax.random.key(seed), 4)
    coords = set_ends(jax.random.randint(seeds[0], (3, FRONT), 0, 1024), jax.random.fold_in(seeds[0], 1), 0, 1023).astype(jnp.int32)
    block_map = jax.random.permutation(seeds[1], NB).astype(jnp.int32)
    pattern = set_ends((jax.random.randint(seeds[2], (PANELS, NB), 0, 2) < 1).astype(jnp.int32), jax.random.fold_in(seeds[2], 1), 0, 1)
    return {"coords": coords, "block_map": block_map, "pattern": pattern}


spread_factor = 89.0
scale_gain = 8.0

def lookup(table, index):
    spots = jnp.arange(table.shape[-1], dtype=jnp.int32)
    return lax.optimization_barrier(jnp.sum(jnp.where(index[..., None] == spots, table, 0), axis=-1))

def member(panel_at, ids, pattern):
    first = panel_at * SNODE_BLOCKS
    stop = first + SNODE_BLOCKS
    value = lookup(pattern[panel_at], ids)
    own = (ids >= first) & (ids < stop)
    before = ids < first
    return jnp.where(own, 1, jnp.where(before, 0, value)).astype(jnp.float32)

def block_mask(row_ids, col_ids, pattern):
    weight = (row_ids[:, None] == col_ids[None, :]).astype(jnp.float32)
    for panel_at in range(PANELS):
        row_in = member(panel_at, row_ids, pattern)
        col_in = member(panel_at, col_ids, pattern)
        weight = weight + row_in[:, None] * col_in[None, :]
    return weight

def wendland(dist_sq, radius):
    ratio = jnp.sqrt(dist_sq) / radius
    rest = jnp.maximum(1.0 - ratio, 0.0)
    rest_sq = rest * rest
    return rest_sq * rest_sq * rest_sq * ((35.0 * ratio + 18.0) * ratio + 3.0) * (1.0 / 3.0)

def reference(coords, block_map, pattern):
    nblocks = NB
    front = NB * BLOCK
    radius = (spread_factor / front) ** (1.0 / 3.0)
    inverse = jnp.zeros((nblocks,), jnp.int32).at[block_map].set(jnp.arange(nblocks, dtype=jnp.int32))
    placed = coords.reshape(3, nblocks, BLOCK)[:, inverse, :]
    points = placed.reshape(3, front).astype(jnp.float32) * (1.0 / 1024.0)
    ids = jnp.arange(nblocks, dtype=jnp.int32)
    mask = block_mask(ids, ids, pattern)
    mask_full = jnp.repeat(mask, BLOCK, axis=1)
    row_blocks = points.reshape(3, nblocks, BLOCK).transpose(1, 0, 2)

    def one_row(inputs):
        rows_here, mask_row = inputs
        dist = (rows_here[0][:, None] - points[0][None, :]) ** 2
        dist = dist + (rows_here[1][:, None] - points[1][None, :]) ** 2
        dist = dist + (rows_here[2][:, None] - points[2][None, :]) ** 2
        return wendland(dist, radius) * mask_row[None, :]
    coupling = lax.map(one_row, (row_blocks, mask_full)).reshape(front, front)
    scale = scale_gain * lax.rsqrt(1.0 + lax.optimization_barrier(jnp.sum(coupling, axis=1)))
    matrix = coupling * scale[:, None] * scale[None, :] + jnp.eye(front, dtype=jnp.float32)
    width = SNODE_BLOCKS * BLOCK
    for panel_at in range(PANELS):
        start = panel_at * width
        stop = start + width
        lower = jnp.linalg.cholesky(matrix[start:stop, start:stop])
        rows_block = matrix[start:, start:stop]
        factor_rows = lax.linalg.triangular_solve(lower, rows_block, left_side=False, lower=True, transpose_a=True)
        matrix = matrix.at[start:, start:stop].set(factor_rows)
        matrix = matrix.at[start:stop, stop:].set(0.0)
        trail = factor_rows[width:]
        matrix = matrix.at[stop:, stop:].add(-jnp.dot(trail, trail.T, precision=lax.Precision.HIGHEST))
    return matrix.reshape(LR, N_PROW, BLOCK, LC, N_PCOL, BLOCK)
```

```python
import functools

import jax
import jax.numpy as jnp
from jax import lax
from jax.experimental import pallas as pl
from jax.experimental.pallas import tpu as pltpu
from jax.sharding import PartitionSpec as P

BLOCK = 128
SNODE_BLOCKS = 4
PANELS = 2
LEAD = PANELS * SNODE_BLOCKS
WIDTH = SNODE_BLOCKS * BLOCK

spread_factor = 89.0
scale_gain = 8.0
grid_step = 1024.0

LOW, HIGH = 0.98, 66.0

f32 = jnp.float32
bf16 = jnp.bfloat16
NN = (((1,), (0,)), ((), ()))
NT = (((1,), (1,)), ((), ()))
TN = (((0,), (0,)), ((), ()))
FEATURES = 32
VMEM_BYTES = 60 * 1024 * 1024


def mm(a, b, dims):
    return lax.dot_general(a, b, dims, preferred_element_type=f32)


def split(a):
    high = a.astype(bf16)
    low = (a - high.astype(f32)).astype(bf16)
    return high, low


def dot1(a, b, dims=NN):
    return mm(a.astype(bf16), b.astype(bf16), dims)


def dot3(a, b, dims=NN):
    a_high, a_low = split(a)
    b_high, b_low = split(b)
    return mm(a_high, b_high, dims) + (mm(a_high, b_low, dims) + mm(a_low, b_high, dims))


def eye(n):
    return (lax.broadcasted_iota(jnp.int32, (n, n), 0) == lax.broadcasted_iota(jnp.int32, (n, n), 1)).astype(f32)


def newton(blocks, n):
    first = 2 / (LOW + HIGH)
    rho = (HIGH - LOW) / (HIGH + LOW)
    one = eye(n)
    step = 2 / (2 - rho * rho)
    rho = rho * rho / (2 - rho * rho)
    found = [(2 * step * first) * one - (step * first * first) * a for a in blocks]
    for at in range(5):
        dot = dot1 if at < 2 else dot3
        step = 2 / (2 - rho * rho) if at < 4 else 1.0
        rho = rho * rho / (2 - rho * rho)
        rest = [(2 * one) - dot(a, x) for a, x in zip(blocks, found)]
        found = [step * dot(x, e) for x, e in zip(found, rest)]
    return found


def chains(work, count):
    sub = lax.broadcasted_iota(jnp.int32, (8, BLOCK), 0)
    zero = jnp.zeros((8, BLOCK), f32)
    for strip in range(BLOCK // 8):
        at = 8 * strip
        state = []
        for b in range(count):
            r = work[b][at : at + 8, 0:BLOCK]
            y = work[b][at : at + 8, BLOCK : 2 * BLOCK]
            c = [jnp.broadcast_to(r[:, at + k : at + k + 1], (8, BLOCK)) for k in range(8)]
            state.append([r, y, c])
        for k in range(8):
            for b in range(count):
                r, y, c = state[b]
                inv = lax.rsqrt(c[k][k : k + 1, :])
                column = c[k] * inv
                below = jnp.where(sub > k, column, 0.0)
                r_row = r[k : k + 1] * inv
                y_row = y[k : k + 1] * inv
                r = jnp.where(sub == k, r_row, r - below * r_row)
                y = jnp.where(sub == k, y_row, y - below * y_row)
                for m in range(k + 1, 8):
                    c[m] = c[m] - below * column[m : m + 1, :]
                state[b] = [r, y, c]
        for b in range(count):
            r, y, _ = state[b]
            work[b][at : at + 8, 0:BLOCK] = r
            work[b][at : at + 8, BLOCK : 2 * BLOCK] = y
            if strip < BLOCK // 8 - 1:
                r_high = r.astype(bf16).astype(f32)
                y_high = y.astype(bf16).astype(f32)
                high = jnp.concatenate([r_high, y_high], 1)
                low = jnp.concatenate([r - r_high, y - y_high], 1)
                left = jnp.concatenate([r_high, r_high, r - r_high, zero], 0).astype(bf16)
                right = jnp.concatenate([high, low, high, jnp.concatenate([zero, zero], 1)], 0).astype(bf16)
                update = mm(left, right, TN)
                work[b][at + 8 :, :] = work[b][at + 8 :, :] - update[at + 8 :, :]


def factor_diagonal(a_ref, x_ref, work):
    half = 2 * BLOCK
    rows = lax.broadcasted_iota(jnp.int32, (BLOCK, BLOCK), 0)
    cols = lax.broadcasted_iota(jnp.int32, (BLOCK, BLOCK), 1)
    lower = cols <= rows
    a11 = a_ref[0:half, 0:half]
    a21 = a_ref[half:, 0:half]
    s2 = a_ref[half:, half:] - dot3(dot3(a21, newton([a11], half)[0]), a21, NT)
    corner = [a11[0:BLOCK, 0:BLOCK], s2[0:BLOCK, 0:BLOCK]]
    side = [a11[BLOCK:, 0:BLOCK], s2[BLOCK:, 0:BLOCK]]
    last = [a11[BLOCK:, BLOCK:], s2[BLOCK:, BLOCK:]]
    inverse = newton(corner, BLOCK)
    for i in range(2):
        work[2 * i][:, 0:BLOCK] = corner[i]
        work[2 * i + 1][:, 0:BLOCK] = last[i] - dot3(dot3(side[i], inverse[i]), side[i], NT)
    for b in range(4):
        work[b][:, BLOCK:] = eye(BLOCK)
    chains(work, 4)
    for i in range(2):
        at = half * i
        xa = jnp.where(lower, work[2 * i][:, BLOCK:], 0.0)
        xb = jnp.where(lower, work[2 * i + 1][:, BLOCK:], 0.0)
        l21 = dot3(side[i], xa, NT)
        x_ref[at : at + BLOCK, at : at + BLOCK] = xa
        x_ref[at : at + BLOCK, at + BLOCK : at + half] = jnp.zeros((BLOCK, BLOCK), f32)
        x_ref[at + BLOCK : at + half, at : at + BLOCK] = -dot3(xb, dot3(l21, xa))
        x_ref[at + BLOCK : at + half, at + BLOCK : at + half] = xb
    x11 = x_ref[0:half, 0:half]
    x22 = x_ref[half:, half:]
    l21 = dot3(a21, x11, NT)
    x_ref[half:, 0:half] = -dot3(x22, dot3(l21, x11))
    x_ref[0:half, half:] = jnp.zeros((half, half), f32)


def pieces(point):
    low = (point & 255).astype(f32)
    mid = ((point >> 8) & 255).astype(f32)
    top = (point >> 16).astype(f32)
    return low, mid, top


def left_features(point):
    low, mid, top = pieces(point)
    norm = lax.broadcasted_iota(jnp.int32, point.shape, 0) == 3
    one = jnp.ones_like(low)
    zero = jnp.zeros_like(low)
    return jnp.concatenate(
        [low, jnp.where(norm, one, low), mid, jnp.where(norm, one, mid), top, jnp.where(norm, one, zero), zero, zero], 0
    ).astype(bf16)


def right_features(point):
    low, mid, top = pieces(point)
    norm = lax.broadcasted_iota(jnp.int32, point.shape, 0) == 3
    one = jnp.ones_like(low)
    zero = jnp.zeros_like(low)
    return jnp.concatenate(
        [
            jnp.where(norm, one, -2.0 * low),
            jnp.where(norm, low, -512.0 * mid),
            jnp.where(norm, 256.0 * one, -512.0 * low),
            jnp.where(norm, 256.0 * mid, -131072.0 * mid),
            jnp.where(norm, 65536.0 * one, zero),
            jnp.where(norm, 65536.0 * top, zero),
            zero,
            zero,
        ],
        0,
    ).astype(bf16)


def wendland(dist_sq, radius):
    unit = 1.0 / (grid_step * radius)
    dist = dist_sq * lax.rsqrt(jnp.maximum(dist_sq, 1.0))
    rest = jnp.maximum(1.0 - unit * dist, 0.0)
    rest_sq = rest * rest
    return (rest_sq * rest_sq) * (rest_sq * (((35.0 / 3.0 * unit * unit) * dist + 6.0 * unit) * dist + 1.0))


def member(panel_at, block, pattern):
    first = panel_at * SNODE_BLOCKS
    own = (block >= first) & (block < first + SNODE_BLOCKS)
    return jnp.where(own, 1, jnp.where(block < first, 0, pattern[panel_at, block]))


def weight(row, col, pattern):
    value = (row == col).astype(jnp.int32)
    for panel_at in range(PANELS):
        value = value + member(panel_at, row, pattern) * member(panel_at, col, pattern)
    return value.astype(f32)


GROUP = 8


def sums_kernel(radius, per, block_map, pattern, points, out, left, lists, weights):
    nblocks = points.shape[0]
    me = lax.axis_index("prow") * lax.axis_size("pcol") + lax.axis_index("pcol")
    own = [block_map[me * per + b] for b in range(per)]
    right = [right_features(points[me * per + b]) for b in range(per)]

    def scan_block(m, counts):
        left[m] = left_features(points[m])
        after = []
        for b in range(per):
            value = weight(own[b], block_map[m], pattern)
            lists[b, counts[b]] = m
            weights[b, counts[b]] = value
            after.append(counts[b] + (value > 0).astype(jnp.int32))
        return tuple(after)

    counts = lax.fori_loop(0, nblocks, scan_block, (0,) * per)
    for b in range(per):
        for g in range(GROUP):
            lists[b, counts[b] + g] = 0
            weights[b, counts[b] + g] = 0.0

    for b in range(per):

        def group(step, total):
            parts = []
            for g in range(GROUP):
                at = step * GROUP + g
                value = wendland(mm(left[lists[b, at]], right[b], TN), radius)
                parts.append(jnp.sum(value.reshape(BLOCK // 8, 8, BLOCK), axis=0) * weights[b, at])
            return total + functools.reduce(lambda x, y: x + y, parts)

        total = lax.fori_loop(0, (counts[b] + GROUP - 1) // GROUP, group, jnp.zeros((8, BLOCK), f32))
        row = jnp.sum(total, axis=0, keepdims=True)
        for d in range(out.shape[0]):
            out[d, b : b + 1, :] = row


def panels_kernel(
    radius, rows_n, cols_n, block_map, pattern, points, totals, out,
    inverse, panel, left, right_lead, right_cols, scale_rows, scale_lead, scale_cols,
    x_high, x_low, s_high, s_low, x_full, cols_high, cols_low, stage, sems, *work,
):
    nblocks = points.shape[0]
    row_count = nblocks // rows_n
    col_count = nblocks // cols_n
    prow_at = lax.axis_index("prow")
    pcol_at = lax.axis_index("pcol")
    col_base = row_count
    next_base = row_count + col_count
    lead_base = next_base + SNODE_BLOCKS
    slots = lead_base + SNODE_BLOCKS

    def block_of(slot):
        lead = jnp.where(slot < lead_base, slot - next_base + SNODE_BLOCKS, slot - lead_base)
        col = (slot - col_base) * cols_n + pcol_at
        return jnp.where(slot < col_base, slot * rows_n + prow_at, jnp.where(slot < next_base, col, lead))

    def invert(m, carry):
        inverse[block_map[m]] = m
        return carry

    lax.fori_loop(0, nblocks, invert, 0)

    def prepare(slot, carry):
        m = inverse[block_of(slot)]
        left[slot] = left_features(points[m])
        scale = scale_gain * lax.rsqrt(1.0 + totals[pl.ds(m, 1), :])
        scale_rows[slot] = jnp.broadcast_to(scale, (BLOCK, BLOCK)).T
        return carry

    lax.fori_loop(0, slots, prepare, 0)
    for j in range(LEAD):
        m = inverse[j]
        right_lead[:, j * BLOCK : (j + 1) * BLOCK] = right_features(points[m])
        scale_lead[j : j + 1, :] = scale_gain * lax.rsqrt(1.0 + totals[pl.ds(m, 1), :])
    for k in range(col_count):
        m = inverse[k * cols_n + pcol_at]
        right_cols[:, k * BLOCK : (k + 1) * BLOCK] = right_features(points[m])
        scale_cols[k : k + 1, :] = scale_gain * lax.rsqrt(1.0 + totals[pl.ds(m, 1), :])

    def couple(slot, carry):
        g = block_of(slot)
        value = wendland(mm(left[slot], right_lead[...], TN), radius)
        at = pl.ds(pl.multiple_of(slot * BLOCK, BLOCK), BLOCK)
        for j in range(LEAD):
            lanes = slice(j * BLOCK, (j + 1) * BLOCK)
            factor = scale_lead[j : j + 1, :] * weight(g, j, pattern)
            panel[at, lanes] = value[:, lanes] * scale_rows[slot] * factor

        @pl.when(g < LEAD)
        def _():
            lanes = pl.ds(pl.multiple_of(g * BLOCK, BLOCK), BLOCK)
            panel[at, lanes] = panel[at, lanes] + eye(BLOCK)

        return carry

    lax.fori_loop(0, slots, couple, 0)

    chunk = 4 * BLOCK
    factor_diagonal(panel.at[pl.ds(lead_base * BLOCK, WIDTH), pl.ds(0, WIDTH)], x_full, work)
    x_high[...], x_low[...] = split(x_full[...])

    def rows_of(c):
        return pl.ds(pl.multiple_of(c * chunk, chunk), chunk)

    def dot3_with(a, high, low):
        a_high, a_low = split(a)
        return mm(a_high, high, NT) + (mm(a_high, low, NT) + mm(a_low, high, NT))

    def solve_first(c, carry):
        panel[rows_of(c), 0:WIDTH] = dot3_with(panel[rows_of(c), 0:WIDTH], x_high[...], x_low[...])
        return carry

    lax.fori_loop(0, lead_base * BLOCK // chunk, solve_first, 0)
    next_rows = pl.ds(next_base * BLOCK, WIDTH)
    s_high[...], s_low[...] = split(panel[next_rows, 0:WIDTH])
    panel[next_rows, WIDTH:] = panel[next_rows, WIDTH:] - dot3_with(panel[next_rows, 0:WIDTH], s_high[...], s_low[...])
    factor_diagonal(panel.at[next_rows, pl.ds(WIDTH, WIDTH)], x_full, work)
    x_high[...], x_low[...] = split(x_full[...])

    def solve_second(c, carry):
        rest = panel[rows_of(c), WIDTH:] - dot3_with(panel[rows_of(c), 0:WIDTH], s_high[...], s_low[...])
        panel[rows_of(c), WIDTH:] = dot3_with(rest, x_high[...], x_low[...])
        return carry

    lax.fori_loop(0, next_base * BLOCK // chunk, solve_second, 0)
    for i in range(row_count):
        if i * rows_n < SNODE_BLOCKS:

            @pl.when(i * rows_n + prow_at < SNODE_BLOCKS)
            def _(i=i):
                panel[i * BLOCK : (i + 1) * BLOCK, WIDTH:] = jnp.zeros((BLOCK, WIDTH), f32)

    def split_cols(k, carry):
        src = pl.ds(pl.multiple_of((col_base + k) * BLOCK, BLOCK), BLOCK)
        dst = pl.ds(pl.multiple_of(k * BLOCK, BLOCK), BLOCK)
        cols_high[dst, :], cols_low[dst, :] = split(panel[src, :])
        return carry

    lax.fori_loop(0, col_count, split_cols, 0)

    per_slot = BLOCK * col_count
    pair = 2

    def copy_out(step, half):
        at = pl.multiple_of(step * (pair * per_slot), pair * per_slot)
        return pltpu.make_async_copy(stage.at[half], out.at[pl.ds(at, pair * per_slot), :], sems.at[half])

    def trail(step, carry):
        half = step % 2

        @pl.when(step >= 2)
        def _():
            copy_out(step - 2, half).wait()

        at = pl.ds(pl.multiple_of(step * pair * BLOCK, BLOCK), pair * BLOCK)
        update = dot3_with(panel[at, :], cols_high[...], cols_low[...])
        for q in range(pair):
            slot = step * pair + q
            g = block_of(slot)
            keep = (g >= LEAD).astype(f32)
            rows = pl.ds(pl.multiple_of(slot * BLOCK, BLOCK), BLOCK)
            value = wendland(mm(left[slot], right_cols[...], TN), radius)
            for k in range(col_count):
                j = k * cols_n + pcol_at
                lanes = slice(k * BLOCK, (k + 1) * BLOCK)
                factor = scale_cols[k : k + 1, :] * weight(g, j, pattern)
                tile = value[:, lanes] * scale_rows[slot] * factor
                tile = (tile - update[q * BLOCK : (q + 1) * BLOCK, lanes]) * keep
                spots = pl.ds(q * per_slot + k, BLOCK, stride=col_count)
                stage[half, spots, :] = tile
                if k * cols_n < LEAD:

                    @pl.when(j < LEAD)
                    def _(j=j, spots=spots):
                        where = pl.ds(pl.multiple_of(j * BLOCK, BLOCK), BLOCK)
                        stage[half, spots, :] = panel[rows, where]

                @pl.when((j == g) & (j >= LEAD))
                def _(spots=spots):
                    stage[half, spots, :] = stage[half, spots, :] + eye(BLOCK)

        copy_out(step, half).start()
        return carry

    steps = row_count // pair
    lax.fori_loop(0, steps, trail, 0)
    for step in range(max(steps - 2, 0), steps):
        copy_out(step, step % 2).wait()


def local(coords, block_map, pattern):
    rows_n = lax.axis_size("prow")
    cols_n = lax.axis_size("pcol")
    devices = rows_n * cols_n
    nblocks = block_map.shape[0]
    per = nblocks // devices
    row_count = nblocks // rows_n
    col_count = nblocks // cols_n
    radius = (spread_factor / (nblocks * BLOCK)) ** (1.0 / 3.0)
    slots = row_count + col_count + LEAD
    axes = ("prow", "pcol")
    mine = jnp.concatenate([coords, jnp.sum(coords * coords, axis=0, keepdims=True)], 0)
    mine = mine.reshape(4, per, BLOCK).transpose(1, 0, 2)
    points = lax.all_to_all(jnp.broadcast_to(mine[None], (devices, per, 4, BLOCK)), axes, 0, 0, tiled=True)
    points = points.reshape(nblocks, 4, BLOCK)
    smem = pl.BlockSpec(memory_space=pltpu.SMEM)
    vmem = pl.BlockSpec(memory_space=pltpu.VMEM)
    params = pltpu.CompilerParams(vmem_limit_bytes=VMEM_BYTES)
    sums = pl.pallas_call(
        functools.partial(sums_kernel, radius, per),
        out_shape=jax.ShapeDtypeStruct((devices, per, BLOCK), f32),
        in_specs=[smem, smem, vmem],
        out_specs=vmem,
        scratch_shapes=[
            pltpu.VMEM((nblocks, FEATURES, BLOCK), bf16),
            pltpu.SMEM((per, nblocks + GROUP), jnp.int32),
            pltpu.SMEM((per, nblocks + GROUP), f32),
        ],
        compiler_params=params,
        name="sums",
    )(block_map, pattern, points)
    totals = lax.all_to_all(sums, axes, 0, 0, tiled=True).reshape(nblocks, BLOCK)
    out = pl.pallas_call(
        functools.partial(panels_kernel, radius, rows_n, cols_n),
        out_shape=jax.ShapeDtypeStruct((row_count * BLOCK * col_count, BLOCK), f32),
        in_specs=[smem, smem, vmem, vmem],
        out_specs=pl.BlockSpec(memory_space=pl.ANY),
        scratch_shapes=[
            pltpu.SMEM((nblocks,), jnp.int32),
            pltpu.VMEM((slots * BLOCK, PANELS * WIDTH), f32),
            pltpu.VMEM((slots, FEATURES, BLOCK), bf16),
            pltpu.VMEM((FEATURES, LEAD * BLOCK), bf16),
            pltpu.VMEM((FEATURES, col_count * BLOCK), bf16),
            pltpu.VMEM((slots, BLOCK, BLOCK), f32),
            pltpu.VMEM((LEAD, BLOCK), f32),
            pltpu.VMEM((col_count, BLOCK), f32),
            pltpu.VMEM((WIDTH, WIDTH), bf16),
            pltpu.VMEM((WIDTH, WIDTH), bf16),
            pltpu.VMEM((WIDTH, WIDTH), bf16),
            pltpu.VMEM((WIDTH, WIDTH), bf16),
            pltpu.VMEM((WIDTH, WIDTH), f32),
            pltpu.VMEM((col_count * BLOCK, PANELS * WIDTH), bf16),
            pltpu.VMEM((col_count * BLOCK, PANELS * WIDTH), bf16),
            pltpu.VMEM((2, 2 * BLOCK * col_count, BLOCK), f32),
            pltpu.SemaphoreType.DMA((2,)),
        ]
        + [pltpu.VMEM((BLOCK, 2 * BLOCK), f32)] * 4,
        compiler_params=params,
        name="panels",
    )(block_map, pattern, points, totals)
    return out.reshape(row_count, 1, BLOCK, col_count, 1, BLOCK)


def solution(mesh):
    placed = (P(None, ("prow", "pcol")), P(), P())
    return jax.shard_map(
        local,
        mesh=mesh,
        in_specs=placed,
        out_specs=P(None, "prow", None, None, "pcol", None),
        check_vma=False,
    )
```

```python
import functools

import jax
import jax.numpy as jnp
from jax import lax
from jax.experimental import pallas as pl
from jax.experimental.pallas import tpu as pltpu
from jax.sharding import PartitionSpec as P

BLOCK = 128
SNODE_BLOCKS = 4
PANELS = 2
LEAD = PANELS * SNODE_BLOCKS
WIDTH = SNODE_BLOCKS * BLOCK

spread_factor = 89.0
scale_gain = 8.0
grid_step = 1024.0

LOW, HIGH = 0.98, 66.0

f32 = jnp.float32
bf16 = jnp.bfloat16
NN = (((1,), (0,)), ((), ()))
NT = (((1,), (1,)), ((), ()))
TN = (((0,), (0,)), ((), ()))
FEATURES = 32
VMEM_BYTES = 60 * 1024 * 1024


def mm(a, b, dims):
    return lax.dot_general(a, b, dims, preferred_element_type=f32)


def split(a):
    high = a.astype(bf16)
    low = (a - high.astype(f32)).astype(bf16)
    return high, low


def dot1(a, b, dims=NN):
    return mm(a.astype(bf16), b.astype(bf16), dims)


def dot3(a, b, dims=NN):
    a_high, a_low = split(a)
    b_high, b_low = split(b)
    return mm(a_high, b_high, dims) + (mm(a_high, b_low, dims) + mm(a_low, b_high, dims))


def eye(n):
    return (lax.broadcasted_iota(jnp.int32, (n, n), 0) == lax.broadcasted_iota(jnp.int32, (n, n), 1)).astype(f32)


def newton(blocks, n):
    first = 2 / (LOW + HIGH)
    rho = (HIGH - LOW) / (HIGH + LOW)
    one = eye(n)
    step = 2 / (2 - rho * rho)
    rho = rho * rho / (2 - rho * rho)
    found = [(2 * step * first) * one - (step * first * first) * a for a in blocks]
    for at in range(5):
        dot = dot1 if at < 2 else dot3
        step = 2 / (2 - rho * rho) if at < 4 else 1.0
        rho = rho * rho / (2 - rho * rho)
        rest = [(2 * one) - dot(a, x) for a, x in zip(blocks, found)]
        found = [step * dot(x, e) for x, e in zip(found, rest)]
    return found


def chains(work, count):
    sub = lax.broadcasted_iota(jnp.int32, (8, BLOCK), 0)
    zero = jnp.zeros((8, BLOCK), f32)
    for strip in range(BLOCK // 8):
        at = 8 * strip
        state = []
        for b in range(count):
            r = work[b][at : at + 8, 0:BLOCK]
            y = work[b][at : at + 8, BLOCK : 2 * BLOCK]
            c = [jnp.broadcast_to(r[:, at + k : at + k + 1], (8, BLOCK)) for k in range(8)]
            state.append([r, y, c])
        for k in range(8):
            for b in range(count):
                r, y, c = state[b]
                inv = lax.rsqrt(c[k][k : k + 1, :])
                column = c[k] * inv
                below = jnp.where(sub > k, column, 0.0)
                r_row = r[k : k + 1] * inv
                y_row = y[k : k + 1] * inv
                r = jnp.where(sub == k, r_row, r - below * r_row)
                y = jnp.where(sub == k, y_row, y - below * y_row)
                for m in range(k + 1, 8):
                    c[m] = c[m] - below * column[m : m + 1, :]
                state[b] = [r, y, c]
        for b in range(count):
            r, y, _ = state[b]
            work[b][at : at + 8, 0:BLOCK] = r
            work[b][at : at + 8, BLOCK : 2 * BLOCK] = y
            if strip < BLOCK // 8 - 1:
                r_high = r.astype(bf16).astype(f32)
                y_high = y.astype(bf16).astype(f32)
                high = jnp.concatenate([r_high, y_high], 1)
                low = jnp.concatenate([r - r_high, y - y_high], 1)
                left = jnp.concatenate([r_high, r_high, r - r_high, zero], 0).astype(bf16)
                right = jnp.concatenate([high, low, high, jnp.concatenate([zero, zero], 1)], 0).astype(bf16)
                update = mm(left, right, TN)
                work[b][at + 8 :, :] = work[b][at + 8 :, :] - update[at + 8 :, :]


def factor_diagonal(a_ref, x_ref, work):
    half = 2 * BLOCK
    rows = lax.broadcasted_iota(jnp.int32, (BLOCK, BLOCK), 0)
    cols = lax.broadcasted_iota(jnp.int32, (BLOCK, BLOCK), 1)
    lower = cols <= rows
    a11 = a_ref[0:half, 0:half]
    a21 = a_ref[half:, 0:half]
    s2 = a_ref[half:, half:] - dot3(dot3(a21, newton([a11], half)[0]), a21, NT)
    corner = [a11[0:BLOCK, 0:BLOCK], s2[0:BLOCK, 0:BLOCK]]
    side = [a11[BLOCK:, 0:BLOCK], s2[BLOCK:, 0:BLOCK]]
    last = [a11[BLOCK:, BLOCK:], s2[BLOCK:, BLOCK:]]
    inverse = newton(corner, BLOCK)
    for i in range(2):
        work[2 * i][:, 0:BLOCK] = corner[i]
        work[2 * i + 1][:, 0:BLOCK] = last[i] - dot3(dot3(side[i], inverse[i]), side[i], NT)
    for b in range(4):
        work[b][:, BLOCK:] = eye(BLOCK)
    chains(work, 4)
    for i in range(2):
        at = half * i
        xa = jnp.where(lower, work[2 * i][:, BLOCK:], 0.0)
        xb = jnp.where(lower, work[2 * i + 1][:, BLOCK:], 0.0)
        l21 = dot3(side[i], xa, NT)
        x_ref[at : at + BLOCK, at : at + BLOCK] = xa
        x_ref[at : at + BLOCK, at + BLOCK : at + half] = jnp.zeros((BLOCK, BLOCK), f32)
        x_ref[at + BLOCK : at + half, at : at + BLOCK] = -dot3(xb, dot3(l21, xa))
        x_ref[at + BLOCK : at + half, at + BLOCK : at + half] = xb
    x11 = x_ref[0:half, 0:half]
    x22 = x_ref[half:, half:]
    l21 = dot3(a21, x11, NT)
    x_ref[half:, 0:half] = -dot3(x22, dot3(l21, x11))
    x_ref[0:half, half:] = jnp.zeros((half, half), f32)


def pieces(point):
    low = (point & 255).astype(f32)
    mid = ((point >> 8) & 255).astype(f32)
    top = (point >> 16).astype(f32)
    return low, mid, top


def left_features(point):
    low, mid, top = pieces(point)
    norm = lax.broadcasted_iota(jnp.int32, point.shape, 0) == 3
    one = jnp.ones_like(low)
    zero = jnp.zeros_like(low)
    return jnp.concatenate(
        [low, jnp.where(norm, one, low), mid, jnp.where(norm, one, mid), top, jnp.where(norm, one, zero), zero, zero], 0
    ).astype(bf16)


def right_features(point):
    low, mid, top = pieces(point)
    norm = lax.broadcasted_iota(jnp.int32, point.shape, 0) == 3
    one = jnp.ones_like(low)
    zero = jnp.zeros_like(low)
    return jnp.concatenate(
        [
            jnp.where(norm, one, -2.0 * low),
            jnp.where(norm, low, -512.0 * mid),
            jnp.where(norm, 256.0 * one, -512.0 * low),
            jnp.where(norm, 256.0 * mid, -131072.0 * mid),
            jnp.where(norm, 65536.0 * one, zero),
            jnp.where(norm, 65536.0 * top, zero),
            zero,
            zero,
        ],
        0,
    ).astype(bf16)


def shape_of(radius):
    unit = 1.0 / (grid_step * radius)
    shift = 9.0 / (35.0 * unit)
    return {"reach": 1.0 / unit, "shift": shift, "bias": 3.0 / (35.0 * unit * unit) - shift * shift, "gain": 35.0 / 3.0 * unit**8}


def wendland(dist_sq, shape):
    dist = dist_sq * lax.rsqrt(jnp.maximum(dist_sq, 1.0))
    rest = jnp.maximum(shape["reach"] - dist, 0.0)
    rest_sq = rest * rest
    moved = dist + shape["shift"]
    return (rest_sq * rest_sq) * (rest_sq * (moved * moved + shape["bias"]))


def member(panel_at, block, pattern):
    first = panel_at * SNODE_BLOCKS
    own = (block >= first) & (block < first + SNODE_BLOCKS)
    return jnp.where(own, 1, jnp.where(block < first, 0, pattern[panel_at, block]))


def weight(row, col, pattern):
    value = (row == col).astype(jnp.int32)
    for panel_at in range(PANELS):
        value = value + member(panel_at, row, pattern) * member(panel_at, col, pattern)
    return value.astype(f32)


GROUP = 8
UNITS = 4


def sums_kernel(shape, per, block_map, pattern, points, out, left, lists, weights):
    nblocks = points.shape[0]
    me = lax.axis_index("prow") * lax.axis_size("pcol") + lax.axis_index("pcol")
    own = [block_map[me * per + b] for b in range(per)]
    right = [right_features(points[me * per + b]) for b in range(per)]

    def scan_block(m, counts):
        left[m] = left_features(points[m])
        after = []
        for b in range(per):
            value = weight(own[b], block_map[m], pattern)
            lists[b, counts[b]] = m
            weights[b, counts[b]] = value * shape["gain"]
            after.append(counts[b] + (value > 0).astype(jnp.int32))
        return tuple(after)

    counts = lax.fori_loop(0, nblocks, scan_block, (0,) * per)
    for b in range(per):
        for g in range(GROUP):
            lists[b, counts[b] + g] = 0
            weights[b, counts[b] + g] = 0.0

    for b in range(per):

        def group(step, total):
            parts = []
            for g in range(GROUP):
                at = step * GROUP + g
                value = wendland(mm(left[lists[b, at]], right[b], TN), shape)
                parts.append(jnp.sum(value.reshape(BLOCK // 8, 8, BLOCK), axis=0) * weights[b, at])
            return total + functools.reduce(lambda x, y: x + y, parts)

        total = lax.fori_loop(0, (counts[b] + GROUP - 1) // GROUP, group, jnp.zeros((8, BLOCK), f32))
        row = jnp.sum(total, axis=0, keepdims=True)
        for d in range(out.shape[0]):
            out[d, b : b + 1, :] = row


def spread_kernel(per, coords, out):
    for b in range(per):
        point = coords[:, b * BLOCK : (b + 1) * BLOCK]
        norm = jnp.sum(point * point, axis=0, keepdims=True)
        point = jnp.concatenate([point, norm], 0)
        for d in range(out.shape[0]):
            out[d, b] = point


def panels_kernel(
    shape, rows_n, cols_n, block_map, pattern, points, totals, out,
    inverse, table, place, units, panel, left, right_lead, right_cols, scale_rows, scale_lead, scale_cols,
    x_high, x_low, s_high, s_low, x_full, cols_high, cols_low, stage, sems, *work,
):
    nblocks = points.shape[0]
    row_count = nblocks // rows_n
    col_count = nblocks // cols_n
    prow_at = lax.axis_index("prow")
    pcol_at = lax.axis_index("pcol")
    col_base = row_count
    next_base = row_count + col_count
    lead_base = next_base + SNODE_BLOCKS
    slots = lead_base + SNODE_BLOCKS
    lead_rows = LEAD // rows_n

    def invert(m, carry):
        inverse[block_map[m]] = m
        return carry

    lax.fori_loop(0, nblocks, invert, 0)

    def sort(base, blocks, lead):
        kinds = []
        first = second = jnp.int32(0)
        for g, at in blocks:
            in_first = member(0, g, pattern) > 0
            in_second = member(1, g, pattern) > 0
            dead = g < LEAD
            kind = jnp.where(dead, 2, jnp.where(in_first, 0, jnp.where(in_second, 1, 2)))
            kinds.append(kind)
            first = first + (kind == 0).astype(jnp.int32)
            second = second + (kind == 1).astype(jnp.int32)
        spots = [base + lead, base + lead + first, base + lead + first + second]
        for (g, at), kind in zip(blocks, kinds):
            spot = jnp.where(kind == 0, spots[0], jnp.where(kind == 1, spots[1], spots[2]))
            table[spot] = g
            place[spot] = at
            for n in range(3):
                spots[n] = spots[n] + (kind == n).astype(jnp.int32)
        return lead + first, lead + first + second

    for i in range(lead_rows):
        table[i] = i * rows_n + prow_at
        place[i] = i
    rows_first, rows_both = sort(0, [(i * rows_n + prow_at, i) for i in range(lead_rows, row_count)], lead_rows)
    cols_first, cols_both = sort(col_base, [(k * cols_n + pcol_at, k) for k in range(col_count)], 0)
    for j in range(SNODE_BLOCKS):
        table[next_base + j] = SNODE_BLOCKS + j
        table[lead_base + j] = j
    linked = jnp.int32(0)
    for j in range(SNODE_BLOCKS, LEAD):
        linked = linked | (pattern[0, j] > 0).astype(jnp.int32)

    def prepare(slot, carry):
        m = inverse[table[slot]]
        left[slot] = left_features(points[m])
        scale = scale_gain * lax.rsqrt(1.0 + totals[pl.ds(m, 1), :])
        scale_rows[slot] = jnp.broadcast_to(scale, (BLOCK, BLOCK)).T
        return carry

    lax.fori_loop(0, slots, prepare, 0)
    for j in range(LEAD):
        m = inverse[j]
        half, at = divmod(j, SNODE_BLOCKS)
        right_lead[half, :, at * BLOCK : (at + 1) * BLOCK] = right_features(points[m])
        scale_lead[half, at : at + 1, :] = scale_gain * lax.rsqrt(1.0 + totals[pl.ds(m, 1), :])
    for k in range(col_count):
        m = inverse[table[col_base + k]]
        right_cols[k // 2, :, k % 2 * BLOCK : (k % 2 + 1) * BLOCK] = right_features(points[m])
        scale_cols[k : k + 1, :] = scale_gain * lax.rsqrt(1.0 + totals[pl.ds(m, 1), :])

    def block_rows(slot):
        return pl.ds(pl.multiple_of(slot * BLOCK, BLOCK), BLOCK)

    def couple(unit):
        slot = unit // 2
        half = unit % 2
        g = table[slot]
        value = wendland(mm(left[slot], right_lead[half], TN), shape)
        for j in range(SNODE_BLOCKS):
            lanes = slice(j * BLOCK, (j + 1) * BLOCK)
            factor = scale_lead[half, j : j + 1, :] * (weight(g, half * SNODE_BLOCKS + j, pattern) * shape["gain"])
            at = pl.ds(pl.multiple_of(half * WIDTH + j * BLOCK, BLOCK), BLOCK)
            panel[block_rows(slot), at] = value[:, lanes] * scale_rows[slot] * factor

    def list_units(slot, count):
        g = table[slot]
        dead = (slot >= col_base) & (slot < next_base) & (g < LEAD)
        in_first = member(0, g, pattern) > 0
        in_second = (member(1, g, pattern) > 0) | (in_first & (linked > 0)) | (g >= SNODE_BLOCKS) & (g < LEAD)
        for half, used in enumerate((in_first, in_second & (g >= SNODE_BLOCKS))):
            used = used & jnp.logical_not(dead)
            units[count] = 2 * slot + half
            count = count + used.astype(jnp.int32)

            @pl.when(jnp.logical_not(used))
            def _(half=half):
                panel[block_rows(slot), half * WIDTH : (half + 1) * WIDTH] = jnp.zeros((BLOCK, WIDTH), f32)

        return count

    count = lax.fori_loop(0, lead_base, list_units, jnp.int32(0))
    for g in range(UNITS):
        units[count + g] = 2 * lead_base + 1

    for j in range(SNODE_BLOCKS):
        couple(jnp.int32(2 * (lead_base + j)))

    def couple_group(step, carry):
        for g in range(UNITS):
            couple(units[step * UNITS + g])
        return carry

    lax.fori_loop(0, (count + UNITS - 1) // UNITS, couple_group, 0)
    for j in range(SNODE_BLOCKS):
        for base, first in ((lead_base, 0), (next_base, WIDTH)):
            at = slice((base + j) * BLOCK, (base + j + 1) * BLOCK)
            lanes = slice(first + j * BLOCK, first + (j + 1) * BLOCK)
            panel[at, lanes] = panel[at, lanes] + eye(BLOCK)
    for i in range(lead_rows):
        at = slice(i * BLOCK, (i + 1) * BLOCK)
        lanes = pl.ds(pl.multiple_of((i * rows_n + prow_at) * BLOCK, BLOCK), BLOCK)
        panel[at, lanes] = panel[at, lanes] + eye(BLOCK)

    def dot3_with(a, high, low):
        a_high, a_low = split(a)
        return mm(a_high, high, NT) + (mm(a_high, low, NT) + mm(a_low, high, NT))

    middle = WIDTH // 2

    def solve(at, first):
        a = panel[at, first : first + WIDTH]
        upper = dot3_with(a[:, :middle], x_high[:middle, :middle], x_low[:middle, :middle])
        panel[at, first + middle : first + WIDTH] = dot3_with(a, x_high[middle:, :], x_low[middle:, :])
        panel[at, first : first + middle] = upper

    def chunks(rows, cols, body):
        row_chunks = (rows + 1) // 2
        col_chunks = (cols + 1) // 2

        def step(c, carry):
            slot = jnp.where(c < row_chunks, 2 * c, col_base + 2 * (c - row_chunks))
            body(pl.ds(pl.multiple_of(slot * BLOCK, 2 * BLOCK), 2 * BLOCK))
            return carry

        lax.fori_loop(0, row_chunks + col_chunks, step, 0)

    factor_diagonal(panel.at[pl.ds(lead_base * BLOCK, WIDTH), pl.ds(0, WIDTH)], x_full, work)
    x_high[...], x_low[...] = split(x_full[...])
    next_rows = pl.ds(next_base * BLOCK, WIDTH)
    solve(next_rows, 0)
    s_high[...], s_low[...] = split(panel[next_rows, 0:WIDTH])
    panel[next_rows, WIDTH:] = panel[next_rows, WIDTH:] - dot3_with(panel[next_rows, 0:WIDTH], s_high[...], s_low[...])

    def first_rows(at):
        solve(at, 0)
        panel[at, WIDTH:] = panel[at, WIDTH:] - dot3_with(panel[at, 0:WIDTH], s_high[...], s_low[...])

    chunks(rows_first, cols_first, first_rows)
    factor_diagonal(panel.at[next_rows, pl.ds(WIDTH, WIDTH)], x_full, work)
    x_high[...], x_low[...] = split(x_full[...])
    chunks(rows_both, cols_both, lambda at: solve(at, WIDTH))
    for i in range(lead_rows):
        if i * rows_n < SNODE_BLOCKS:

            @pl.when(i * rows_n + prow_at < SNODE_BLOCKS)
            def _(i=i):
                panel[i * BLOCK : (i + 1) * BLOCK, WIDTH:] = jnp.zeros((BLOCK, WIDTH), f32)

    def split_cols(k, carry):
        cols_high[block_rows(k), :], cols_low[block_rows(k), :] = split(panel[block_rows(col_base + k), :])
        return carry

    lax.fori_loop(0, (cols_both + 1) // 2 * 2, split_cols, 0)

    per_slot = BLOCK * col_count
    row_live = (rows_both + 1) // 2
    row_two = (rows_first + 1) // 2
    col_live = (cols_both + 1) // 2
    col_two = (cols_first + 1) // 2

    def copies_out(step, half):
        made = []
        for q in range(2):
            at = pl.multiple_of(place[2 * step + q] * per_slot, per_slot)
            made.append(
                pltpu.make_async_copy(stage.at[half, pl.ds(q * per_slot, per_slot), :], out.at[pl.ds(at, per_slot), :], sems.at[half, q])
            )
        return made

    def trail(step, carry):
        half = step % 2

        @pl.when(step >= 2)
        def _():
            for copy in copies_out(step - 2, half):
                copy.wait()

        def spots(q, k):
            return pl.ds(q * per_slot + k, BLOCK, stride=col_count)

        def tiles(c, carry):
            live = (step < row_live) & (c < col_live) & (step >= lead_rows // 2)
            two = (step < row_two) & (c < col_two)
            row_at = pl.ds(pl.multiple_of(step * 2 * BLOCK, 2 * BLOCK), 2 * BLOCK)
            col_at = pl.ds(pl.multiple_of(c * 2 * BLOCK, 2 * BLOCK), 2 * BLOCK)

            def body(first):
                update = dot3_with(panel[row_at, first:], cols_high[col_at, first:], cols_low[col_at, first:])
                for q in range(2):
                    slot = 2 * step + q
                    g = table[slot]
                    value = wendland(mm(left[slot], right_cols[c], TN), shape)
                    for e in range(2):
                        lanes = slice(e * BLOCK, (e + 1) * BLOCK)
                        spot = col_base + 2 * c + e
                        factor = scale_cols[pl.ds(2 * c + e, 1), :] * (weight(g, table[spot], pattern) * shape["gain"])
                        tile = value[:, lanes] * scale_rows[slot] * factor - update[q * BLOCK : (q + 1) * BLOCK, lanes]
                        if lead_rows % 2:
                            tile = tile * (g >= LEAD).astype(f32)
                        stage[half, spots(q, place[spot]), :] = tile

            @pl.when(live & two)
            def _():
                body(0)

            @pl.when(live & jnp.logical_not(two))
            def _():
                body(WIDTH)

            @pl.when(jnp.logical_not(live))
            def _():
                for q in range(2):
                    for e in range(2):
                        stage[half, spots(q, place[col_base + 2 * c + e]), :] = jnp.zeros((BLOCK, BLOCK), f32)

            return carry

        lax.fori_loop(0, col_count // 2, tiles, 0)
        for q in range(2):
            slot = 2 * step + q
            g = table[slot]
            k_same = g // cols_n
            here = (k_same * cols_n + pcol_at == g) & (g >= LEAD)
            same = spots(q, k_same)

            @pl.when(here & (slot >= rows_both))
            def _(slot=slot, g=g, same=same):
                m = inverse[g]
                value = wendland(mm(left[slot], right_features(points[m]), TN), shape)
                factor = scale_gain * lax.rsqrt(1.0 + totals[pl.ds(m, 1), :]) * (weight(g, g, pattern) * shape["gain"])
                stage[half, same, :] = value * scale_rows[slot] * factor

            @pl.when(here)
            def _(same=same):
                stage[half, same, :] = stage[half, same, :] + eye(BLOCK)

            for k in range(col_count):
                if k * cols_n < LEAD:
                    j = k * cols_n + pcol_at

                    @pl.when(j < LEAD)
                    def _(k=k, j=j, q=q, slot=slot):
                        where = pl.ds(pl.multiple_of(j * BLOCK, BLOCK), BLOCK)
                        stage[half, spots(q, k), :] = panel[block_rows(slot), where]

        for copy in copies_out(step, half):
            copy.start()
        return carry

    steps = row_count // 2
    lax.fori_loop(0, steps, trail, 0)
    for step in range(max(steps - 2, 0), steps):
        for copy in copies_out(step, step % 2):
            copy.wait()


def local(coords, block_map, pattern):
    rows_n = lax.axis_size("prow")
    cols_n = lax.axis_size("pcol")
    devices = rows_n * cols_n
    nblocks = block_map.shape[0]
    per = nblocks // devices
    row_count = nblocks // rows_n
    col_count = nblocks // cols_n
    radius = (spread_factor / (nblocks * BLOCK)) ** (1.0 / 3.0)
    slots = row_count + col_count + LEAD
    axes = ("prow", "pcol")
    smem = pl.BlockSpec(memory_space=pltpu.SMEM)
    vmem = pl.BlockSpec(memory_space=pltpu.VMEM)
    params = pltpu.CompilerParams(vmem_limit_bytes=VMEM_BYTES)
    shape = shape_of(radius)
    mine = pl.pallas_call(
        functools.partial(spread_kernel, per),
        out_shape=jax.ShapeDtypeStruct((devices, per, 4, BLOCK), jnp.int32),
        in_specs=[vmem],
        out_specs=vmem,
        name="spread",
    )(coords)
    points = lax.all_to_all(mine, axes, 0, 0, tiled=True).reshape(nblocks, 4, BLOCK)
    sums = pl.pallas_call(
        functools.partial(sums_kernel, shape, per),
        out_shape=jax.ShapeDtypeStruct((devices, per, BLOCK), f32),
        in_specs=[smem, smem, vmem],
        out_specs=vmem,
        scratch_shapes=[
            pltpu.VMEM((nblocks, FEATURES, BLOCK), bf16),
            pltpu.SMEM((per, nblocks + GROUP), jnp.int32),
            pltpu.SMEM((per, nblocks + GROUP), f32),
        ],
        compiler_params=params,
        name="sums",
    )(block_map, pattern, points)
    totals = lax.all_to_all(sums, axes, 0, 0, tiled=True).reshape(nblocks, BLOCK)
    out = pl.pallas_call(
        functools.partial(panels_kernel, shape, rows_n, cols_n),
        out_shape=jax.ShapeDtypeStruct((row_count * BLOCK * col_count, BLOCK), f32),
        in_specs=[smem, smem, vmem, vmem],
        out_specs=pl.BlockSpec(memory_space=pl.ANY),
        scratch_shapes=[
            pltpu.SMEM((nblocks,), jnp.int32),
            pltpu.SMEM((slots,), jnp.int32),
            pltpu.SMEM((slots,), jnp.int32),
            pltpu.SMEM((2 * slots + UNITS,), jnp.int32),
            pltpu.VMEM((slots * BLOCK, PANELS * WIDTH), f32),
            pltpu.VMEM((slots, FEATURES, BLOCK), bf16),
            pltpu.VMEM((PANELS, FEATURES, WIDTH), bf16),
            pltpu.VMEM((col_count // 2, FEATURES, 2 * BLOCK), bf16),
            pltpu.VMEM((slots, BLOCK, BLOCK), f32),
            pltpu.VMEM((PANELS, SNODE_BLOCKS, BLOCK), f32),
            pltpu.VMEM((col_count, BLOCK), f32),
            pltpu.VMEM((WIDTH, WIDTH), bf16),
            pltpu.VMEM((WIDTH, WIDTH), bf16),
            pltpu.VMEM((WIDTH, WIDTH), bf16),
            pltpu.VMEM((WIDTH, WIDTH), bf16),
            pltpu.VMEM((WIDTH, WIDTH), f32),
            pltpu.VMEM((col_count * BLOCK, PANELS * WIDTH), bf16),
            pltpu.VMEM((col_count * BLOCK, PANELS * WIDTH), bf16),
            pltpu.VMEM((2, 2 * BLOCK * col_count, BLOCK), f32),
            pltpu.SemaphoreType.DMA((2, 2)),
        ]
        + [pltpu.VMEM((BLOCK, 2 * BLOCK), f32)] * 4,
        compiler_params=params,
        name="panels",
    )(block_map, pattern, points, totals)
    return out.reshape(row_count, 1, BLOCK, col_count, 1, BLOCK)


def solution(mesh):
    placed = (P(None, ("prow", "pcol")), P(), P())
    return jax.shard_map(
        local,
        mesh=mesh,
        in_specs=placed,
        out_specs=P(None, "prow", None, None, "pcol", None),
        check_vma=False,
    )
```

```python
import functools

import jax
import jax.numpy as jnp
from jax import lax
from jax.experimental import pallas as pl
from jax.experimental.pallas import tpu as pltpu
from jax.sharding import PartitionSpec as P

BLOCK = 128
SNODE_BLOCKS = 4
PANELS = 2
LEAD = PANELS * SNODE_BLOCKS
WIDTH = SNODE_BLOCKS * BLOCK

spread_factor = 89.0
scale_gain = 8.0
grid_step = 1024.0

LOW, HIGH = 0.98, 66.0

f32 = jnp.float32
bf16 = jnp.bfloat16
NN = (((1,), (0,)), ((), ()))
NT = (((1,), (1,)), ((), ()))
TN = (((0,), (0,)), ((), ()))
FEATURES = 32
VMEM_BYTES = 60 * 1024 * 1024


def mm(a, b, dims):
    return lax.dot_general(a, b, dims, preferred_element_type=f32)


def split(a):
    high = a.astype(bf16)
    low = (a - high.astype(f32)).astype(bf16)
    return high, low


def dot1(a, b, dims=NN):
    return mm(a.astype(bf16), b.astype(bf16), dims)


def mm3(a_high, a_low, b_high, b_low, dims):
    rows = a_high.shape[0]
    both = mm(jnp.concatenate([a_high, a_low], 0), b_high, dims)
    return (both[:rows] + both[rows:]) + mm(a_high, b_low, dims)


def dot3(a, b, dims=NN):
    a_high, a_low = split(a)
    b_high, b_low = split(b)
    return mm3(a_high, a_low, b_high, b_low, dims)


def eye(n):
    return (lax.broadcasted_iota(jnp.int32, (n, n), 0) == lax.broadcasted_iota(jnp.int32, (n, n), 1)).astype(f32)


class Background:
    def __init__(self, pieces, in_newton, in_chain):
        self.pieces = pieces
        self.weights = {"newton": in_newton, "chain": in_chain}
        self.total = 20 * in_newton + BLOCK // 8 * in_chain
        self.at = 0
        self.done = 0

    def tick(self, kind):
        self.at += self.weights[kind]
        upto = len(self.pieces) * self.at // self.total
        for piece in self.pieces[self.done : upto]:
            piece()
        self.done = max(self.done, upto)

    def finish(self):
        for piece in self.pieces[self.done :]:
            piece()
        self.done = len(self.pieces)


def newton(blocks, n, background):
    first = 2 / (LOW + HIGH)
    rho = (HIGH - LOW) / (HIGH + LOW)
    one = eye(n)
    step = 2 / (2 - rho * rho)
    rho = rho * rho / (2 - rho * rho)
    found = [(2 * step * first) * one - (step * first * first) * a for a in blocks]
    for at in range(5):
        dot = dot1 if at < 2 else dot3
        step = 2 / (2 - rho * rho) if at < 4 else 1.0
        rho = rho * rho / (2 - rho * rho)
        rest = [(2 * one) - dot(a, x) for a, x in zip(blocks, found)]
        background.tick("newton")
        found = [step * dot(x, e) for x, e in zip(found, rest)]
        background.tick("newton")
    return found


def chains(work, count, background):
    sub = lax.broadcasted_iota(jnp.int32, (8, BLOCK), 0)
    zero = jnp.zeros((8, BLOCK), f32)
    for strip in range(BLOCK // 8):
        at = 8 * strip
        state = []
        for b in range(count):
            r = work[b][at : at + 8, 0:BLOCK]
            y = work[b][at : at + 8, BLOCK : 2 * BLOCK]
            c = [jnp.broadcast_to(r[:, at + k : at + k + 1], (8, BLOCK)) for k in range(8)]
            state.append([r, y, c])
        for k in range(8):
            for b in range(count):
                r, y, c = state[b]
                inv = lax.rsqrt(c[k][k : k + 1, :])
                column = c[k] * inv
                below = jnp.where(sub > k, column, 0.0)
                r_row = r[k : k + 1] * inv
                y_row = y[k : k + 1] * inv
                r = jnp.where(sub == k, r_row, r - below * r_row)
                y = jnp.where(sub == k, y_row, y - below * y_row)
                for m in range(k + 1, 8):
                    c[m] = c[m] - below * column[m : m + 1, :]
                state[b] = [r, y, c]
        background.tick("chain")
        for b in range(count):
            r, y, _ = state[b]
            work[b][at : at + 8, 0:BLOCK] = r
            work[b][at : at + 8, BLOCK : 2 * BLOCK] = y
            if strip < BLOCK // 8 - 1:
                r_high = r.astype(bf16).astype(f32)
                y_high = y.astype(bf16).astype(f32)
                high = jnp.concatenate([r_high, y_high], 1)
                low = jnp.concatenate([r - r_high, y - y_high], 1)
                left = jnp.concatenate([r_high, r_high, r - r_high, zero], 0).astype(bf16)
                right = jnp.concatenate([high, low, high, jnp.concatenate([zero, zero], 1)], 0).astype(bf16)
                update = mm(left, right, TN)
                work[b][at + 8 :, :] = work[b][at + 8 :, :] - update[at + 8 :, :]


def factor_diagonal(a_ref, x_ref, work, background):
    half = 2 * BLOCK
    rows = lax.broadcasted_iota(jnp.int32, (BLOCK, BLOCK), 0)
    cols = lax.broadcasted_iota(jnp.int32, (BLOCK, BLOCK), 1)
    lower = cols <= rows
    a11 = a_ref[0:half, 0:half]
    a21 = a_ref[half:, 0:half]
    s2 = a_ref[half:, half:] - dot3(dot3(a21, newton([a11], half, background)[0]), a21, NT)
    corner = [a11[0:BLOCK, 0:BLOCK], s2[0:BLOCK, 0:BLOCK]]
    side = [a11[BLOCK:, 0:BLOCK], s2[BLOCK:, 0:BLOCK]]
    last = [a11[BLOCK:, BLOCK:], s2[BLOCK:, BLOCK:]]
    inverse = newton(corner, BLOCK, background)
    for i in range(2):
        work[2 * i][:, 0:BLOCK] = corner[i]
        work[2 * i + 1][:, 0:BLOCK] = last[i] - dot3(dot3(side[i], inverse[i]), side[i], NT)
    for b in range(4):
        work[b][:, BLOCK:] = eye(BLOCK)
    chains(work, 4, background)
    background.finish()
    for i in range(2):
        at = half * i
        xa = jnp.where(lower, work[2 * i][:, BLOCK:], 0.0)
        xb = jnp.where(lower, work[2 * i + 1][:, BLOCK:], 0.0)
        l21 = dot3(side[i], xa, NT)
        x_ref[at : at + BLOCK, at : at + BLOCK] = xa
        x_ref[at : at + BLOCK, at + BLOCK : at + half] = jnp.zeros((BLOCK, BLOCK), f32)
        x_ref[at + BLOCK : at + half, at : at + BLOCK] = -dot3(xb, dot3(l21, xa))
        x_ref[at + BLOCK : at + half, at + BLOCK : at + half] = xb
    x11 = x_ref[0:half, 0:half]
    x22 = x_ref[half:, half:]
    l21 = dot3(a21, x11, NT)
    x_ref[half:, 0:half] = -dot3(x22, dot3(l21, x11))
    x_ref[0:half, half:] = jnp.zeros((half, half), f32)


def pieces(point):
    low = (point & 255).astype(f32)
    mid = ((point >> 8) & 255).astype(f32)
    top = (point >> 16).astype(f32)
    return low, mid, top


def left_features(point):
    low, mid, top = pieces(point)
    norm = lax.broadcasted_iota(jnp.int32, point.shape, 0) == 3
    one = jnp.ones_like(low)
    zero = jnp.zeros_like(low)
    return jnp.concatenate(
        [low, jnp.where(norm, one, low), mid, jnp.where(norm, one, mid), top, jnp.where(norm, one, zero), zero, zero], 0
    ).astype(bf16)


def right_features(point):
    low, mid, top = pieces(point)
    norm = lax.broadcasted_iota(jnp.int32, point.shape, 0) == 3
    one = jnp.ones_like(low)
    zero = jnp.zeros_like(low)
    return jnp.concatenate(
        [
            jnp.where(norm, one, -2.0 * low),
            jnp.where(norm, low, -512.0 * mid),
            jnp.where(norm, 256.0 * one, -512.0 * low),
            jnp.where(norm, 256.0 * mid, -131072.0 * mid),
            jnp.where(norm, 65536.0 * one, zero),
            jnp.where(norm, 65536.0 * top, zero),
            zero,
            zero,
        ],
        0,
    ).astype(bf16)


def shape_of(radius):
    unit = 1.0 / (grid_step * radius)
    shift = 9.0 / (35.0 * unit)
    return {"reach": 1.0 / unit, "shift": shift, "bias": 3.0 / (35.0 * unit * unit) - shift * shift, "gain": 35.0 / 3.0 * unit**8}


def wendland(dist_sq, shape):
    dist = dist_sq * lax.rsqrt(jnp.maximum(dist_sq, 1.0))
    rest = jnp.maximum(shape["reach"] - dist, 0.0)
    rest_sq = rest * rest
    moved = dist + shape["shift"]
    return (rest_sq * rest_sq) * (rest_sq * (moved * moved + shape["bias"]))


def member(panel_at, block, pattern):
    first = panel_at * SNODE_BLOCKS
    own = (block >= first) & (block < first + SNODE_BLOCKS)
    return jnp.where(own, 1, jnp.where(block < first, 0, pattern[panel_at, block]))


def weight(row, col, pattern):
    value = (row == col).astype(jnp.int32)
    for panel_at in range(PANELS):
        value = value + member(panel_at, row, pattern) * member(panel_at, col, pattern)
    return value.astype(f32)


GROUP = 8
UNITS = 24
FIRSTS = 8
NEWTON_SHARE = 1


def sums_kernel(shape, per, block_map, pattern, points, out, left, lists, weights):
    nblocks = points.shape[0]
    me = lax.axis_index("prow") * lax.axis_size("pcol") + lax.axis_index("pcol")
    own = [block_map[me * per + b] for b in range(per)]
    right = [right_features(points[me * per + b]) for b in range(per)]

    def scan_block(m, counts):
        left[m] = left_features(points[m])
        after = []
        for b in range(per):
            value = weight(own[b], block_map[m], pattern)
            lists[b, counts[b]] = m
            weights[b, counts[b]] = value * shape["gain"]
            after.append(counts[b] + (value > 0).astype(jnp.int32))
        return tuple(after)

    counts = lax.fori_loop(0, nblocks, scan_block, (0,) * per)
    for b in range(per):
        for g in range(GROUP):
            lists[b, counts[b] + g] = 0
            weights[b, counts[b] + g] = 0.0

    for b in range(per):

        def group(step, total):
            parts = []
            for g in range(GROUP):
                at = step * GROUP + g
                value = wendland(mm(left[lists[b, at]], right[b], TN), shape)
                parts.append(jnp.sum(value.reshape(BLOCK // 8, 8, BLOCK), axis=0) * weights[b, at])
            return total + functools.reduce(lambda x, y: x + y, parts)

        total = lax.fori_loop(0, (counts[b] + GROUP - 1) // GROUP, group, jnp.zeros((8, BLOCK), f32))
        row = jnp.sum(total, axis=0, keepdims=True)
        for d in range(out.shape[0]):
            out[d, b : b + 1, :] = row


def spread_kernel(per, coords, out):
    for b in range(per):
        point = coords[:, b * BLOCK : (b + 1) * BLOCK]
        norm = jnp.sum(point * point, axis=0, keepdims=True)
        point = jnp.concatenate([point, norm], 0)
        for d in range(out.shape[0]):
            out[d, b] = point


def panels_kernel(
    shape, rows_n, cols_n, block_map, pattern, points, totals, out,
    inverse, table, place, units, firsts, panel, high, low, left, right_lead, right_cols, scale_rows, scale_lead, scale_cols,
    diagonal, x_high, x_low, x_full, stage, sems, *work,
):
    nblocks = points.shape[0]
    row_count = nblocks // rows_n
    col_count = nblocks // cols_n
    prow_at = lax.axis_index("prow")
    pcol_at = lax.axis_index("pcol")
    col_base = row_count
    next_base = row_count + col_count
    lead_base = next_base + SNODE_BLOCKS
    slots = lead_base + SNODE_BLOCKS
    lead_rows = LEAD // rows_n

    def invert(m, carry):
        inverse[block_map[m]] = m
        return carry

    lax.fori_loop(0, nblocks, invert, 0)

    def sort(base, blocks, lead):
        kinds = []
        first = second = jnp.int32(0)
        for g, at in blocks:
            in_first = member(0, g, pattern) > 0
            in_second = member(1, g, pattern) > 0
            dead = g < LEAD
            kind = jnp.where(dead, 2, jnp.where(in_first, 0, jnp.where(in_second, 1, 2)))
            kinds.append(kind)
            first = first + (kind == 0).astype(jnp.int32)
            second = second + (kind == 1).astype(jnp.int32)
        spots = [base + lead, base + lead + first, base + lead + first + second]
        for (g, at), kind in zip(blocks, kinds):
            spot = jnp.where(kind == 0, spots[0], jnp.where(kind == 1, spots[1], spots[2]))
            table[spot] = g
            place[spot] = at
            for n in range(3):
                spots[n] = spots[n] + (kind == n).astype(jnp.int32)
        return lead + first, lead + first + second

    for i in range(lead_rows):
        table[i] = i * rows_n + prow_at
        place[i] = i
    rows_first, rows_both = sort(0, [(i * rows_n + prow_at, i) for i in range(lead_rows, row_count)], lead_rows)
    cols_first, cols_both = sort(col_base, [(k * cols_n + pcol_at, k) for k in range(col_count)], 0)
    for j in range(SNODE_BLOCKS):
        table[next_base + j] = SNODE_BLOCKS + j
        table[lead_base + j] = j
    def block_rows(slot):
        return pl.ds(pl.multiple_of(slot * BLOCK, BLOCK), BLOCK)

    def pair_rows(slot):
        return pl.ds(pl.multiple_of(slot * BLOCK, 2 * BLOCK), 2 * BLOCK)

    def scale_of(m):
        return scale_gain * lax.rsqrt(1.0 + totals[pl.ds(m, 1), :])

    def prepare(slot):
        m = inverse[table[slot]]
        left[slot] = left_features(points[m])
        scale_rows[slot] = jnp.broadcast_to(scale_of(m), (BLOCK, BLOCK)).T

    def prepare_lead(j):
        m = inverse[j]
        half, at = divmod(j, SNODE_BLOCKS)
        right_lead[j] = right_features(points[m])
        scale_lead[half, at : at + 1, :] = scale_of(m)

    def prepare_col(k):
        m = inverse[table[col_base + k]]
        right_cols[k // 2, :, k % 2 * BLOCK : (k % 2 + 1) * BLOCK] = right_features(points[m])
        scale_cols[k : k + 1, :] = scale_of(m)

    def coupled(slot, half, j):
        value = wendland(mm(left[slot], right_lead[half * SNODE_BLOCKS + j], TN), shape)
        scale = scale_lead[half, j : j + 1, :] * (weight(table[slot], half * SNODE_BLOCKS + j, pattern) * shape["gain"])
        return value * scale_rows[slot] * scale

    def couple(at, j):
        unit = units[at]
        slot = unit // 2
        half = unit % 2
        lanes = pl.ds(pl.multiple_of(half * WIDTH + j * BLOCK, BLOCK), BLOCK)
        panel[block_rows(slot), lanes] = coupled(slot, half, j)

    def even(n):
        return (n + 1) // 2 * 2

    count = jnp.int32(0)
    for base, size, ends in ((next_base, SNODE_BLOCKS, (SNODE_BLOCKS,) * PANELS), (0, row_count, (even(rows_first), even(rows_both))), (col_base, col_count, (even(cols_first), even(cols_both)))):
        for at in range(size):
            for half in range(PANELS):
                units[count] = 2 * (base + at) + half
                count = count + jnp.int32(at < ends[half])
    for n in range(UNITS):
        units[count + n] = 2 * lead_base + 1

    first_count = jnp.int32(0)
    for base, size, used in ((0, row_count, rows_first), (col_base, col_count, cols_first)):
        for c in range(0, size, 2):
            firsts[first_count] = base + c
            first_count = first_count + (c < used).astype(jnp.int32)
    for n in range(FIRSTS):
        firsts[first_count + n] = lead_base

    for j in range(SNODE_BLOCKS):
        prepare(lead_base + j)
        prepare_lead(j)
    for i in range(SNODE_BLOCKS):
        for j in range(SNODE_BLOCKS):
            value = coupled(lead_base + i, 0, j)
            diagonal[i * BLOCK : (i + 1) * BLOCK, j * BLOCK : (j + 1) * BLOCK] = value + eye(BLOCK) if i == j else value

    def several(parts):
        def run():
            for part in parts:
                part()

        return run

    parts = [functools.partial(prepare_lead, j) for j in range(SNODE_BLOCKS, LEAD)]
    parts += [functools.partial(prepare, slot) for slot in range(lead_base)]
    parts += [functools.partial(prepare_col, k) for k in range(col_count)]
    pieces = [several(parts[n : n + 5]) for n in range(0, len(parts), 5)]
    parts = [functools.partial(couple, at, j) for at in range(UNITS) for j in range(SNODE_BLOCKS)]
    pieces += [several(parts[n : n + 2]) for n in range(0, len(parts), 2)]
    factor_diagonal(diagonal, x_full, work, Background(pieces, 1, 1))
    x_high[...], x_low[...] = split(x_full[...])

    def couple_more(step, carry):
        for n in range(2):
            for j in range(SNODE_BLOCKS):
                couple(UNITS + 2 * step + n, j)
        return carry

    lax.fori_loop(0, (jnp.maximum(count - UNITS, 0) + 1) // 2, couple_more, 0)
    for i in range(lead_rows):
        at = slice(i * BLOCK, (i + 1) * BLOCK)
        lanes = pl.ds(pl.multiple_of((i * rows_n + prow_at) * BLOCK, BLOCK), BLOCK)
        panel[at, lanes] = panel[at, lanes] + eye(BLOCK)

    middle = WIDTH // 2

    def solve(at, first):
        a_high, a_low = split(panel[at, first : first + WIDTH])
        for begin, end in ((0, middle), (middle, WIDTH)):
            part = mm3(a_high[:, :end], a_low[:, :end], x_high[begin:end, :end], x_low[begin:end, :end], NT)
            lanes = slice(first + begin, first + end)
            panel[at, lanes] = part
            high[at, lanes], low[at, lanes] = split(part)

    next_rows = slice(next_base * BLOCK, lead_base * BLOCK)
    for c in range(next_base, lead_base, 2):
        solve(pair_rows(c), 0)

    def subtract(at, out_ref, out_at):
        for lanes in (slice(0, middle), slice(middle, WIDTH)):
            rows = slice(next_base * BLOCK + lanes.start, next_base * BLOCK + lanes.stop)
            done = mm3(high[at, :WIDTH], low[at, :WIDTH], high[rows, :WIDTH], low[rows, :WIDTH], NT)
            from_at = slice(WIDTH + lanes.start, WIDTH + lanes.stop)
            if out_ref is panel:
                panel[at, from_at] = panel[at, from_at] - done
            else:
                out_ref[out_at, lanes] = panel[at, from_at] - done

    for c in range(0, SNODE_BLOCKS, 2):
        subtract(pair_rows(next_base + c), diagonal, slice(c * BLOCK, (c + 2) * BLOCK))
    for j in range(SNODE_BLOCKS):
        at = slice(j * BLOCK, (j + 1) * BLOCK)
        diagonal[at, at] = diagonal[at, at] + eye(BLOCK)

    def first_solve(n):
        solve(pair_rows(firsts[n]), 0)

    def first_subtract(n):
        subtract(pair_rows(firsts[n]), panel, None)

    pieces = [functools.partial(f, n) for n in range(FIRSTS) for f in (first_solve, first_subtract)]
    factor_diagonal(diagonal, x_full, work, Background(pieces, NEWTON_SHARE, 4))

    def first_more(n, carry):
        first_solve(n)
        first_subtract(n)
        return carry

    lax.fori_loop(FIRSTS, first_count, first_more, 0)
    x_high[...], x_low[...] = split(x_full[...])
    row_chunks = (rows_both + 1) // 2

    def second(c, carry):
        slot = jnp.where(c < row_chunks, 2 * c, col_base + 2 * (c - row_chunks))
        solve(pair_rows(slot), WIDTH)
        return carry

    lax.fori_loop(0, row_chunks + (cols_both + 1) // 2, second, 0)
    for i in range(lead_rows):
        if i * rows_n < SNODE_BLOCKS:

            @pl.when(i * rows_n + prow_at < SNODE_BLOCKS)
            def _(i=i):
                panel[i * BLOCK : (i + 1) * BLOCK, WIDTH:] = jnp.zeros((BLOCK, WIDTH), f32)

    per_slot = BLOCK * col_count
    row_live = (rows_both + 1) // 2
    row_two = (rows_first + 1) // 2
    col_live = (cols_both + 1) // 2
    col_two = (cols_first + 1) // 2

    def copies_out(step, half):
        made = []
        for q in range(2):
            at = pl.multiple_of(place[2 * step + q] * per_slot, per_slot)
            made.append(
                pltpu.make_async_copy(stage.at[half, pl.ds(q * per_slot, per_slot), :], out.at[pl.ds(at, per_slot), :], sems.at[half, q])
            )
        return made

    def trail(step, carry):
        half = step % 2

        @pl.when(step >= 2)
        def _():
            for copy in copies_out(step - 2, half):
                copy.wait()

        def spots(q, k):
            return pl.ds(q * per_slot + k, BLOCK, stride=col_count)

        def tiles(c, carry):
            live = (step < row_live) & (c < col_live) & (step >= lead_rows // 2)
            two = (step < row_two) & (c < col_two)
            row_at = pair_rows(2 * step)
            col_at = pair_rows(col_base + 2 * c)

            def body(first):
                tiles = []
                for q in range(2):
                    slot = 2 * step + q
                    value = wendland(mm(left[slot], right_cols[c], TN), shape)
                    for e in range(2):
                        spot = col_base + 2 * c + e
                        factor = scale_cols[pl.ds(2 * c + e, 1), :] * (weight(table[slot], table[spot], pattern) * shape["gain"])
                        tiles.append(value[:, e * BLOCK : (e + 1) * BLOCK] * scale_rows[slot] * factor)
                update = mm3(high[row_at, first:], low[row_at, first:], high[col_at, first:], low[col_at, first:], NT)
                for q in range(2):
                    g = table[2 * step + q]
                    for e in range(2):
                        spot = col_base + 2 * c + e
                        tile = tiles[2 * q + e] - update[q * BLOCK : (q + 1) * BLOCK, e * BLOCK : (e + 1) * BLOCK]
                        if lead_rows % 2:
                            tile = tile * (g >= LEAD).astype(f32)
                        stage[half, spots(q, place[spot]), :] = tile

            @pl.when(live & two)
            def _():
                body(0)

            @pl.when(live & jnp.logical_not(two))
            def _():
                body(WIDTH)

            @pl.when(jnp.logical_not(live))
            def _():
                for q in range(2):
                    for e in range(2):
                        stage[half, spots(q, place[col_base + 2 * c + e]), :] = jnp.zeros((BLOCK, BLOCK), f32)

            return carry

        lax.fori_loop(0, col_count // 2, tiles, 0)
        for q in range(2):
            slot = 2 * step + q
            g = table[slot]
            k_same = g // cols_n
            here = (k_same * cols_n + pcol_at == g) & (g >= LEAD)
            same = spots(q, k_same)

            @pl.when(here & (slot >= rows_both))
            def _(slot=slot, g=g, same=same):
                m = inverse[g]
                value = wendland(mm(left[slot], right_features(points[m]), TN), shape)
                factor = scale_gain * lax.rsqrt(1.0 + totals[pl.ds(m, 1), :]) * (weight(g, g, pattern) * shape["gain"])
                stage[half, same, :] = value * scale_rows[slot] * factor

            @pl.when(here)
            def _(same=same):
                stage[half, same, :] = stage[half, same, :] + eye(BLOCK)

            for k in range(col_count):
                if k * cols_n < LEAD:
                    j = k * cols_n + pcol_at

                    filled = slot < jnp.where(j < SNODE_BLOCKS, even(rows_first), even(rows_both))

                    @pl.when((j < LEAD) & filled)
                    def _(k=k, j=j, q=q, slot=slot):
                        where = pl.ds(pl.multiple_of(j * BLOCK, BLOCK), BLOCK)
                        stage[half, spots(q, k), :] = panel[block_rows(slot), where]

                    @pl.when((j < LEAD) & jnp.logical_not(filled))
                    def _(k=k, q=q):
                        stage[half, spots(q, k), :] = jnp.zeros((BLOCK, BLOCK), f32)

        for copy in copies_out(step, half):
            copy.start()
        return carry

    steps = row_count // 2
    lax.fori_loop(0, steps, trail, 0)
    for step in range(max(steps - 2, 0), steps):
        for copy in copies_out(step, step % 2):
            copy.wait()


def local(coords, block_map, pattern):
    rows_n = lax.axis_size("prow")
    cols_n = lax.axis_size("pcol")
    devices = rows_n * cols_n
    nblocks = block_map.shape[0]
    per = nblocks // devices
    row_count = nblocks // rows_n
    col_count = nblocks // cols_n
    radius = (spread_factor / (nblocks * BLOCK)) ** (1.0 / 3.0)
    slots = row_count + col_count + LEAD
    rows_kept = (slots - SNODE_BLOCKS + 2) * BLOCK
    axes = ("prow", "pcol")
    smem = pl.BlockSpec(memory_space=pltpu.SMEM)
    vmem = pl.BlockSpec(memory_space=pltpu.VMEM)
    params = pltpu.CompilerParams(vmem_limit_bytes=VMEM_BYTES)
    shape = shape_of(radius)
    mine = pl.pallas_call(
        functools.partial(spread_kernel, per),
        out_shape=jax.ShapeDtypeStruct((devices, per, 4, BLOCK), jnp.int32),
        in_specs=[vmem],
        out_specs=vmem,
        name="spread",
    )(coords)
    points = lax.all_to_all(mine, axes, 0, 0, tiled=True).reshape(nblocks, 4, BLOCK)
    sums = pl.pallas_call(
        functools.partial(sums_kernel, shape, per),
        out_shape=jax.ShapeDtypeStruct((devices, per, BLOCK), f32),
        in_specs=[smem, smem, vmem],
        out_specs=vmem,
        scratch_shapes=[
            pltpu.VMEM((nblocks, FEATURES, BLOCK), bf16),
            pltpu.SMEM((per, nblocks + GROUP), jnp.int32),
            pltpu.SMEM((per, nblocks + GROUP), f32),
        ],
        compiler_params=params,
        name="sums",
    )(block_map, pattern, points)
    totals = lax.all_to_all(sums, axes, 0, 0, tiled=True).reshape(nblocks, BLOCK)
    out = pl.pallas_call(
        functools.partial(panels_kernel, shape, rows_n, cols_n),
        out_shape=jax.ShapeDtypeStruct((row_count * BLOCK * col_count, BLOCK), f32),
        in_specs=[smem, smem, vmem, vmem],
        out_specs=pl.BlockSpec(memory_space=pl.ANY),
        scratch_shapes=[
            pltpu.SMEM((nblocks,), jnp.int32),
            pltpu.SMEM((slots,), jnp.int32),
            pltpu.SMEM((slots,), jnp.int32),
            pltpu.SMEM((2 * slots + UNITS,), jnp.int32),
            pltpu.SMEM((slots + FIRSTS,), jnp.int32),
            pltpu.VMEM((rows_kept, PANELS * WIDTH), f32),
            pltpu.VMEM((rows_kept, PANELS * WIDTH), bf16),
            pltpu.VMEM((rows_kept, PANELS * WIDTH), bf16),
            pltpu.VMEM((slots, FEATURES, BLOCK), bf16),
            pltpu.VMEM((LEAD, FEATURES, BLOCK), bf16),
            pltpu.VMEM((col_count // 2, FEATURES, 2 * BLOCK), bf16),
            pltpu.VMEM((slots, BLOCK, BLOCK), f32),
            pltpu.VMEM((PANELS, SNODE_BLOCKS, BLOCK), f32),
            pltpu.VMEM((col_count, BLOCK), f32),
            pltpu.VMEM((WIDTH, WIDTH), f32),
            pltpu.VMEM((WIDTH, WIDTH), bf16),
            pltpu.VMEM((WIDTH, WIDTH), bf16),
            pltpu.VMEM((WIDTH, WIDTH), f32),
            pltpu.VMEM((2, 2 * BLOCK * col_count, BLOCK), f32),
            pltpu.SemaphoreType.DMA((2, 2)),
        ]
        + [pltpu.VMEM((BLOCK, 2 * BLOCK), f32)] * 4,
        compiler_params=params,
        name="panels",
    )(block_map, pattern, points, totals)
    return out.reshape(row_count, 1, BLOCK, col_count, 1, BLOCK)


def solution(mesh):
    placed = (P(None, ("prow", "pcol")), P(), P())
    return jax.shard_map(
        local,
        mesh=mesh,
        in_specs=placed,
        out_specs=P(None, "prow", None, None, "pcol", None),
        check_vma=False,
    )
```

```python
import functools

import jax
import jax.numpy as jnp
from jax import lax
from jax.experimental import pallas as pl
from jax.experimental.pallas import tpu as pltpu
from jax.sharding import PartitionSpec as P

BLOCK = 128
SNODE_BLOCKS = 4
PANELS = 2
LEAD = PANELS * SNODE_BLOCKS
WIDTH = SNODE_BLOCKS * BLOCK

spread_factor = 89.0
scale_gain = 8.0
grid_step = 1024.0

LOW, HIGH = 0.98, 66.0

f32 = jnp.float32
bf16 = jnp.bfloat16
STRIPS = 2
NN = (((1,), (0,)), ((), ()))
NT = (((1,), (1,)), ((), ()))
TN = (((0,), (0,)), ((), ()))
FEATURES = 32
VMEM_BYTES = 60 * 1024 * 1024


def mm(a, b, dims):
    return lax.dot_general(a, b, dims, preferred_element_type=f32)


def split(a):
    high = a.astype(bf16)
    low = (a - high.astype(f32)).astype(bf16)
    return high, low


def dot1(a, b, dims=NN):
    return mm(a.astype(bf16), b.astype(bf16), dims)


def mm3(a_high, a_low, b_high, b_low, dims):
    rows = a_high.shape[0]
    both = mm(jnp.concatenate([a_high, a_low], 0), b_high, dims)
    return (both[:rows] + both[rows:]) + mm(a_high, b_low, dims)


def dot3(a, b, dims=NN):
    a_high, a_low = split(a)
    b_high, b_low = split(b)
    return mm3(a_high, a_low, b_high, b_low, dims)


def eye(n):
    return (lax.broadcasted_iota(jnp.int32, (n, n), 0) == lax.broadcasted_iota(jnp.int32, (n, n), 1)).astype(f32)


def newton(blocks, n, beside):
    first = 2 / (LOW + HIGH)
    rho = (HIGH - LOW) / (HIGH + LOW)
    one = eye(n)
    step = 2 / (2 - rho * rho)
    rho = rho * rho / (2 - rho * rho)
    found = [(2 * step * first) * one - (step * first * first) * a for a in blocks]
    for at in range(5):
        dot = dot1 if at < 2 else dot3
        step = 2 / (2 - rho * rho) if at < 4 else 1.0
        rho = rho * rho / (2 - rho * rho)
        rest = [(2 * one) - dot(a, x) for a, x in zip(blocks, found)]
        next(beside, None)
        found = [step * dot(x, e) for x, e in zip(found, rest)]
        next(beside, None)
    return found


def chains(work, count, beside):
    sub = lax.broadcasted_iota(jnp.int32, (8, BLOCK), 0)
    lane = lax.broadcasted_iota(jnp.int32, (8, BLOCK), 1)
    zero = jnp.zeros((8, BLOCK), f32)

    def strip(step, part):
        n = step * STRIPS + part
        at = n * 8
        rows = pl.ds(pl.multiple_of(at, 8), 8)
        beside(step, part)
        state = []
        for b in range(count):
            r = work[b][rows, 0:BLOCK]
            y = work[b][rows, BLOCK : 2 * BLOCK]
            turned = pltpu.roll(r, lax.rem(BLOCK - at, BLOCK), 1)
            c = [jnp.broadcast_to(turned[:, k : k + 1], (8, BLOCK)) for k in range(8)]
            state.append([r, y, c])
        for k in range(8):
            for b in range(count):
                r, y, c = state[b]
                inv = lax.rsqrt(c[k][k : k + 1, :])
                column = c[k] * inv
                below = jnp.where(sub > k, column, 0.0)
                r_row = r[k : k + 1] * inv
                y_row = y[k : k + 1] * inv
                r = jnp.where(sub == k, r_row, r - below * r_row)
                y = jnp.where(sub == k, y_row, y - below * y_row)
                for m in range(k + 1, 8):
                    c[m] = c[m] - below * column[m : m + 1, :]
                state[b] = [r, y, c]
        later = lane >= at + 8
        for b in range(count):
            r, y, _ = state[b]
            work[b][rows, 0:BLOCK] = r
            work[b][rows, BLOCK : 2 * BLOCK] = y
            r_high = r.astype(bf16).astype(f32)
            y_high = y.astype(bf16).astype(f32)
            high = jnp.concatenate([r_high, y_high], 1)
            low = jnp.concatenate([r - r_high, y - y_high], 1)
            left_high = jnp.where(later, r_high, 0.0)
            left_low = jnp.where(later, r - r_high, 0.0)
            left = jnp.concatenate([left_high, left_high, left_low, zero], 0).astype(bf16)
            right = jnp.concatenate([high, low, high, jnp.concatenate([zero, zero], 1)], 0).astype(bf16)
            work[b][...] = work[b][...] - mm(left, right, TN)

    def strips(step, carry):
        for n in range(STRIPS):
            strip(step, n)
        return carry

    lax.fori_loop(0, BLOCK // 8 // STRIPS, strips, 0)


def factor_diagonal(a_ref, x_ref, work, beside_newton, beside_strip):
    half = 2 * BLOCK
    rows = lax.broadcasted_iota(jnp.int32, (BLOCK, BLOCK), 0)
    cols = lax.broadcasted_iota(jnp.int32, (BLOCK, BLOCK), 1)
    lower = cols <= rows
    a11 = a_ref[0:half, 0:half]
    a21 = a_ref[half:, 0:half]
    s2 = a_ref[half:, half:] - dot3(dot3(a21, newton([a11], half, beside_newton)[0]), a21, NT)
    corner = [a11[0:BLOCK, 0:BLOCK], s2[0:BLOCK, 0:BLOCK]]
    side = [a11[BLOCK:, 0:BLOCK], s2[BLOCK:, 0:BLOCK]]
    last = [a11[BLOCK:, BLOCK:], s2[BLOCK:, BLOCK:]]
    inverse = newton(corner, BLOCK, beside_newton)
    for i in range(2):
        work[2 * i][:, 0:BLOCK] = corner[i]
        work[2 * i + 1][:, 0:BLOCK] = last[i] - dot3(dot3(side[i], inverse[i]), side[i], NT)
    for b in range(4):
        work[b][:, BLOCK:] = eye(BLOCK)
    for _ in beside_newton:
        pass
    chains(work, 4, beside_strip)
    for i in range(2):
        at = half * i
        xa = jnp.where(lower, work[2 * i][:, BLOCK:], 0.0)
        xb = jnp.where(lower, work[2 * i + 1][:, BLOCK:], 0.0)
        l21 = dot3(side[i], xa, NT)
        x_ref[at : at + BLOCK, at : at + BLOCK] = xa
        x_ref[at : at + BLOCK, at + BLOCK : at + half] = jnp.zeros((BLOCK, BLOCK), f32)
        x_ref[at + BLOCK : at + half, at : at + BLOCK] = -dot3(xb, dot3(l21, xa))
        x_ref[at + BLOCK : at + half, at + BLOCK : at + half] = xb
    x11 = x_ref[0:half, 0:half]
    x22 = x_ref[half:, half:]
    l21 = dot3(a21, x11, NT)
    x_ref[half:, 0:half] = -dot3(x22, dot3(l21, x11))
    x_ref[0:half, half:] = jnp.zeros((half, half), f32)


def pieces(point):
    low = (point & 255).astype(f32)
    mid = ((point >> 8) & 255).astype(f32)
    top = (point >> 16).astype(f32)
    return low, mid, top


def left_features(point):
    low, mid, top = pieces(point)
    norm = lax.broadcasted_iota(jnp.int32, point.shape, 0) == 3
    one = jnp.ones_like(low)
    zero = jnp.zeros_like(low)
    return jnp.concatenate(
        [low, jnp.where(norm, one, low), mid, jnp.where(norm, one, mid), top, jnp.where(norm, one, zero), zero, zero], 0
    ).astype(bf16)


def right_features(point):
    low, mid, top = pieces(point)
    norm = lax.broadcasted_iota(jnp.int32, point.shape, 0) == 3
    one = jnp.ones_like(low)
    zero = jnp.zeros_like(low)
    return jnp.concatenate(
        [
            jnp.where(norm, one, -2.0 * low),
            jnp.where(norm, low, -512.0 * mid),
            jnp.where(norm, 256.0 * one, -512.0 * low),
            jnp.where(norm, 256.0 * mid, -131072.0 * mid),
            jnp.where(norm, 65536.0 * one, zero),
            jnp.where(norm, 65536.0 * top, zero),
            zero,
            zero,
        ],
        0,
    ).astype(bf16)


def shape_of(radius):
    unit = 1.0 / (grid_step * radius)
    shift = 9.0 / (35.0 * unit)
    return {"reach": 1.0 / unit, "shift": shift, "bias": 3.0 / (35.0 * unit * unit) - shift * shift, "gain": 35.0 / 3.0 * unit**8}


def wendland(dist_sq, shape):
    dist = dist_sq * lax.rsqrt(jnp.maximum(dist_sq, 1.0))
    rest = jnp.maximum(shape["reach"] - dist, 0.0)
    rest_sq = rest * rest
    moved = dist + shape["shift"]
    return (rest_sq * rest_sq) * (rest_sq * (moved * moved + shape["bias"]))


def member(panel_at, block, pattern):
    first = panel_at * SNODE_BLOCKS
    own = (block >= first) & (block < first + SNODE_BLOCKS)
    return jnp.where(own, 1, jnp.where(block < first, 0, pattern[panel_at, block]))


def weight(row, col, pattern):
    value = (row == col).astype(jnp.int32)
    for panel_at in range(PANELS):
        value = value + member(panel_at, row, pattern) * member(panel_at, col, pattern)
    return value.astype(f32)


GROUP = 8
UNITS = 32
FIRSTS = 8


def sums_kernel(shape, per, block_map, pattern, points, out, left, lists, weights):
    nblocks = points.shape[0]
    me = lax.axis_index("prow") * lax.axis_size("pcol") + lax.axis_index("pcol")
    own = [block_map[me * per + b] for b in range(per)]
    right = [right_features(points[me * per + b]) for b in range(per)]

    def scan_block(m, counts):
        left[m] = left_features(points[m])
        after = []
        for b in range(per):
            value = weight(own[b], block_map[m], pattern)
            lists[b, counts[b]] = m
            weights[b, counts[b]] = value * shape["gain"]
            after.append(counts[b] + (value > 0).astype(jnp.int32))
        return tuple(after)

    counts = lax.fori_loop(0, nblocks, scan_block, (0,) * per)
    for b in range(per):
        for g in range(GROUP):
            lists[b, counts[b] + g] = 0
            weights[b, counts[b] + g] = 0.0

    for b in range(per):

        def group(step, total):
            parts = []
            for g in range(GROUP):
                at = step * GROUP + g
                value = wendland(mm(left[lists[b, at]], right[b], TN), shape)
                parts.append(jnp.sum(value.reshape(BLOCK // 8, 8, BLOCK), axis=0) * weights[b, at])
            return total + functools.reduce(lambda x, y: x + y, parts)

        total = lax.fori_loop(0, (counts[b] + GROUP - 1) // GROUP, group, jnp.zeros((8, BLOCK), f32))
        row = jnp.sum(total, axis=0, keepdims=True)
        for d in range(out.shape[0]):
            out[d, b : b + 1, :] = row


def spread_kernel(per, coords, out):
    for b in range(per):
        point = coords[:, b * BLOCK : (b + 1) * BLOCK]
        norm = jnp.sum(point * point, axis=0, keepdims=True)
        point = jnp.concatenate([point, norm], 0)
        for d in range(out.shape[0]):
            out[d, b] = point


def panels_kernel(
    shape, rows_n, cols_n, block_map, pattern, points, totals, out,
    inverse, table, place, units, firsts, panel, high, low, left, right_lead, right_cols, scale_rows, scale_lead, scale_cols,
    diagonal, x_high, x_low, x_full, stage, sems, *work,
):
    nblocks = points.shape[0]
    row_count = nblocks // rows_n
    col_count = nblocks // cols_n
    prow_at = lax.axis_index("prow")
    pcol_at = lax.axis_index("pcol")
    col_base = row_count
    next_base = row_count + col_count
    lead_base = next_base + SNODE_BLOCKS
    slots = lead_base + SNODE_BLOCKS
    lead_rows = LEAD // rows_n

    def invert(m, carry):
        inverse[block_map[m]] = m
        return carry

    lax.fori_loop(0, nblocks, invert, 0)

    def sort(base, blocks, lead):
        kinds = []
        first = second = jnp.int32(0)
        for g, at in blocks:
            in_first = member(0, g, pattern) > 0
            in_second = member(1, g, pattern) > 0
            dead = g < LEAD
            kind = jnp.where(dead, 2, jnp.where(in_first, 0, jnp.where(in_second, 1, 2)))
            kinds.append(kind)
            first = first + (kind == 0).astype(jnp.int32)
            second = second + (kind == 1).astype(jnp.int32)
        spots = [base + lead, base + lead + first, base + lead + first + second]
        for (g, at), kind in zip(blocks, kinds):
            spot = jnp.where(kind == 0, spots[0], jnp.where(kind == 1, spots[1], spots[2]))
            table[spot] = g
            place[spot] = at
            for n in range(3):
                spots[n] = spots[n] + (kind == n).astype(jnp.int32)
        return lead + first, lead + first + second

    for i in range(lead_rows):
        table[i] = i * rows_n + prow_at
        place[i] = i
    rows_first, rows_both = sort(0, [(i * rows_n + prow_at, i) for i in range(lead_rows, row_count)], lead_rows)
    cols_first, cols_both = sort(col_base, [(k * cols_n + pcol_at, k) for k in range(col_count)], 0)
    for j in range(SNODE_BLOCKS):
        table[next_base + j] = SNODE_BLOCKS + j
        table[lead_base + j] = j
    def block_rows(slot):
        return pl.ds(pl.multiple_of(slot * BLOCK, BLOCK), BLOCK)

    def pair_rows(slot):
        return pl.ds(pl.multiple_of(slot * BLOCK, 2 * BLOCK), 2 * BLOCK)

    def scale_of(m):
        return scale_gain * lax.rsqrt(1.0 + totals[pl.ds(m, 1), :])

    def prepare(slot):
        m = inverse[table[slot]]
        left[slot] = left_features(points[m])
        scale_rows[slot] = jnp.broadcast_to(scale_of(m), (BLOCK, BLOCK)).T

    def prepare_lead(j):
        m = inverse[j]
        half, at = divmod(j, SNODE_BLOCKS)
        right_lead[j] = right_features(points[m])
        scale_lead[half, at : at + 1, :] = scale_of(m)

    def prepare_col(k):
        m = inverse[table[col_base + k]]
        right_cols[k // 2, :, k % 2 * BLOCK : (k % 2 + 1) * BLOCK] = right_features(points[m])
        scale_cols[k : k + 1, :] = scale_of(m)

    def coupled(slot, half, j):
        value = wendland(mm(left[slot], right_lead[half * SNODE_BLOCKS + j], TN), shape)
        scale = scale_lead[half, j : j + 1, :] * (weight(table[slot], half * SNODE_BLOCKS + j, pattern) * shape["gain"])
        return value * scale_rows[slot] * scale

    def couple(at, j):
        unit = units[at]
        slot = unit // 2
        half = unit % 2
        lanes = pl.ds(pl.multiple_of(half * WIDTH + j * BLOCK, BLOCK), BLOCK)
        panel[block_rows(slot), lanes] = coupled(slot, half, j)

    def even(n):
        return (n + 1) // 2 * 2

    count = jnp.int32(0)
    for base, size, ends in ((next_base, SNODE_BLOCKS, (SNODE_BLOCKS,) * PANELS), (0, row_count, (even(rows_first), even(rows_both))), (col_base, col_count, (even(cols_first), even(cols_both)))):
        for at in range(size):
            for half in range(PANELS):
                units[count] = 2 * (base + at) + half
                count = count + jnp.int32(at < ends[half])
    for n in range(UNITS):
        units[count + n] = 2 * lead_base + 1

    first_count = jnp.int32(0)
    for base, size, used in ((0, row_count, rows_first), (col_base, col_count, cols_first)):
        for c in range(0, size, 2):
            firsts[first_count] = base + c
            first_count = first_count + (c < used).astype(jnp.int32)
    for n in range(FIRSTS):
        firsts[first_count + n] = lead_base

    for j in range(SNODE_BLOCKS):
        prepare(lead_base + j)
        prepare_lead(j)
    for i in range(SNODE_BLOCKS):
        for j in range(SNODE_BLOCKS):
            value = coupled(lead_base + i, 0, j)
            diagonal[i * BLOCK : (i + 1) * BLOCK, j * BLOCK : (j + 1) * BLOCK] = value + eye(BLOCK) if i == j else value

    def run(parts, count):
        for n in range(count):
            for part in parts[len(parts) * n // count : len(parts) * (n + 1) // count]:
                part()
            yield

    parts = [functools.partial(prepare_lead, j) for j in range(SNODE_BLOCKS, LEAD)]
    parts += [functools.partial(prepare, slot) for slot in range(lead_base)]
    parts += [functools.partial(prepare_col, k) for k in range(col_count)]

    def couple_beside(step, part):
        n = step * STRIPS + part
        for unit in range(2):
            for j in range(SNODE_BLOCKS):
                couple(2 * n + unit, j)

    factor_diagonal(diagonal, x_full, work, run(parts, 20), couple_beside)
    x_high[...], x_low[...] = split(x_full[...])

    def couple_more(step, carry):
        for n in range(2):
            for j in range(SNODE_BLOCKS):
                couple(UNITS + 2 * step + n, j)
        return carry

    lax.fori_loop(0, (jnp.maximum(count - UNITS, 0) + 1) // 2, couple_more, 0)
    for i in range(lead_rows):
        at = slice(i * BLOCK, (i + 1) * BLOCK)
        lanes = pl.ds(pl.multiple_of((i * rows_n + prow_at) * BLOCK, BLOCK), BLOCK)
        panel[at, lanes] = panel[at, lanes] + eye(BLOCK)

    middle = WIDTH // 2

    def solve(at, first):
        a_high, a_low = split(panel[at, first : first + WIDTH])
        for begin, end in ((0, middle), (middle, WIDTH)):
            part = mm3(a_high[:, :end], a_low[:, :end], x_high[begin:end, :end], x_low[begin:end, :end], NT)
            lanes = slice(first + begin, first + end)
            panel[at, lanes] = part
            high[at, lanes], low[at, lanes] = split(part)

    next_rows = slice(next_base * BLOCK, lead_base * BLOCK)
    for c in range(next_base, lead_base, 2):
        solve(pair_rows(c), 0)

    def subtract(at, out_ref, out_at):
        for lanes in (slice(0, middle), slice(middle, WIDTH)):
            rows = slice(next_base * BLOCK + lanes.start, next_base * BLOCK + lanes.stop)
            done = mm3(high[at, :WIDTH], low[at, :WIDTH], high[rows, :WIDTH], low[rows, :WIDTH], NT)
            from_at = slice(WIDTH + lanes.start, WIDTH + lanes.stop)
            if out_ref is panel:
                panel[at, from_at] = panel[at, from_at] - done
            else:
                out_ref[out_at, lanes] = panel[at, from_at] - done

    for c in range(0, SNODE_BLOCKS, 2):
        subtract(pair_rows(next_base + c), diagonal, slice(c * BLOCK, (c + 2) * BLOCK))
    for j in range(SNODE_BLOCKS):
        at = slice(j * BLOCK, (j + 1) * BLOCK)
        diagonal[at, at] = diagonal[at, at] + eye(BLOCK)

    def first_solve(n):
        solve(pair_rows(firsts[n]), 0)

    def first_subtract(n):
        subtract(pair_rows(firsts[n]), panel, None)

    def first_beside(step, part):
        if part == 0:
            first_solve(step)
        else:
            first_subtract(step)

    factor_diagonal(diagonal, x_full, work, iter(()), first_beside)

    def first_more(n, carry):
        first_solve(n)
        first_subtract(n)
        return carry

    lax.fori_loop(FIRSTS, first_count, first_more, 0)
    x_high[...], x_low[...] = split(x_full[...])
    row_chunks = (rows_both + 1) // 2
    second_count = row_chunks + (cols_both + 1) // 2

    def second(step, carry):
        for n in range(2):
            c = 2 * step + n
            slot = jnp.where(c < row_chunks, 2 * c, col_base + 2 * (c - row_chunks))
            solve(pair_rows(jnp.where(c < second_count, slot, lead_base)), WIDTH)
        return carry

    lax.fori_loop(0, (second_count + 1) // 2, second, 0)
    for i in range(lead_rows):
        if i * rows_n < SNODE_BLOCKS:

            @pl.when(i * rows_n + prow_at < SNODE_BLOCKS)
            def _(i=i):
                panel[i * BLOCK : (i + 1) * BLOCK, WIDTH:] = jnp.zeros((BLOCK, WIDTH), f32)

    per_slot = BLOCK * col_count
    row_live = (rows_both + 1) // 2
    row_two = (rows_first + 1) // 2
    col_live = (cols_both + 1) // 2
    col_two = (cols_first + 1) // 2

    def copies_out(step, half):
        made = []
        for q in range(2):
            at = pl.multiple_of(place[2 * step + q] * per_slot, per_slot)
            made.append(
                pltpu.make_async_copy(stage.at[half, pl.ds(q * per_slot, per_slot), :], out.at[pl.ds(at, per_slot), :], sems.at[half, q])
            )
        return made

    def trail(step, carry):
        half = step % 2

        @pl.when(step >= 2)
        def _():
            for copy in copies_out(step - 2, half):
                copy.wait()

        def spots(q, k):
            return pl.ds(q * per_slot + k, BLOCK, stride=col_count)

        def tiles(c, carry):
            live = (step < row_live) & (c < col_live) & (step >= lead_rows // 2)
            two = (step < row_two) & (c < col_two)
            row_at = pair_rows(2 * step)
            col_at = pair_rows(col_base + 2 * c)

            def body(first):
                tiles = []
                for q in range(2):
                    slot = 2 * step + q
                    value = wendland(mm(left[slot], right_cols[c], TN), shape)
                    for e in range(2):
                        spot = col_base + 2 * c + e
                        factor = scale_cols[pl.ds(2 * c + e, 1), :] * (weight(table[slot], table[spot], pattern) * shape["gain"])
                        tiles.append(value[:, e * BLOCK : (e + 1) * BLOCK] * scale_rows[slot] * factor)
                update = mm3(high[row_at, first:], low[row_at, first:], high[col_at, first:], low[col_at, first:], NT)
                for q in range(2):
                    g = table[2 * step + q]
                    for e in range(2):
                        spot = col_base + 2 * c + e
                        tile = tiles[2 * q + e] - update[q * BLOCK : (q + 1) * BLOCK, e * BLOCK : (e + 1) * BLOCK]
                        if lead_rows % 2:
                            tile = tile * (g >= LEAD).astype(f32)
                        stage[half, spots(q, place[spot]), :] = tile

            @pl.when(live & two)
            def _():
                body(0)

            @pl.when(live & jnp.logical_not(two))
            def _():
                body(WIDTH)

            @pl.when(jnp.logical_not(live))
            def _():
                for q in range(2):
                    for e in range(2):
                        stage[half, spots(q, place[col_base + 2 * c + e]), :] = jnp.zeros((BLOCK, BLOCK), f32)

            return carry

        lax.fori_loop(0, col_count // 2, tiles, 0)
        for q in range(2):
            slot = 2 * step + q
            g = table[slot]
            k_same = g // cols_n
            here = (k_same * cols_n + pcol_at == g) & (g >= LEAD)
            same = spots(q, k_same)

            @pl.when(here & (slot >= rows_both))
            def _(slot=slot, g=g, same=same):
                m = inverse[g]
                value = wendland(mm(left[slot], right_features(points[m]), TN), shape)
                factor = scale_gain * lax.rsqrt(1.0 + totals[pl.ds(m, 1), :]) * (weight(g, g, pattern) * shape["gain"])
                stage[half, same, :] = value * scale_rows[slot] * factor

            @pl.when(here)
            def _(same=same):
                stage[half, same, :] = stage[half, same, :] + eye(BLOCK)

            for k in range(col_count):
                if k * cols_n < LEAD:
                    j = k * cols_n + pcol_at

                    filled = slot < jnp.where(j < SNODE_BLOCKS, even(rows_first), even(rows_both))

                    @pl.when((j < LEAD) & filled)
                    def _(k=k, j=j, q=q, slot=slot):
                        where = pl.ds(pl.multiple_of(j * BLOCK, BLOCK), BLOCK)
                        stage[half, spots(q, k), :] = panel[block_rows(slot), where]

                    @pl.when((j < LEAD) & jnp.logical_not(filled))
                    def _(k=k, q=q):
                        stage[half, spots(q, k), :] = jnp.zeros((BLOCK, BLOCK), f32)

        for copy in copies_out(step, half):
            copy.start()
        return carry

    steps = row_count // 2
    lax.fori_loop(0, steps, trail, 0)
    for step in range(max(steps - 2, 0), steps):
        for copy in copies_out(step, step % 2):
            copy.wait()


def local(coords, block_map, pattern):
    rows_n = lax.axis_size("prow")
    cols_n = lax.axis_size("pcol")
    devices = rows_n * cols_n
    nblocks = block_map.shape[0]
    per = nblocks // devices
    row_count = nblocks // rows_n
    col_count = nblocks // cols_n
    radius = (spread_factor / (nblocks * BLOCK)) ** (1.0 / 3.0)
    slots = row_count + col_count + LEAD
    rows_kept = (slots - SNODE_BLOCKS + 2) * BLOCK
    axes = ("prow", "pcol")
    smem = pl.BlockSpec(memory_space=pltpu.SMEM)
    vmem = pl.BlockSpec(memory_space=pltpu.VMEM)
    params = pltpu.CompilerParams(vmem_limit_bytes=VMEM_BYTES)
    shape = shape_of(radius)
    mine = pl.pallas_call(
        functools.partial(spread_kernel, per),
        out_shape=jax.ShapeDtypeStruct((devices, per, 4, BLOCK), jnp.int32),
        in_specs=[vmem],
        out_specs=vmem,
        name="spread",
    )(coords)
    points = lax.all_to_all(mine, axes, 0, 0, tiled=True).reshape(nblocks, 4, BLOCK)
    sums = pl.pallas_call(
        functools.partial(sums_kernel, shape, per),
        out_shape=jax.ShapeDtypeStruct((devices, per, BLOCK), f32),
        in_specs=[smem, smem, vmem],
        out_specs=vmem,
        scratch_shapes=[
            pltpu.VMEM((nblocks, FEATURES, BLOCK), bf16),
            pltpu.SMEM((per, nblocks + GROUP), jnp.int32),
            pltpu.SMEM((per, nblocks + GROUP), f32),
        ],
        compiler_params=params,
        name="sums",
    )(block_map, pattern, points)
    totals = lax.all_to_all(sums, axes, 0, 0, tiled=True).reshape(nblocks, BLOCK)
    out = pl.pallas_call(
        functools.partial(panels_kernel, shape, rows_n, cols_n),
        out_shape=jax.ShapeDtypeStruct((row_count * BLOCK * col_count, BLOCK), f32),
        in_specs=[smem, smem, vmem, vmem],
        out_specs=pl.BlockSpec(memory_space=pl.ANY),
        scratch_shapes=[
            pltpu.SMEM((nblocks,), jnp.int32),
            pltpu.SMEM((slots,), jnp.int32),
            pltpu.SMEM((slots,), jnp.int32),
            pltpu.SMEM((2 * slots + UNITS,), jnp.int32),
            pltpu.SMEM((slots + FIRSTS,), jnp.int32),
            pltpu.VMEM((rows_kept, PANELS * WIDTH), f32),
            pltpu.VMEM((rows_kept, PANELS * WIDTH), bf16),
            pltpu.VMEM((rows_kept, PANELS * WIDTH), bf16),
            pltpu.VMEM((slots, FEATURES, BLOCK), bf16),
            pltpu.VMEM((LEAD, FEATURES, BLOCK), bf16),
            pltpu.VMEM((col_count // 2, FEATURES, 2 * BLOCK), bf16),
            pltpu.VMEM((slots, BLOCK, BLOCK), f32),
            pltpu.VMEM((PANELS, SNODE_BLOCKS, BLOCK), f32),
            pltpu.VMEM((col_count, BLOCK), f32),
            pltpu.VMEM((WIDTH, WIDTH), f32),
            pltpu.VMEM((WIDTH, WIDTH), bf16),
            pltpu.VMEM((WIDTH, WIDTH), bf16),
            pltpu.VMEM((WIDTH, WIDTH), f32),
            pltpu.VMEM((2, 2 * BLOCK * col_count, BLOCK), f32),
            pltpu.SemaphoreType.DMA((2, 2)),
        ]
        + [pltpu.VMEM((BLOCK, 2 * BLOCK), f32)] * 4,
        compiler_params=params,
        name="panels",
    )(block_map, pattern, points, totals)
    return out.reshape(row_count, 1, BLOCK, col_count, 1, BLOCK)


def solution(mesh):
    placed = (P(None, ("prow", "pcol")), P(), P())
    return jax.shard_map(
        local,
        mesh=mesh,
        in_specs=placed,
        out_specs=P(None, "prow", None, None, "pcol", None),
        check_vma=False,
    )
```

```python
import functools

import jax
import jax.numpy as jnp
from jax import lax
from jax.experimental import pallas as pl
from jax.experimental.pallas import tpu as pltpu
from jax.sharding import PartitionSpec as P

BLOCK = 128
SNODE_BLOCKS = 4
PANELS = 2
LEAD = PANELS * SNODE_BLOCKS
WIDTH = SNODE_BLOCKS * BLOCK

spread_factor = 89.0
scale_gain = 8.0
grid_step = 1024.0

LOW, HIGH = 0.98, 66.0

f32 = jnp.float32
bf16 = jnp.bfloat16
NN = (((1,), (0,)), ((), ()))
NT = (((1,), (1,)), ((), ()))
TN = (((0,), (0,)), ((), ()))
FEATURES = 32
VMEM_BYTES = 60 * 1024 * 1024


def mm(a, b, dims):
    return lax.dot_general(a, b, dims, preferred_element_type=f32)


def split(a):
    high = a.astype(bf16)
    low = (a - high.astype(f32)).astype(bf16)
    return high, low


def dot1(a, b, dims=NN):
    return mm(a.astype(bf16), b.astype(bf16), dims)


def mm3(a_high, a_low, b_high, b_low, dims):
    rows = a_high.shape[0]
    both = mm(jnp.concatenate([a_high, a_low], 0), b_high, dims)
    return (both[:rows] + both[rows:]) + mm(a_high, b_low, dims)


def dot3(a, b, dims=NN):
    a_high, a_low = split(a)
    b_high, b_low = split(b)
    return mm3(a_high, a_low, b_high, b_low, dims)


def eye(n):
    return (lax.broadcasted_iota(jnp.int32, (n, n), 0) == lax.broadcasted_iota(jnp.int32, (n, n), 1)).astype(f32)


def newton(blocks, n, beside):
    first = 2 / (LOW + HIGH)
    rho = (HIGH - LOW) / (HIGH + LOW)
    one = eye(n)
    step = 2 / (2 - rho * rho)
    rho = rho * rho / (2 - rho * rho)
    found = [(2 * step * first) * one - (step * first * first) * a for a in blocks]
    for at in range(5):
        dot = dot1 if at < 2 else dot3
        step = 2 / (2 - rho * rho) if at < 4 else 1.0
        rho = rho * rho / (2 - rho * rho)
        rest = [(2 * one) - dot(a, x) for a, x in zip(blocks, found)]
        next(beside, None)
        found = [step * dot(x, e) for x, e in zip(found, rest)]
        next(beside, None)
    return found


def chains(work, count, per_step, beside):
    sub = lax.broadcasted_iota(jnp.int32, (8, BLOCK), 0)
    lane = lax.broadcasted_iota(jnp.int32, (8, BLOCK), 1)
    zero = jnp.zeros((8, BLOCK), f32)

    def strip(step, part):
        n = step * per_step + part
        at = n * 8
        rows = pl.ds(pl.multiple_of(at, 8), 8)
        beside(step, part)
        state = []
        for b in range(count):
            r = work[b][rows, 0:BLOCK]
            y = work[b][rows, BLOCK : 2 * BLOCK]
            turned = pltpu.roll(r, lax.rem(BLOCK - at, BLOCK), 1)
            c = [jnp.broadcast_to(turned[:, k : k + 1], (8, BLOCK)) for k in range(8)]
            state.append([r, y, c])
        for k in range(8):
            for b in range(count):
                r, y, c = state[b]
                inv = lax.rsqrt(c[k][k : k + 1, :])
                column = c[k] * inv
                below = jnp.where(sub > k, column, 0.0)
                r_row = r[k : k + 1] * inv
                y_row = y[k : k + 1] * inv
                r = jnp.where(sub == k, r_row, r - below * r_row)
                y = jnp.where(sub == k, y_row, y - below * y_row)
                for m in range(k + 1, 8):
                    c[m] = c[m] - below * column[m : m + 1, :]
                state[b] = [r, y, c]
        later = lane >= at + 8
        for b in range(count):
            r, y, _ = state[b]
            work[b][rows, 0:BLOCK] = r
            work[b][rows, BLOCK : 2 * BLOCK] = y
            r_high = r.astype(bf16).astype(f32)
            y_high = y.astype(bf16).astype(f32)
            high = jnp.concatenate([r_high, y_high], 1)
            low = jnp.concatenate([r - r_high, y - y_high], 1)
            left_high = jnp.where(later, r_high, 0.0)
            left_low = jnp.where(later, r - r_high, 0.0)
            left = jnp.concatenate([left_high, left_high, left_low, zero], 0).astype(bf16)
            right = jnp.concatenate([high, low, high, jnp.concatenate([zero, zero], 1)], 0).astype(bf16)
            work[b][...] = work[b][...] - mm(left, right, TN)

    def strips(step, carry):
        for n in range(per_step):
            strip(step, n)
        return carry

    lax.fori_loop(0, BLOCK // 8 // per_step, strips, 0)


def factor_diagonal(a_ref, x_ref, work, beside_newton, per_step, beside_strip):
    half = 2 * BLOCK
    rows = lax.broadcasted_iota(jnp.int32, (BLOCK, BLOCK), 0)
    cols = lax.broadcasted_iota(jnp.int32, (BLOCK, BLOCK), 1)
    lower = cols <= rows
    a11 = a_ref[0:half, 0:half]
    a21 = a_ref[half:, 0:half]
    s2 = a_ref[half:, half:] - dot3(dot3(a21, newton([a11], half, beside_newton)[0]), a21, NT)
    corner = [a11[0:BLOCK, 0:BLOCK], s2[0:BLOCK, 0:BLOCK]]
    side = [a11[BLOCK:, 0:BLOCK], s2[BLOCK:, 0:BLOCK]]
    last = [a11[BLOCK:, BLOCK:], s2[BLOCK:, BLOCK:]]
    inverse = newton(corner, BLOCK, beside_newton)
    for i in range(2):
        work[2 * i][:, 0:BLOCK] = corner[i]
        work[2 * i + 1][:, 0:BLOCK] = last[i] - dot3(dot3(side[i], inverse[i]), side[i], NT)
    for b in range(4):
        work[b][:, BLOCK:] = eye(BLOCK)
    for _ in beside_newton:
        pass
    chains(work, 4, per_step, beside_strip)
    for i in range(2):
        at = half * i
        xa = jnp.where(lower, work[2 * i][:, BLOCK:], 0.0)
        xb = jnp.where(lower, work[2 * i + 1][:, BLOCK:], 0.0)
        l21 = dot3(side[i], xa, NT)
        x_ref[at : at + BLOCK, at : at + BLOCK] = xa
        x_ref[at : at + BLOCK, at + BLOCK : at + half] = jnp.zeros((BLOCK, BLOCK), f32)
        x_ref[at + BLOCK : at + half, at : at + BLOCK] = -dot3(xb, dot3(l21, xa))
        x_ref[at + BLOCK : at + half, at + BLOCK : at + half] = xb
    x11 = x_ref[0:half, 0:half]
    x22 = x_ref[half:, half:]
    l21 = dot3(a21, x11, NT)
    x_ref[half:, 0:half] = -dot3(x22, dot3(l21, x11))
    x_ref[0:half, half:] = jnp.zeros((half, half), f32)


def pieces(point):
    low = (point & 255).astype(f32)
    mid = ((point >> 8) & 255).astype(f32)
    top = (point >> 16).astype(f32)
    return low, mid, top


def left_features(point):
    low, mid, top = pieces(point)
    norm = lax.broadcasted_iota(jnp.int32, point.shape, 0) == 3
    one = jnp.ones_like(low)
    zero = jnp.zeros_like(low)
    return jnp.concatenate(
        [low, jnp.where(norm, one, low), mid, jnp.where(norm, one, mid), top, jnp.where(norm, one, zero), zero, zero], 0
    ).astype(bf16)


def right_features(point):
    low, mid, top = pieces(point)
    norm = lax.broadcasted_iota(jnp.int32, point.shape, 0) == 3
    one = jnp.ones_like(low)
    zero = jnp.zeros_like(low)
    return jnp.concatenate(
        [
            jnp.where(norm, one, -2.0 * low),
            jnp.where(norm, low, -512.0 * mid),
            jnp.where(norm, 256.0 * one, -512.0 * low),
            jnp.where(norm, 256.0 * mid, -131072.0 * mid),
            jnp.where(norm, 65536.0 * one, zero),
            jnp.where(norm, 65536.0 * top, zero),
            zero,
            zero,
        ],
        0,
    ).astype(bf16)


def shape_of(radius):
    unit = 1.0 / (grid_step * radius)
    shift = 9.0 / (35.0 * unit)
    return {"reach": 1.0 / unit, "shift": shift, "bias": 3.0 / (35.0 * unit * unit) - shift * shift, "gain": 35.0 / 3.0 * unit**8}


def wendland(dist_sq, shape):
    dist = dist_sq * lax.rsqrt(jnp.maximum(dist_sq, 1.0))
    rest = jnp.maximum(shape["reach"] - dist, 0.0)
    rest_sq = rest * rest
    moved = dist + shape["shift"]
    return (rest_sq * rest_sq) * (rest_sq * (moved * moved + shape["bias"]))


def member(panel_at, block, pattern):
    first = panel_at * SNODE_BLOCKS
    own = (block >= first) & (block < first + SNODE_BLOCKS)
    return jnp.where(own, 1, jnp.where(block < first, 0, pattern[panel_at, block]))


def weight(row, col, pattern):
    value = (row == col).astype(jnp.int32)
    for panel_at in range(PANELS):
        value = value + member(panel_at, row, pattern) * member(panel_at, col, pattern)
    return value.astype(f32)


SCAN = 4
GROUP = 8
UNITS = 32
FIRSTS = 4
CHUNK = 4


def sums_kernel(shape, per, block_map, pattern, points, out, left, lists, weights):
    nblocks = points.shape[0]
    me = lax.axis_index("prow") * lax.axis_size("pcol") + lax.axis_index("pcol")
    own = [block_map[me * per + b] for b in range(per)]
    right = [right_features(points[me * per + b]) for b in range(per)]

    def scan_block(m, counts):
        left[m] = left_features(points[m])
        after = []
        for b in range(per):
            value = weight(own[b], block_map[m], pattern)
            lists[b, counts[b]] = m
            weights[b, counts[b]] = value * shape["gain"]
            after.append(counts[b] + (value > 0).astype(jnp.int32))
        return tuple(after)

    def scan_blocks(step, counts):
        for n in range(SCAN):
            counts = scan_block(step * SCAN + n, counts)
        return counts

    counts = lax.fori_loop(0, nblocks // SCAN, scan_blocks, (0,) * per)
    for b in range(per):
        for g in range(GROUP):
            lists[b, counts[b] + g] = 0
            weights[b, counts[b] + g] = 0.0

    for b in range(per):

        def group(step, total):
            parts = []
            for g in range(GROUP):
                at = step * GROUP + g
                value = wendland(mm(left[lists[b, at]], right[b], TN), shape)
                parts.append(jnp.sum(value.reshape(BLOCK // 8, 8, BLOCK), axis=0) * weights[b, at])
            return total + functools.reduce(lambda x, y: x + y, parts)

        total = lax.fori_loop(0, (counts[b] + GROUP - 1) // GROUP, group, jnp.zeros((8, BLOCK), f32))
        row = jnp.sum(total, axis=0, keepdims=True)
        for d in range(out.shape[0]):
            out[d, b : b + 1, :] = row


def spread_kernel(per, coords, out):
    for b in range(per):
        point = coords[:, b * BLOCK : (b + 1) * BLOCK]
        norm = jnp.sum(point * point, axis=0, keepdims=True)
        point = jnp.concatenate([point, norm], 0)
        for d in range(out.shape[0]):
            out[d, b] = point


def panels_kernel(
    shape, rows_n, cols_n, block_map, pattern, points, totals, out,
    inverse, table, place, units, firsts, panel, high, low, left, right_lead, right_cols, scale_rows, scale_lead, scale_cols,
    diagonal, x_high, x_low, x_full, stage, sems, *work,
):
    nblocks = points.shape[0]
    row_count = nblocks // rows_n
    col_count = nblocks // cols_n
    prow_at = lax.axis_index("prow")
    pcol_at = lax.axis_index("pcol")
    col_base = row_count
    next_base = row_count + col_count
    lead_base = next_base + SNODE_BLOCKS
    slots = lead_base + SNODE_BLOCKS
    lead_rows = LEAD // rows_n

    def invert(m, carry):
        inverse[block_map[m]] = m
        return carry

    lax.fori_loop(0, nblocks, invert, 0)

    def block_rows(slot):
        return pl.ds(pl.multiple_of(slot * BLOCK, BLOCK), BLOCK)

    def pair_rows(slot):
        return pl.ds(pl.multiple_of(slot * BLOCK, 2 * BLOCK), 2 * BLOCK)

    def chunk_rows(slot):
        return pl.ds(pl.multiple_of(slot * BLOCK, CHUNK * BLOCK), CHUNK * BLOCK)

    def scale_of(m):
        return scale_gain * lax.rsqrt(1.0 + totals[pl.ds(m, 1), :])

    def prepare(slot):
        m = inverse[table[slot]]
        left[slot] = left_features(points[m])
        scale_rows[slot] = jnp.broadcast_to(scale_of(m), (BLOCK, BLOCK)).T

    def prepare_lead(j):
        m = inverse[j]
        half, at = divmod(j, SNODE_BLOCKS)
        right_lead[j] = right_features(points[m])
        scale_lead[half, at : at + 1, :] = scale_of(m)

    def prepare_col(k):
        m = inverse[table[col_base + k]]
        right_cols[k // 2, :, k % 2 * BLOCK : (k % 2 + 1) * BLOCK] = right_features(points[m])
        scale_cols[k : k + 1, :] = scale_of(m)

    def coupled(slot, half, j):
        value = wendland(mm(left[slot], right_lead[half * SNODE_BLOCKS + j], TN), shape)
        scale = scale_lead[half, j : j + 1, :] * (weight(table[slot], half * SNODE_BLOCKS + j, pattern) * shape["gain"])
        return value * scale_rows[slot] * scale

    def couple(at, j):
        unit = units[at]
        slot = unit // 2
        half = unit % 2
        lanes = pl.ds(pl.multiple_of(half * WIDTH + j * BLOCK, BLOCK), BLOCK)
        panel[block_rows(slot), lanes] = coupled(slot, half, j)

    for j in range(SNODE_BLOCKS):
        table[next_base + j] = SNODE_BLOCKS + j
        table[lead_base + j] = j
    for j in range(SNODE_BLOCKS):
        prepare(lead_base + j)
        prepare_lead(j)
    for i in range(SNODE_BLOCKS):
        for j in range(SNODE_BLOCKS):
            value = coupled(lead_base + i, 0, j)
            diagonal[i * BLOCK : (i + 1) * BLOCK, j * BLOCK : (j + 1) * BLOCK] = value + eye(BLOCK) if i == j else value

    def sort(base, blocks, lead):
        kinds = []
        first = second = jnp.int32(0)
        for g, at in blocks:
            in_first = member(0, g, pattern) > 0
            in_second = member(1, g, pattern) > 0
            dead = g < LEAD
            kind = jnp.where(dead, 2, jnp.where(in_first, 0, jnp.where(in_second, 1, 2)))
            kinds.append(kind)
            first = first + (kind == 0).astype(jnp.int32)
            second = second + (kind == 1).astype(jnp.int32)
        spots = [base + lead, base + lead + first, base + lead + first + second]
        for (g, at), kind in zip(blocks, kinds):
            spot = jnp.where(kind == 0, spots[0], jnp.where(kind == 1, spots[1], spots[2]))
            table[spot] = g
            place[spot] = at
            for n in range(3):
                spots[n] = spots[n] + (kind == n).astype(jnp.int32)
        return lead + first, lead + first + second

    for i in range(lead_rows):
        table[i] = i * rows_n + prow_at
        place[i] = i
    rows_first, rows_both = sort(0, [(i * rows_n + prow_at, i) for i in range(lead_rows, row_count)], lead_rows)
    cols_first, cols_both = sort(col_base, [(k * cols_n + pcol_at, k) for k in range(col_count)], 0)
    def whole(n):
        return (n + CHUNK - 1) // CHUNK * CHUNK

    count = jnp.int32(0)
    for base, size, ends in ((next_base, SNODE_BLOCKS, (SNODE_BLOCKS,) * PANELS), (0, row_count, (rows_first, rows_both)), (col_base, col_count, (cols_first, cols_both))):
        for at in range(size):
            for half in range(PANELS):
                units[count] = 2 * (base + at) + half
                count = count + jnp.int32(at < ends[half])
    for n in range(UNITS):
        units[count + n] = 2 * lead_base + 1

    first_count = jnp.int32(0)
    for base, size, used in ((0, row_count, rows_first), (col_base, col_count, cols_first)):
        for c in range(0, size, CHUNK):
            firsts[first_count] = base + c
            first_count = first_count + (c < used).astype(jnp.int32)
    for n in range(FIRSTS):
        firsts[first_count + n] = lead_base

    def run(parts, count):
        for n in range(count):
            for part in parts[len(parts) * n // count : len(parts) * (n + 1) // count]:
                part()
            yield

    parts = [functools.partial(prepare_lead, j) for j in range(SNODE_BLOCKS, LEAD)]
    parts += [functools.partial(prepare, slot) for slot in range(lead_base)]
    parts += [functools.partial(prepare_col, k) for k in range(col_count)]

    def couple_beside(step, part):
        n = 2 * step + part
        for unit in range(2):
            for j in range(SNODE_BLOCKS):
                couple(2 * n + unit, j)

    factor_diagonal(diagonal, x_full, work, run(parts, 20), 2, couple_beside)
    x_high[...], x_low[...] = split(x_full[...])

    def couple_more(step, carry):
        for n in range(2):
            for j in range(SNODE_BLOCKS):
                couple(UNITS + 2 * step + n, j)
        return carry

    lax.fori_loop(0, (jnp.maximum(count - UNITS, 0) + 1) // 2, couple_more, 0)
    for base, ends in ((0, (rows_first, rows_both)), (col_base, (cols_first, cols_both))):
        for half, end in enumerate(ends):

            def clear(slot, carry, half=half):
                panel[block_rows(slot), half * WIDTH : (half + 1) * WIDTH] = jnp.zeros((BLOCK, WIDTH), f32)
                return carry

            lax.fori_loop(base + end, base + whole(end), clear, 0)
    for i in range(lead_rows):
        at = slice(i * BLOCK, (i + 1) * BLOCK)
        lanes = pl.ds(pl.multiple_of((i * rows_n + prow_at) * BLOCK, BLOCK), BLOCK)
        panel[at, lanes] = panel[at, lanes] + eye(BLOCK)

    middle = WIDTH // 2

    def solve(at, first):
        a_high, a_low = split(panel[at, first : first + WIDTH])
        for begin, end in ((0, middle), (middle, WIDTH)):
            part = mm3(a_high[:, :end], a_low[:, :end], x_high[begin:end, :end], x_low[begin:end, :end], NT)
            lanes = slice(first + begin, first + end)
            panel[at, lanes] = part
            high[at, lanes], low[at, lanes] = split(part)

    next_rows = slice(next_base * BLOCK, lead_base * BLOCK)
    solve(next_rows, 0)

    def subtract(at, out_ref, out_at):
        for lanes in (slice(0, middle), slice(middle, WIDTH)):
            rows = slice(next_base * BLOCK + lanes.start, next_base * BLOCK + lanes.stop)
            done = mm3(high[at, :WIDTH], low[at, :WIDTH], high[rows, :WIDTH], low[rows, :WIDTH], NT)
            from_at = slice(WIDTH + lanes.start, WIDTH + lanes.stop)
            if out_ref is panel:
                panel[at, from_at] = panel[at, from_at] - done
            else:
                out_ref[out_at, lanes] = panel[at, from_at] - done

    subtract(next_rows, diagonal, slice(0, WIDTH))
    for j in range(SNODE_BLOCKS):
        at = slice(j * BLOCK, (j + 1) * BLOCK)
        diagonal[at, at] = diagonal[at, at] + eye(BLOCK)

    def first_solve(n):
        solve(chunk_rows(firsts[n]), 0)

    def first_subtract(n):
        subtract(chunk_rows(firsts[n]), panel, None)

    def first_beside(step, part):
        if part == 0:
            first_solve(step)
        if part == 2:
            first_subtract(step)

    factor_diagonal(diagonal, x_full, work, iter(()), 4, first_beside)

    def first_more(n, carry):
        first_solve(n)
        first_subtract(n)
        return carry

    lax.fori_loop(FIRSTS, first_count, first_more, 0)
    x_high[...], x_low[...] = split(x_full[...])
    row_chunks = whole(rows_both) // CHUNK

    def second(c, carry):
        slot = jnp.where(c < row_chunks, CHUNK * c, col_base + CHUNK * (c - row_chunks))
        solve(chunk_rows(slot), WIDTH)
        return carry

    lax.fori_loop(0, row_chunks + whole(cols_both) // CHUNK, second, 0)
    for i in range(lead_rows):
        if i * rows_n < SNODE_BLOCKS:

            @pl.when(i * rows_n + prow_at < SNODE_BLOCKS)
            def _(i=i):
                panel[i * BLOCK : (i + 1) * BLOCK, WIDTH:] = jnp.zeros((BLOCK, WIDTH), f32)

    per_slot = BLOCK * col_count
    row_live = whole(rows_both) // CHUNK
    row_two = whole(rows_first) // CHUNK
    col_live = (cols_both + 1) // 2
    col_two = (cols_first + 1) // 2

    def copies_out(step, half):
        made = []
        for q in range(CHUNK):
            at = pl.multiple_of(place[CHUNK * step + q] * per_slot, per_slot)
            made.append(
                pltpu.make_async_copy(stage.at[half, pl.ds(q * per_slot, per_slot), :], out.at[pl.ds(at, per_slot), :], sems.at[half, q])
            )
        return made

    def trail(step, carry):
        half = step % 2

        @pl.when(step >= 2)
        def _():
            for copy in copies_out(step - 2, half):
                copy.wait()

        def spots(q, k):
            return pl.ds(q * per_slot + k, BLOCK, stride=col_count)

        def tiles(c, carry):
            live = (step < row_live) & (c < col_live)
            two = (step < row_two) & (c < col_two)
            row_at = chunk_rows(CHUNK * step)
            col_at = pair_rows(col_base + 2 * c)

            def body(first):
                tiles = []
                for q in range(CHUNK):
                    slot = CHUNK * step + q
                    value = wendland(mm(left[slot], right_cols[c], TN), shape)
                    for e in range(2):
                        spot = col_base + 2 * c + e
                        factor = scale_cols[pl.ds(2 * c + e, 1), :] * (weight(table[slot], table[spot], pattern) * shape["gain"])
                        tiles.append(value[:, e * BLOCK : (e + 1) * BLOCK] * scale_rows[slot] * factor)
                update = mm3(high[row_at, first:], low[row_at, first:], high[col_at, first:], low[col_at, first:], NT)
                for q in range(CHUNK):
                    for e in range(2):
                        spot = col_base + 2 * c + e
                        tile = tiles[2 * q + e] - update[q * BLOCK : (q + 1) * BLOCK, e * BLOCK : (e + 1) * BLOCK]
                        stage[half, spots(q, place[spot]), :] = tile

            @pl.when(live & two)
            def _():
                body(0)

            @pl.when(live & jnp.logical_not(two))
            def _():
                body(WIDTH)

            @pl.when(jnp.logical_not(live))
            def _():
                for q in range(CHUNK):
                    for e in range(2):
                        stage[half, spots(q, place[col_base + 2 * c + e]), :] = jnp.zeros((BLOCK, BLOCK), f32)

            return carry

        lax.fori_loop(0, col_count // 2, tiles, 0)

        @pl.when(step == 0)
        def _():
            for q in range(lead_rows):
                for k in range(col_count):
                    stage[half, spots(q, k), :] = jnp.zeros((BLOCK, BLOCK), f32)

        for q in range(CHUNK):
            slot = CHUNK * step + q
            g = table[slot]
            k_same = g // cols_n
            here = (k_same * cols_n + pcol_at == g) & (g >= LEAD)
            same = spots(q, k_same)

            @pl.when(here & (slot >= rows_both))
            def _(slot=slot, g=g, same=same):
                m = inverse[g]
                value = wendland(mm(left[slot], right_features(points[m]), TN), shape)
                factor = scale_gain * lax.rsqrt(1.0 + totals[pl.ds(m, 1), :]) * (weight(g, g, pattern) * shape["gain"])
                stage[half, same, :] = value * scale_rows[slot] * factor

            @pl.when(here)
            def _(same=same):
                stage[half, same, :] = stage[half, same, :] + eye(BLOCK)

            for k in range(col_count):
                if k * cols_n < LEAD:
                    j = k * cols_n + pcol_at

                    filled = slot < jnp.where(j < SNODE_BLOCKS, rows_first, rows_both)

                    @pl.when((j < LEAD) & filled)
                    def _(k=k, j=j, q=q, slot=slot):
                        where = pl.ds(pl.multiple_of(j * BLOCK, BLOCK), BLOCK)
                        stage[half, spots(q, k), :] = panel[block_rows(slot), where]

                    @pl.when((j < LEAD) & jnp.logical_not(filled))
                    def _(k=k, q=q):
                        stage[half, spots(q, k), :] = jnp.zeros((BLOCK, BLOCK), f32)

        for copy in copies_out(step, half):
            copy.start()
        return carry

    steps = row_count // CHUNK
    lax.fori_loop(0, steps, trail, 0)
    for step in range(max(steps - 2, 0), steps):
        for copy in copies_out(step, step % 2):
            copy.wait()


def local(coords, block_map, pattern):
    rows_n = lax.axis_size("prow")
    cols_n = lax.axis_size("pcol")
    devices = rows_n * cols_n
    nblocks = block_map.shape[0]
    per = nblocks // devices
    row_count = nblocks // rows_n
    col_count = nblocks // cols_n
    radius = (spread_factor / (nblocks * BLOCK)) ** (1.0 / 3.0)
    slots = row_count + col_count + LEAD
    rows_kept = (slots - SNODE_BLOCKS + CHUNK) * BLOCK
    axes = ("prow", "pcol")
    smem = pl.BlockSpec(memory_space=pltpu.SMEM)
    vmem = pl.BlockSpec(memory_space=pltpu.VMEM)
    params = pltpu.CompilerParams(vmem_limit_bytes=VMEM_BYTES)
    shape = shape_of(radius)
    mine = pl.pallas_call(
        functools.partial(spread_kernel, per),
        out_shape=jax.ShapeDtypeStruct((devices, per, 4, BLOCK), jnp.int32),
        in_specs=[vmem],
        out_specs=vmem,
        name="spread",
    )(coords)
    points = lax.all_to_all(mine, axes, 0, 0, tiled=True).reshape(nblocks, 4, BLOCK)
    sums = pl.pallas_call(
        functools.partial(sums_kernel, shape, per),
        out_shape=jax.ShapeDtypeStruct((devices, per, BLOCK), f32),
        in_specs=[smem, smem, vmem],
        out_specs=vmem,
        scratch_shapes=[
            pltpu.VMEM((nblocks, FEATURES, BLOCK), bf16),
            pltpu.SMEM((per, nblocks + GROUP), jnp.int32),
            pltpu.SMEM((per, nblocks + GROUP), f32),
        ],
        compiler_params=params,
        name="sums",
    )(block_map, pattern, points)
    totals = lax.all_to_all(sums, axes, 0, 0, tiled=True).reshape(nblocks, BLOCK)
    out = pl.pallas_call(
        functools.partial(panels_kernel, shape, rows_n, cols_n),
        out_shape=jax.ShapeDtypeStruct((row_count * BLOCK * col_count, BLOCK), f32),
        in_specs=[smem, smem, vmem, vmem],
        out_specs=pl.BlockSpec(memory_space=pl.ANY),
        scratch_shapes=[
            pltpu.SMEM((nblocks,), jnp.int32),
            pltpu.SMEM((slots,), jnp.int32),
            pltpu.SMEM((slots,), jnp.int32),
            pltpu.SMEM((2 * slots + UNITS,), jnp.int32),
            pltpu.SMEM((slots + FIRSTS,), jnp.int32),
            pltpu.VMEM((rows_kept, PANELS * WIDTH), f32),
            pltpu.VMEM((rows_kept, PANELS * WIDTH), bf16),
            pltpu.VMEM((rows_kept, PANELS * WIDTH), bf16),
            pltpu.VMEM((slots, FEATURES, BLOCK), bf16),
            pltpu.VMEM((LEAD, FEATURES, BLOCK), bf16),
            pltpu.VMEM((col_count // 2, FEATURES, 2 * BLOCK), bf16),
            pltpu.VMEM((slots, BLOCK, BLOCK), f32),
            pltpu.VMEM((PANELS, SNODE_BLOCKS, BLOCK), f32),
            pltpu.VMEM((col_count, BLOCK), f32),
            pltpu.VMEM((WIDTH, WIDTH), f32),
            pltpu.VMEM((WIDTH, WIDTH), bf16),
            pltpu.VMEM((WIDTH, WIDTH), bf16),
            pltpu.VMEM((WIDTH, WIDTH), f32),
            pltpu.VMEM((2, CHUNK * BLOCK * col_count, BLOCK), f32),
            pltpu.SemaphoreType.DMA((2, CHUNK)),
        ]
        + [pltpu.VMEM((BLOCK, 2 * BLOCK), f32)] * 4,
        compiler_params=params,
        name="panels",
    )(block_map, pattern, points, totals)
    return out.reshape(row_count, 1, BLOCK, col_count, 1, BLOCK)


def solution(mesh):
    placed = (P(None, ("prow", "pcol")), P(), P())
    return jax.shard_map(
        local,
        mesh=mesh,
        in_specs=placed,
        out_specs=P(None, "prow", None, None, "pcol", None),
        check_vma=False,
    )
```

```python
import functools

import jax
import jax.numpy as jnp
from jax import lax
from jax.experimental import pallas as pl
from jax.experimental.pallas import tpu as pltpu
from jax.sharding import PartitionSpec as P

BLOCK = 128
SNODE_BLOCKS = 4
PANELS = 2
LEAD = PANELS * SNODE_BLOCKS
WIDTH = SNODE_BLOCKS * BLOCK

spread_factor = 89.0
scale_gain = 8.0
grid_step = 1024.0

LOW, HIGH = 0.98, 66.0

f32 = jnp.float32
bf16 = jnp.bfloat16
NN = (((1,), (0,)), ((), ()))
NT = (((1,), (1,)), ((), ()))
TN = (((0,), (0,)), ((), ()))
FEATURES = 32
VMEM_BYTES = 60 * 1024 * 1024


def mm(a, b, dims):
    return lax.dot_general(a, b, dims, preferred_element_type=f32)


def split(a):
    high = a.astype(bf16)
    low = (a - high.astype(f32)).astype(bf16)
    return high, low


def dot1(a, b, dims=NN):
    return mm(a.astype(bf16), b.astype(bf16), dims)


def mm3(a_high, a_low, b_high, b_low, dims):
    rows = a_high.shape[0]
    both = mm(jnp.concatenate([a_high, a_low], 0), b_high, dims)
    return (both[:rows] + both[rows:]) + mm(a_high, b_low, dims)


def dot3(a, b, dims=NN):
    a_high, a_low = split(a)
    b_high, b_low = split(b)
    return mm3(a_high, a_low, b_high, b_low, dims)


def eye(n):
    return (lax.broadcasted_iota(jnp.int32, (n, n), 0) == lax.broadcasted_iota(jnp.int32, (n, n), 1)).astype(f32)


def newton(blocks, n, beside):
    first = 2 / (LOW + HIGH)
    rho = (HIGH - LOW) / (HIGH + LOW)
    one = eye(n)
    step = 2 / (2 - rho * rho)
    rho = rho * rho / (2 - rho * rho)
    found = [(2 * step * first) * one - (step * first * first) * a for a in blocks]
    for at in range(5):
        dot = dot1 if at < 2 else dot3
        step = 2 / (2 - rho * rho) if at < 4 else 1.0
        rho = rho * rho / (2 - rho * rho)
        rest = [(2 * one) - dot(a, x) for a, x in zip(blocks, found)]
        next(beside, None)
        found = [step * dot(x, e) for x, e in zip(found, rest)]
        next(beside, None)
    return found


def chains(work, count, per_step, beside):
    sub = lax.broadcasted_iota(jnp.int32, (8, BLOCK), 0)
    lane = lax.broadcasted_iota(jnp.int32, (8, BLOCK), 1)
    zero = jnp.zeros((8, BLOCK), f32)

    def strip(step, part):
        n = step * per_step + part
        at = n * 8
        rows = pl.ds(pl.multiple_of(at, 8), 8)
        beside(step, part)
        state = []
        for b in range(count):
            r = work[b][rows, 0:BLOCK]
            y = work[b][rows, BLOCK : 2 * BLOCK]
            turned = pltpu.roll(r, lax.rem(BLOCK - at, BLOCK), 1)
            c = [jnp.broadcast_to(turned[:, k : k + 1], (8, BLOCK)) for k in range(8)]
            state.append([r, y, c])
        for k in range(8):
            for b in range(count):
                r, y, c = state[b]
                inv = lax.rsqrt(c[k][k : k + 1, :])
                column = c[k] * inv
                below = jnp.where(sub > k, column, 0.0)
                r_row = r[k : k + 1] * inv
                y_row = y[k : k + 1] * inv
                r = jnp.where(sub == k, r_row, r - below * r_row)
                y = jnp.where(sub == k, y_row, y - below * y_row)
                for m in range(k + 1, 8):
                    c[m] = c[m] - below * column[m : m + 1, :]
                state[b] = [r, y, c]
        later = lane >= at + 8
        for b in range(count):
            r, y, _ = state[b]
            work[b][rows, 0:BLOCK] = r
            work[b][rows, BLOCK : 2 * BLOCK] = y
            r_high = r.astype(bf16).astype(f32)
            y_high = y.astype(bf16).astype(f32)
            high = jnp.concatenate([r_high, y_high], 1)
            low = jnp.concatenate([r - r_high, y - y_high], 1)
            left_high = jnp.where(later, r_high, 0.0)
            left_low = jnp.where(later, r - r_high, 0.0)
            left = jnp.concatenate([left_high, left_high, left_low, zero], 0).astype(bf16)
            right = jnp.concatenate([high, low, high, jnp.concatenate([zero, zero], 1)], 0).astype(bf16)
            work[b][...] = work[b][...] - mm(left, right, TN)

    def strips(step, carry):
        for n in range(per_step):
            strip(step, n)
        return carry

    lax.fori_loop(0, BLOCK // 8 // per_step, strips, 0)


def factor_diagonal(a_ref, x_ref, work, beside_newton, per_step, beside_strip):
    half = 2 * BLOCK
    rows = lax.broadcasted_iota(jnp.int32, (BLOCK, BLOCK), 0)
    cols = lax.broadcasted_iota(jnp.int32, (BLOCK, BLOCK), 1)
    lower = cols <= rows
    a11 = a_ref[0:half, 0:half]
    a21 = a_ref[half:, 0:half]
    s2 = a_ref[half:, half:] - dot3(dot3(a21, newton([a11], half, beside_newton)[0]), a21, NT)
    corner = [a11[0:BLOCK, 0:BLOCK], s2[0:BLOCK, 0:BLOCK]]
    side = [a11[BLOCK:, 0:BLOCK], s2[BLOCK:, 0:BLOCK]]
    last = [a11[BLOCK:, BLOCK:], s2[BLOCK:, BLOCK:]]
    inverse = newton(corner, BLOCK, beside_newton)
    for i in range(2):
        work[2 * i][:, 0:BLOCK] = corner[i]
        work[2 * i + 1][:, 0:BLOCK] = last[i] - dot3(dot3(side[i], inverse[i]), side[i], NT)
    for b in range(4):
        work[b][:, BLOCK:] = eye(BLOCK)
    for _ in beside_newton:
        pass
    chains(work, 4, per_step, beside_strip)
    for i in range(2):
        at = half * i
        xa = jnp.where(lower, work[2 * i][:, BLOCK:], 0.0)
        xb = jnp.where(lower, work[2 * i + 1][:, BLOCK:], 0.0)
        l21 = dot3(side[i], xa, NT)
        x_ref[at : at + BLOCK, at : at + BLOCK] = xa
        x_ref[at : at + BLOCK, at + BLOCK : at + half] = jnp.zeros((BLOCK, BLOCK), f32)
        x_ref[at + BLOCK : at + half, at : at + BLOCK] = -dot3(xb, dot3(l21, xa))
        x_ref[at + BLOCK : at + half, at + BLOCK : at + half] = xb
    x11 = x_ref[0:half, 0:half]
    x22 = x_ref[half:, half:]
    l21 = dot3(a21, x11, NT)
    x_ref[half:, 0:half] = -dot3(x22, dot3(l21, x11))
    x_ref[0:half, half:] = jnp.zeros((half, half), f32)


def pieces(point):
    low = (point & 255).astype(f32)
    mid = ((point >> 8) & 255).astype(f32)
    top = (point >> 16).astype(f32)
    return low, mid, top


def left_features(point):
    low, mid, top = pieces(point)
    norm = lax.broadcasted_iota(jnp.int32, point.shape, 0) == 3
    one = jnp.ones_like(low)
    zero = jnp.zeros_like(low)
    return jnp.concatenate(
        [low, jnp.where(norm, one, low), mid, jnp.where(norm, one, mid), top, jnp.where(norm, one, zero), zero, zero], 0
    ).astype(bf16)


def right_features(point):
    low, mid, top = pieces(point)
    norm = lax.broadcasted_iota(jnp.int32, point.shape, 0) == 3
    one = jnp.ones_like(low)
    zero = jnp.zeros_like(low)
    return jnp.concatenate(
        [
            jnp.where(norm, one, -2.0 * low),
            jnp.where(norm, low, -512.0 * mid),
            jnp.where(norm, 256.0 * one, -512.0 * low),
            jnp.where(norm, 256.0 * mid, -131072.0 * mid),
            jnp.where(norm, 65536.0 * one, zero),
            jnp.where(norm, 65536.0 * top, zero),
            zero,
            zero,
        ],
        0,
    ).astype(bf16)


def shape_of(radius):
    unit = 1.0 / (grid_step * radius)
    shift = 9.0 / (35.0 * unit)
    return {"reach": 1.0 / unit, "shift": shift, "bias": 3.0 / (35.0 * unit * unit) - shift * shift, "gain": 35.0 / 3.0 * unit**8}


def wendland(dist_sq, shape):
    dist = dist_sq * lax.rsqrt(jnp.maximum(dist_sq, 1.0))
    rest = jnp.maximum(shape["reach"] - dist, 0.0)
    rest_sq = rest * rest
    moved = dist + shape["shift"]
    return (rest_sq * rest_sq) * (rest_sq * (moved * moved + shape["bias"]))


def member(panel_at, block, pattern):
    first = panel_at * SNODE_BLOCKS
    own = (block >= first) & (block < first + SNODE_BLOCKS)
    return jnp.where(own, 1, jnp.where(block < first, 0, pattern[panel_at, block]))


def weight(row, col, pattern):
    value = (row == col).astype(jnp.int32)
    for panel_at in range(PANELS):
        value = value + member(panel_at, row, pattern) * member(panel_at, col, pattern)
    return value.astype(f32)


SCAN = 4
GROUP = 8
UNITS = 32
FIRSTS = 4
CHUNK = 4


def sums_kernel(shape, per, block_map, pattern, points, out, left, lists, weights):
    nblocks = points.shape[0]
    me = lax.axis_index("prow") * lax.axis_size("pcol") + lax.axis_index("pcol")
    own = [block_map[me * per + b] for b in range(per)]
    right = [right_features(points[me * per + b]) for b in range(per)]

    def scan_block(m, counts):
        left[m] = left_features(points[m])
        after = []
        for b in range(per):
            value = weight(own[b], block_map[m], pattern)
            lists[b, counts[b]] = m
            weights[b, counts[b]] = value * shape["gain"]
            after.append(counts[b] + (value > 0).astype(jnp.int32))
        return tuple(after)

    def scan_blocks(step, counts):
        for n in range(SCAN):
            counts = scan_block(step * SCAN + n, counts)
        return counts

    counts = lax.fori_loop(0, nblocks // SCAN, scan_blocks, (0,) * per)
    for b in range(per):
        for g in range(GROUP):
            lists[b, counts[b] + g] = 0
            weights[b, counts[b] + g] = 0.0

    for b in range(per):

        def group(step, total):
            parts = []
            for g in range(GROUP):
                at = step * GROUP + g
                value = wendland(mm(left[lists[b, at]], right[b], TN), shape)
                parts.append(jnp.sum(value.reshape(BLOCK // 8, 8, BLOCK), axis=0) * weights[b, at])
            return total + functools.reduce(lambda x, y: x + y, parts)

        total = lax.fori_loop(0, (counts[b] + GROUP - 1) // GROUP, group, jnp.zeros((8, BLOCK), f32))
        row = jnp.sum(total, axis=0, keepdims=True)
        for d in range(out.shape[0]):
            out[d, b : b + 1, :] = row


def spread_kernel(per, coords, out):
    for b in range(per):
        point = coords[:, b * BLOCK : (b + 1) * BLOCK]
        norm = jnp.sum(point * point, axis=0, keepdims=True)
        point = jnp.concatenate([point, norm], 0)
        for d in range(out.shape[0]):
            out[d, b] = point


def panels_kernel(
    shape, rows_n, cols_n, block_map, pattern, points, totals, out,
    inverse, table, place, units, firsts, seconds, panel, high, low, left, right_lead, right_cols, scale_rows, scale_lead, scale_cols,
    diagonal, x_high, x_low, x_full, stage, sems, *work,
):
    nblocks = points.shape[0]
    row_count = nblocks // rows_n
    col_count = nblocks // cols_n
    prow_at = lax.axis_index("prow")
    pcol_at = lax.axis_index("pcol")
    col_base = row_count
    next_base = row_count + col_count
    lead_base = next_base + SNODE_BLOCKS
    slots = lead_base + SNODE_BLOCKS
    lead_rows = LEAD // rows_n

    def invert(m, carry):
        inverse[block_map[m]] = m
        return carry

    lax.fori_loop(0, nblocks, invert, 0)

    def block_rows(slot):
        return pl.ds(pl.multiple_of(slot * BLOCK, BLOCK), BLOCK)

    def pair_rows(slot):
        return pl.ds(pl.multiple_of(slot * BLOCK, 2 * BLOCK), 2 * BLOCK)

    def chunk_rows(slot):
        return pl.ds(pl.multiple_of(slot * BLOCK, CHUNK * BLOCK), CHUNK * BLOCK)

    def scale_of(m):
        return scale_gain * lax.rsqrt(1.0 + totals[pl.ds(m, 1), :])

    def prepare(slot):
        m = inverse[table[slot]]
        left[slot] = left_features(points[m])
        scale_rows[slot] = jnp.broadcast_to(scale_of(m), (BLOCK, BLOCK)).T

    def prepare_lead(j):
        m = inverse[j]
        half, at = divmod(j, SNODE_BLOCKS)
        right_lead[j] = right_features(points[m])
        scale_lead[half, at : at + 1, :] = scale_of(m)

    def prepare_col(k):
        m = inverse[table[col_base + k]]
        right_cols[k // 2, :, k % 2 * BLOCK : (k % 2 + 1) * BLOCK] = right_features(points[m])
        scale_cols[k : k + 1, :] = scale_of(m)

    def coupled(slot, half, j):
        value = wendland(mm(left[slot], right_lead[half * SNODE_BLOCKS + j], TN), shape)
        scale = scale_lead[half, j : j + 1, :] * (weight(table[slot], half * SNODE_BLOCKS + j, pattern) * shape["gain"])
        return value * scale_rows[slot] * scale

    def couple(at, j):
        unit = units[at]
        slot = unit // 2
        half = unit % 2
        lanes = pl.ds(pl.multiple_of(half * WIDTH + j * BLOCK, BLOCK), BLOCK)
        panel[block_rows(slot), lanes] = coupled(slot, half, j)

    for j in range(SNODE_BLOCKS):
        table[next_base + j] = SNODE_BLOCKS + j
        table[lead_base + j] = j
    for j in range(SNODE_BLOCKS):
        prepare(lead_base + j)
        prepare_lead(j)
    for i in range(SNODE_BLOCKS):
        for j in range(SNODE_BLOCKS):
            value = coupled(lead_base + i, 0, j)
            diagonal[i * BLOCK : (i + 1) * BLOCK, j * BLOCK : (j + 1) * BLOCK] = value + eye(BLOCK) if i == j else value

    def sort(base, blocks):
        kinds = []
        first = second = jnp.int32(0)
        for g, at in blocks:
            in_first = member(0, g, pattern) > 0
            in_second = member(1, g, pattern) > 0
            dead = g < LEAD
            kind = jnp.where(dead, 2, jnp.where(in_first, 0, jnp.where(in_second, 1, 2)))
            kinds.append(kind)
            first = first + (kind == 0).astype(jnp.int32)
            second = second + (kind == 1).astype(jnp.int32)
        spots = [base, base + first, base + first + second]
        for (g, at), kind in zip(blocks, kinds):
            spot = jnp.where(kind == 0, spots[0], jnp.where(kind == 1, spots[1], spots[2]))
            table[spot] = g
            place[spot] = at
            for n in range(3):
                spots[n] = spots[n] + (kind == n).astype(jnp.int32)
        return first, first + second

    real_rows = row_count - lead_rows
    for i in range(lead_rows):
        table[real_rows + i] = i * rows_n + prow_at
        place[real_rows + i] = i
    rows_first, rows_both = sort(0, [(i * rows_n + prow_at, i) for i in range(lead_rows, row_count)])
    cols_first, cols_both = sort(col_base, [(k * cols_n + pcol_at, k) for k in range(col_count)])
    def whole(n):
        return (n + CHUNK - 1) // CHUNK * CHUNK

    count = jnp.int32(0)
    for base, size, ends in ((next_base, SNODE_BLOCKS, (SNODE_BLOCKS,) * PANELS), (0, row_count, (rows_first, rows_both)), (col_base, col_count, (cols_first, cols_both))):
        for at in range(size):
            for half in range(PANELS):
                units[count] = 2 * (base + at) + half
                used = jnp.int32(at < ends[half]) if base or at < real_rows else 1
                count = count + used
    for n in range(UNITS):
        units[count + n] = 2 * lead_base + 1

    def list_chunks(rows, cols, out):
        count = jnp.int32(0)
        for base, size, end in ((0, row_count, rows), (col_base, col_count, cols)):
            for c in range(0, size, CHUNK):
                out[count] = base + c
                count = count + (1 if c == row_count - CHUNK and not base else (c < end).astype(jnp.int32))
        return count

    first_count = list_chunks(rows_first, cols_first, firsts)
    second_count = list_chunks(rows_both, cols_both, seconds)
    for n in range(FIRSTS):
        firsts[first_count + n] = lead_base

    def run(parts, count):
        for n in range(count):
            for part in parts[len(parts) * n // count : len(parts) * (n + 1) // count]:
                part()
            yield

    parts = [functools.partial(prepare_lead, j) for j in range(SNODE_BLOCKS, LEAD)]
    parts += [functools.partial(prepare, slot) for slot in range(lead_base)]
    parts += [functools.partial(prepare_col, k) for k in range(col_count)]

    def couple_beside(step, part):
        n = 2 * step + part
        for unit in range(2):
            for j in range(SNODE_BLOCKS):
                couple(2 * n + unit, j)

    factor_diagonal(diagonal, x_full, work, run(parts, 20), 2, couple_beside)
    x_high[...], x_low[...] = split(x_full[...])

    def couple_more(step, carry):
        for n in range(4):
            for j in range(SNODE_BLOCKS):
                couple(UNITS + 4 * step + n, j)
        return carry

    lax.fori_loop(0, (jnp.maximum(count - UNITS, 0) + 3) // 4, couple_more, 0)
    for base, stop, ends in ((0, real_rows, (rows_first, rows_both)), (col_base, col_count, (cols_first, cols_both))):
        for half, end in enumerate(ends):

            def clear(slot, carry, half=half):
                panel[block_rows(slot), half * WIDTH : (half + 1) * WIDTH] = jnp.zeros((BLOCK, WIDTH), f32)
                return carry

            lax.fori_loop(base + end, base + stop, clear, 0)
    for i in range(lead_rows):
        at = slice((real_rows + i) * BLOCK, (real_rows + i + 1) * BLOCK)
        lanes = pl.ds(pl.multiple_of((i * rows_n + prow_at) * BLOCK, BLOCK), BLOCK)
        panel[at, lanes] = panel[at, lanes] + eye(BLOCK)

    middle = WIDTH // 2

    def solve(at, first):
        a_high, a_low = split(panel[at, first : first + WIDTH])
        for begin, end in ((0, middle), (middle, WIDTH)):
            part = mm3(a_high[:, :end], a_low[:, :end], x_high[begin:end, :end], x_low[begin:end, :end], NT)
            lanes = slice(first + begin, first + end)
            panel[at, lanes] = part
            high[at, lanes], low[at, lanes] = split(part)

    next_rows = slice(next_base * BLOCK, lead_base * BLOCK)
    solve(next_rows, 0)

    def subtract(at, out_ref, out_at):
        for lanes in (slice(0, middle), slice(middle, WIDTH)):
            rows = slice(next_base * BLOCK + lanes.start, next_base * BLOCK + lanes.stop)
            done = mm3(high[at, :WIDTH], low[at, :WIDTH], high[rows, :WIDTH], low[rows, :WIDTH], NT)
            from_at = slice(WIDTH + lanes.start, WIDTH + lanes.stop)
            if out_ref is panel:
                panel[at, from_at] = panel[at, from_at] - done
            else:
                out_ref[out_at, lanes] = panel[at, from_at] - done

    subtract(next_rows, diagonal, slice(0, WIDTH))
    for j in range(SNODE_BLOCKS):
        at = slice(j * BLOCK, (j + 1) * BLOCK)
        diagonal[at, at] = diagonal[at, at] + eye(BLOCK)

    def first_solve(n):
        solve(chunk_rows(firsts[n]), 0)

    def first_subtract(n):
        subtract(chunk_rows(firsts[n]), panel, None)

    def first_beside(step, part):
        if part == 0:
            first_solve(step)
        if part == 2:
            first_subtract(step)

    factor_diagonal(diagonal, x_full, work, iter(()), 4, first_beside)

    def first_more(n, carry):
        first_solve(n)
        first_subtract(n)
        return carry

    lax.fori_loop(FIRSTS, first_count, first_more, 0)
    x_high[...], x_low[...] = split(x_full[...])
    def second(n, carry):
        solve(chunk_rows(seconds[n]), WIDTH)
        return carry

    lax.fori_loop(0, second_count, second, 0)
    for i in range(lead_rows):
        if i * rows_n < SNODE_BLOCKS:

            @pl.when(i * rows_n + prow_at < SNODE_BLOCKS)
            def _(i=i):
                panel[(real_rows + i) * BLOCK : (real_rows + i + 1) * BLOCK, WIDTH:] = jnp.zeros((BLOCK, WIDTH), f32)

    per_slot = BLOCK * col_count
    row_live = whole(rows_both) // CHUNK
    row_two = whole(rows_first) // CHUNK
    col_live = (cols_both + 1) // 2
    col_two = (cols_first + 1) // 2

    def copies_out(step, half):
        made = []
        for q in range(CHUNK):
            at = pl.multiple_of(place[CHUNK * step + q] * per_slot, per_slot)
            made.append(
                pltpu.make_async_copy(stage.at[half, pl.ds(q * per_slot, per_slot), :], out.at[pl.ds(at, per_slot), :], sems.at[half, q])
            )
        return made

    steps = row_count // CHUNK

    def trail(step, carry):
        half = step % 2

        @pl.when(step >= 2)
        def _():
            for copy in copies_out(step - 2, half):
                copy.wait()

        def spots(q, k):
            return pl.ds(q * per_slot + k, BLOCK, stride=col_count)

        def tiles(c, carry):
            live = (step < row_live) & (c < col_live)
            two = (step < row_two) & (c < col_two)
            row_at = chunk_rows(CHUNK * step)
            col_at = pair_rows(col_base + 2 * c)

            def body(first):
                tiles = []
                for q in range(CHUNK):
                    slot = CHUNK * step + q
                    value = wendland(mm(left[slot], right_cols[c], TN), shape)
                    for e in range(2):
                        spot = col_base + 2 * c + e
                        factor = scale_cols[pl.ds(2 * c + e, 1), :] * (weight(table[slot], table[spot], pattern) * shape["gain"])
                        tiles.append(value[:, e * BLOCK : (e + 1) * BLOCK] * scale_rows[slot] * factor)
                update = mm3(high[row_at, first:], low[row_at, first:], high[col_at, first:], low[col_at, first:], NT)
                for q in range(CHUNK):
                    for e in range(2):
                        spot = col_base + 2 * c + e
                        tile = tiles[2 * q + e] - update[q * BLOCK : (q + 1) * BLOCK, e * BLOCK : (e + 1) * BLOCK]
                        stage[half, spots(q, place[spot]), :] = tile

            @pl.when(live & two)
            def _():
                body(0)

            @pl.when(live & jnp.logical_not(two))
            def _():
                body(WIDTH)

            @pl.when(jnp.logical_not(live))
            def _():
                for q in range(CHUNK):
                    for e in range(2):
                        stage[half, spots(q, place[col_base + 2 * c + e]), :] = jnp.zeros((BLOCK, BLOCK), f32)

            return carry

        lax.fori_loop(0, col_count // 2, tiles, 0)

        @pl.when(step == steps - 1)
        def _():
            for q in range(CHUNK - lead_rows, CHUNK):
                for k in range(col_count):
                    stage[half, spots(q, k), :] = jnp.zeros((BLOCK, BLOCK), f32)

        for q in range(CHUNK):
            slot = CHUNK * step + q
            g = table[slot]
            k_same = g // cols_n
            here = (k_same * cols_n + pcol_at == g) & (g >= LEAD)
            same = spots(q, k_same)

            @pl.when(here & (slot >= rows_both))
            def _(slot=slot, g=g, same=same):
                m = inverse[g]
                value = wendland(mm(left[slot], right_features(points[m]), TN), shape)
                factor = scale_gain * lax.rsqrt(1.0 + totals[pl.ds(m, 1), :]) * (weight(g, g, pattern) * shape["gain"])
                stage[half, same, :] = value * scale_rows[slot] * factor

            @pl.when(here)
            def _(same=same):
                stage[half, same, :] = stage[half, same, :] + eye(BLOCK)

            for k in range(col_count):
                if k * cols_n < LEAD:
                    j = k * cols_n + pcol_at

                    filled = (slot < jnp.where(j < SNODE_BLOCKS, rows_first, rows_both)) | (slot >= real_rows)

                    @pl.when((j < LEAD) & filled)
                    def _(k=k, j=j, q=q, slot=slot):
                        where = pl.ds(pl.multiple_of(j * BLOCK, BLOCK), BLOCK)
                        stage[half, spots(q, k), :] = panel[block_rows(slot), where]

                    @pl.when((j < LEAD) & jnp.logical_not(filled))
                    def _(k=k, q=q):
                        stage[half, spots(q, k), :] = jnp.zeros((BLOCK, BLOCK), f32)

        for copy in copies_out(step, half):
            copy.start()
        return carry

    lax.fori_loop(0, steps, trail, 0)
    for step in range(max(steps - 2, 0), steps):
        for copy in copies_out(step, step % 2):
            copy.wait()


def local(coords, block_map, pattern):
    rows_n = lax.axis_size("prow")
    cols_n = lax.axis_size("pcol")
    devices = rows_n * cols_n
    nblocks = block_map.shape[0]
    per = nblocks // devices
    row_count = nblocks // rows_n
    col_count = nblocks // cols_n
    radius = (spread_factor / (nblocks * BLOCK)) ** (1.0 / 3.0)
    slots = row_count + col_count + LEAD
    rows_kept = (slots - SNODE_BLOCKS + CHUNK) * BLOCK
    axes = ("prow", "pcol")
    smem = pl.BlockSpec(memory_space=pltpu.SMEM)
    vmem = pl.BlockSpec(memory_space=pltpu.VMEM)
    params = pltpu.CompilerParams(vmem_limit_bytes=VMEM_BYTES)
    shape = shape_of(radius)
    mine = pl.pallas_call(
        functools.partial(spread_kernel, per),
        out_shape=jax.ShapeDtypeStruct((devices, per, 4, BLOCK), jnp.int32),
        in_specs=[vmem],
        out_specs=vmem,
        name="spread",
    )(coords)
    points = lax.all_to_all(mine, axes, 0, 0, tiled=True).reshape(nblocks, 4, BLOCK)
    sums = pl.pallas_call(
        functools.partial(sums_kernel, shape, per),
        out_shape=jax.ShapeDtypeStruct((devices, per, BLOCK), f32),
        in_specs=[smem, smem, vmem],
        out_specs=vmem,
        scratch_shapes=[
            pltpu.VMEM((nblocks, FEATURES, BLOCK), bf16),
            pltpu.SMEM((per, nblocks + GROUP), jnp.int32),
            pltpu.SMEM((per, nblocks + GROUP), f32),
        ],
        compiler_params=params,
        name="sums",
    )(block_map, pattern, points)
    totals = lax.all_to_all(sums, axes, 0, 0, tiled=True).reshape(nblocks, BLOCK)
    out = pl.pallas_call(
        functools.partial(panels_kernel, shape, rows_n, cols_n),
        out_shape=jax.ShapeDtypeStruct((row_count * BLOCK * col_count, BLOCK), f32),
        in_specs=[smem, smem, vmem, vmem],
        out_specs=pl.BlockSpec(memory_space=pl.ANY),
        scratch_shapes=[
            pltpu.SMEM((nblocks,), jnp.int32),
            pltpu.SMEM((slots,), jnp.int32),
            pltpu.SMEM((slots,), jnp.int32),
            pltpu.SMEM((2 * slots + UNITS,), jnp.int32),
            pltpu.SMEM((slots + FIRSTS,), jnp.int32),
            pltpu.SMEM((slots,), jnp.int32),
            pltpu.VMEM((rows_kept, PANELS * WIDTH), f32),
            pltpu.VMEM((rows_kept, PANELS * WIDTH), bf16),
            pltpu.VMEM((rows_kept, PANELS * WIDTH), bf16),
            pltpu.VMEM((slots, FEATURES, BLOCK), bf16),
            pltpu.VMEM((LEAD, FEATURES, BLOCK), bf16),
            pltpu.VMEM((col_count // 2, FEATURES, 2 * BLOCK), bf16),
            pltpu.VMEM((slots, BLOCK, BLOCK), f32),
            pltpu.VMEM((PANELS, SNODE_BLOCKS, BLOCK), f32),
            pltpu.VMEM((col_count, BLOCK), f32),
            pltpu.VMEM((WIDTH, WIDTH), f32),
            pltpu.VMEM((WIDTH, WIDTH), bf16),
            pltpu.VMEM((WIDTH, WIDTH), bf16),
            pltpu.VMEM((WIDTH, WIDTH), f32),
            pltpu.VMEM((2, CHUNK * BLOCK * col_count, BLOCK), f32),
            pltpu.SemaphoreType.DMA((2, CHUNK)),
        ]
        + [pltpu.VMEM((BLOCK, 2 * BLOCK), f32)] * 4,
        compiler_params=params,
        name="panels",
    )(block_map, pattern, points, totals)
    return out.reshape(row_count, 1, BLOCK, col_count, 1, BLOCK)


def solution(mesh):
    placed = (P(None, ("prow", "pcol")), P(), P())
    return jax.shard_map(
        local,
        mesh=mesh,
        in_specs=placed,
        out_specs=P(None, "prow", None, None, "pcol", None),
        check_vma=False,
    )
```

```python
import functools

import jax
import jax.numpy as jnp
from jax import lax
from jax.experimental import pallas as pl
from jax.experimental.pallas import tpu as pltpu
from jax.sharding import PartitionSpec as P

BLOCK = 128
SNODE_BLOCKS = 4
PANELS = 2
LEAD = PANELS * SNODE_BLOCKS
WIDTH = SNODE_BLOCKS * BLOCK

spread_factor = 89.0
scale_gain = 8.0
grid_step = 1024.0

LOW, HIGH = 0.98, 66.0

f32 = jnp.float32
bf16 = jnp.bfloat16
NN = (((1,), (0,)), ((), ()))
NT = (((1,), (1,)), ((), ()))
TN = (((0,), (0,)), ((), ()))
FEATURES = 32
VMEM_BYTES = 60 * 1024 * 1024


def mm(a, b, dims):
    return lax.dot_general(a, b, dims, preferred_element_type=f32)


def split(a):
    high = a.astype(bf16)
    low = (a - high.astype(f32)).astype(bf16)
    return high, low


def dot1(a, b, dims=NN):
    return mm(a.astype(bf16), b.astype(bf16), dims)


def mm3(a_high, a_low, b_high, b_low, dims):
    rows = a_high.shape[0]
    both = mm(jnp.concatenate([a_high, a_low], 0), b_high, dims)
    return (both[:rows] + both[rows:]) + mm(a_high, b_low, dims)


def dot3(a, b, dims=NN):
    a_high, a_low = split(a)
    b_high, b_low = split(b)
    return mm3(a_high, a_low, b_high, b_low, dims)


def eye(n):
    return (lax.broadcasted_iota(jnp.int32, (n, n), 0) == lax.broadcasted_iota(jnp.int32, (n, n), 1)).astype(f32)


def newton(blocks, n, beside):
    first = 2 / (LOW + HIGH)
    rho = (HIGH - LOW) / (HIGH + LOW)
    one = eye(n)
    step = 2 / (2 - rho * rho)
    rho = rho * rho / (2 - rho * rho)
    found = [(2 * step * first) * one - (step * first * first) * a for a in blocks]
    for at in range(5):
        dot = dot1 if at < 2 else dot3
        step = 2 / (2 - rho * rho) if at < 4 else 1.0
        rho = rho * rho / (2 - rho * rho)
        rest = [(2 * one) - dot(a, x) for a, x in zip(blocks, found)]
        next(beside, None)
        found = [step * dot(x, e) for x, e in zip(found, rest)]
        next(beside, None)
    return found


def chains(work, count, per_step, beside):
    sub = lax.broadcasted_iota(jnp.int32, (8, BLOCK), 0)
    lane = lax.broadcasted_iota(jnp.int32, (8, BLOCK), 1)
    zero = jnp.zeros((8, BLOCK), f32)

    def strip(step, part):
        n = step * per_step + part
        at = n * 8
        rows = pl.ds(pl.multiple_of(at, 8), 8)
        beside(step, part)
        state = []
        for b in range(count):
            r = work[b][rows, 0:BLOCK]
            y = work[b][rows, BLOCK : 2 * BLOCK]
            turned = pltpu.roll(r, lax.rem(BLOCK - at, BLOCK), 1)
            c = [jnp.broadcast_to(turned[:, k : k + 1], (8, BLOCK)) for k in range(8)]
            state.append([r, y, c])
        for k in range(8):
            for b in range(count):
                r, y, c = state[b]
                inv = lax.rsqrt(c[k][k : k + 1, :])
                column = c[k] * inv
                below = jnp.where(sub > k, column, 0.0)
                r_row = r[k : k + 1] * inv
                y_row = y[k : k + 1] * inv
                r = jnp.where(sub == k, r_row, r - below * r_row)
                y = jnp.where(sub == k, y_row, y - below * y_row)
                for m in range(k + 1, 8):
                    c[m] = c[m] - below * column[m : m + 1, :]
                state[b] = [r, y, c]
        later = lane >= at + 8
        for b in range(count):
            r, y, _ = state[b]
            work[b][rows, 0:BLOCK] = r
            work[b][rows, BLOCK : 2 * BLOCK] = y
            r_high = r.astype(bf16).astype(f32)
            y_high = y.astype(bf16).astype(f32)
            high = jnp.concatenate([r_high, y_high], 1)
            low = jnp.concatenate([r - r_high, y - y_high], 1)
            left_high = jnp.where(later, r_high, 0.0)
            left_low = jnp.where(later, r - r_high, 0.0)
            left = jnp.concatenate([left_high, left_high, left_low, zero], 0).astype(bf16)
            right = jnp.concatenate([high, low, high, jnp.concatenate([zero, zero], 1)], 0).astype(bf16)
            work[b][...] = work[b][...] - mm(left, right, TN)

    def strips(step, carry):
        for n in range(per_step):
            strip(step, n)
        return carry

    lax.fori_loop(0, BLOCK // 8 // per_step, strips, 0)


def factor_diagonal(a_ref, x_ref, work, beside_newton, per_step, beside_strip):
    half = 2 * BLOCK
    rows = lax.broadcasted_iota(jnp.int32, (BLOCK, BLOCK), 0)
    cols = lax.broadcasted_iota(jnp.int32, (BLOCK, BLOCK), 1)
    lower = cols <= rows
    a11 = a_ref[0:half, 0:half]
    a21 = a_ref[half:, 0:half]
    s2 = a_ref[half:, half:] - dot3(dot3(a21, newton([a11], half, beside_newton)[0]), a21, NT)
    corner = [a11[0:BLOCK, 0:BLOCK], s2[0:BLOCK, 0:BLOCK]]
    side = [a11[BLOCK:, 0:BLOCK], s2[BLOCK:, 0:BLOCK]]
    last = [a11[BLOCK:, BLOCK:], s2[BLOCK:, BLOCK:]]
    inverse = newton(corner, BLOCK, beside_newton)
    for i in range(2):
        work[2 * i][:, 0:BLOCK] = corner[i]
        work[2 * i + 1][:, 0:BLOCK] = last[i] - dot3(dot3(side[i], inverse[i]), side[i], NT)
    for b in range(4):
        work[b][:, BLOCK:] = eye(BLOCK)
    for _ in beside_newton:
        pass
    chains(work, 4, per_step, beside_strip)
    for i in range(2):
        at = half * i
        xa = jnp.where(lower, work[2 * i][:, BLOCK:], 0.0)
        xb = jnp.where(lower, work[2 * i + 1][:, BLOCK:], 0.0)
        l21 = dot3(side[i], xa, NT)
        x_ref[at : at + BLOCK, at : at + BLOCK] = xa
        x_ref[at : at + BLOCK, at + BLOCK : at + half] = jnp.zeros((BLOCK, BLOCK), f32)
        x_ref[at + BLOCK : at + half, at : at + BLOCK] = -dot3(xb, dot3(l21, xa))
        x_ref[at + BLOCK : at + half, at + BLOCK : at + half] = xb
    x11 = x_ref[0:half, 0:half]
    x22 = x_ref[half:, half:]
    l21 = dot3(a21, x11, NT)
    x_ref[half:, 0:half] = -dot3(x22, dot3(l21, x11))
    x_ref[0:half, half:] = jnp.zeros((half, half), f32)


def pieces(point):
    low = (point & 255).astype(f32)
    mid = ((point >> 8) & 255).astype(f32)
    top = (point >> 16).astype(f32)
    return low, mid, top


def left_features(point):
    low, mid, top = pieces(point)
    norm = lax.broadcasted_iota(jnp.int32, point.shape, 0) == 3
    one = jnp.ones_like(low)
    zero = jnp.zeros_like(low)
    return jnp.concatenate(
        [low, jnp.where(norm, one, low), mid, jnp.where(norm, one, mid), top, jnp.where(norm, one, zero), zero, zero], 0
    ).astype(bf16)


def right_features(point):
    low, mid, top = pieces(point)
    norm = lax.broadcasted_iota(jnp.int32, point.shape, 0) == 3
    one = jnp.ones_like(low)
    zero = jnp.zeros_like(low)
    return jnp.concatenate(
        [
            jnp.where(norm, one, -2.0 * low),
            jnp.where(norm, low, -512.0 * mid),
            jnp.where(norm, 256.0 * one, -512.0 * low),
            jnp.where(norm, 256.0 * mid, -131072.0 * mid),
            jnp.where(norm, 65536.0 * one, zero),
            jnp.where(norm, 65536.0 * top, zero),
            zero,
            zero,
        ],
        0,
    ).astype(bf16)


def shape_of(radius):
    unit = 1.0 / (grid_step * radius)
    shift = 9.0 / (35.0 * unit)
    return {"reach": 1.0 / unit, "shift": shift, "bias": 3.0 / (35.0 * unit * unit) - shift * shift, "gain": 35.0 / 3.0 * unit**8}


def wendland(dist_sq, shape):
    dist = dist_sq * lax.rsqrt(jnp.maximum(dist_sq, 1.0))
    rest = jnp.maximum(shape["reach"] - dist, 0.0)
    rest_sq = rest * rest
    moved = dist + shape["shift"]
    return (rest_sq * rest_sq) * (rest_sq * (moved * moved + shape["bias"]))


def member(panel_at, block, pattern):
    first = panel_at * SNODE_BLOCKS
    own = (block >= first) & (block < first + SNODE_BLOCKS)
    return jnp.where(own, 1, jnp.where(block < first, 0, pattern[panel_at, block]))


def weight(row, col, pattern):
    value = (row == col).astype(jnp.int32)
    for panel_at in range(PANELS):
        value = value + member(panel_at, row, pattern) * member(panel_at, col, pattern)
    return value.astype(f32)


SCAN = 4
GROUP = 16
UNITS = 32
FIRSTS = 4
CHUNK = 4


def sums_kernel(shape, per, block_map, pattern, points, out, left, lists, weights):
    nblocks = points.shape[0]
    me = lax.axis_index("prow") * lax.axis_size("pcol") + lax.axis_index("pcol")
    own = [block_map[me * per + b] for b in range(per)]
    right = [right_features(points[me * per + b]) for b in range(per)]

    def scan_block(m, counts):
        left[m] = left_features(points[m])
        after = []
        for b in range(per):
            value = weight(own[b], block_map[m], pattern)
            lists[b, counts[b]] = m
            weights[b, counts[b]] = value * shape["gain"]
            after.append(counts[b] + (value > 0).astype(jnp.int32))
        return tuple(after)

    def scan_blocks(step, counts):
        for n in range(SCAN):
            counts = scan_block(step * SCAN + n, counts)
        return counts

    counts = lax.fori_loop(0, nblocks // SCAN, scan_blocks, (0,) * per)
    for b in range(per):
        for g in range(GROUP):
            lists[b, counts[b] + g] = 0
            weights[b, counts[b] + g] = 0.0

    for b in range(per):

        def group(step, total):
            parts = []
            for g in range(GROUP):
                at = step * GROUP + g
                value = wendland(mm(left[lists[b, at]], right[b], TN), shape)
                parts.append(jnp.sum(value.reshape(BLOCK // 8, 8, BLOCK), axis=0) * weights[b, at])
            return total + functools.reduce(lambda x, y: x + y, parts)

        total = lax.fori_loop(0, (counts[b] + GROUP - 1) // GROUP, group, jnp.zeros((8, BLOCK), f32))
        row = jnp.sum(total, axis=0, keepdims=True)
        for d in range(out.shape[0]):
            out[d, b : b + 1, :] = row


def spread_kernel(per, coords, out):
    for b in range(per):
        point = coords[:, b * BLOCK : (b + 1) * BLOCK]
        norm = jnp.sum(point * point, axis=0, keepdims=True)
        point = jnp.concatenate([point, norm], 0)
        for d in range(out.shape[0]):
            out[d, b] = point


def panels_kernel(
    shape, rows_n, cols_n, block_map, pattern, points, totals, out,
    inverse, table, place, units, firsts, seconds, panel, high, low, left, right_lead, right_cols, scale_rows, scale_lead, scale_cols,
    diagonal, x_high, x_low, x_full, stage, sems, *work,
):
    nblocks = points.shape[0]
    row_count = nblocks // rows_n
    col_count = nblocks // cols_n
    prow_at = lax.axis_index("prow")
    pcol_at = lax.axis_index("pcol")
    col_base = row_count
    next_base = row_count + col_count
    lead_base = next_base + SNODE_BLOCKS
    slots = lead_base + SNODE_BLOCKS
    lead_rows = LEAD // rows_n

    def invert(m, carry):
        inverse[block_map[m]] = m
        return carry

    lax.fori_loop(0, nblocks, invert, 0)

    def block_rows(slot):
        if isinstance(slot, int):
            return slice(slot * BLOCK, (slot + 1) * BLOCK)
        return pl.ds(pl.multiple_of(slot * BLOCK, BLOCK), BLOCK)

    def pair_rows(slot):
        return pl.ds(pl.multiple_of(slot * BLOCK, 2 * BLOCK), 2 * BLOCK)

    def chunk_rows(slot):
        return pl.ds(pl.multiple_of(slot * BLOCK, CHUNK * BLOCK), CHUNK * BLOCK)

    def scale_of(m):
        return scale_gain * lax.rsqrt(1.0 + totals[pl.ds(m, 1), :])

    def prepare(slot):
        m = inverse[table[slot]]
        left[slot] = left_features(points[m])
        scale_rows[slot] = jnp.broadcast_to(scale_of(m), (BLOCK, BLOCK)).T

    def prepare_lead(j):
        m = inverse[j]
        half, at = divmod(j, SNODE_BLOCKS)
        right_lead[j] = right_features(points[m])
        scale_lead[half, at : at + 1, :] = scale_of(m)

    def prepare_col(k):
        m = inverse[table[col_base + k]]
        right_cols[k // 2, :, k % 2 * BLOCK : (k % 2 + 1) * BLOCK] = right_features(points[m])
        scale_cols[k : k + 1, :] = scale_of(m)

    def coupled(slot, half, j):
        value = wendland(mm(left[slot], right_lead[half * SNODE_BLOCKS + j], TN), shape)
        scale = scale_lead[half, j : j + 1, :] * (weight(table[slot], half * SNODE_BLOCKS + j, pattern) * shape["gain"])
        return value * scale_rows[slot] * scale

    def couple(at, j):
        unit = units[at]
        slot = unit // 2
        half = unit % 2
        lanes = pl.ds(pl.multiple_of(half * WIDTH + j * BLOCK, BLOCK), BLOCK)
        panel[block_rows(slot), lanes] = coupled(slot, half, j)

    for j in range(SNODE_BLOCKS):
        table[next_base + j] = SNODE_BLOCKS + j
        table[lead_base + j] = j
    for j in range(SNODE_BLOCKS):
        prepare(lead_base + j)
        prepare_lead(j)
    for i in range(SNODE_BLOCKS):
        for j in range(SNODE_BLOCKS):
            if i < SNODE_BLOCKS // 2 <= j:
                continue
            value = coupled(lead_base + i, 0, j)
            diagonal[i * BLOCK : (i + 1) * BLOCK, j * BLOCK : (j + 1) * BLOCK] = value + eye(BLOCK) if i == j else value

    def sort(base, blocks):
        kinds = []
        first = second = jnp.int32(0)
        for g, at in blocks:
            in_first = member(0, g, pattern) > 0
            in_second = member(1, g, pattern) > 0
            dead = g < LEAD
            kind = jnp.where(dead, 2, jnp.where(in_first, 0, jnp.where(in_second, 1, 2)))
            kinds.append(kind)
            first = first + (kind == 0).astype(jnp.int32)
            second = second + (kind == 1).astype(jnp.int32)
        spots = [base, base + first, base + first + second]
        for (g, at), kind in zip(blocks, kinds):
            spot = jnp.where(kind == 0, spots[0], jnp.where(kind == 1, spots[1], spots[2]))
            table[spot] = g
            place[spot] = at
            for n in range(3):
                spots[n] = spots[n] + (kind == n).astype(jnp.int32)
        return first, first + second

    real_rows = row_count - lead_rows
    for i in range(lead_rows):
        table[real_rows + i] = i * rows_n + prow_at
        place[real_rows + i] = i
    rows_first, rows_both = sort(0, [(i * rows_n + prow_at, i) for i in range(lead_rows, row_count)])
    cols_first, cols_both = sort(col_base, [(k * cols_n + pcol_at, k) for k in range(col_count)])
    def whole(n):
        return (n + CHUNK - 1) // CHUNK * CHUNK

    count = jnp.int32(0)
    for base, size, ends in ((next_base, SNODE_BLOCKS, (SNODE_BLOCKS,) * PANELS), (0, row_count, (rows_first, rows_both)), (col_base, col_count, (cols_first, cols_both))):
        for at in range(size):
            for half in range(PANELS):
                units[count] = 2 * (base + at) + half
                used = jnp.int32(at < ends[half]) if base or at < real_rows else 1
                count = count + used
    for n in range(UNITS):
        units[count + n] = 2 * lead_base + 1

    def list_slots(rows, cols, out, chunks):
        count = jnp.int32(0)
        for base, size, end in ((0, row_count, rows), (col_base, col_count, cols)):
            for at in range(size):
                out[count] = base + at
                count = count + (1 if not base and at >= real_rows else (at < end).astype(jnp.int32))
        for n in range(CHUNK * chunks):
            out[count + n] = lead_base + n % CHUNK
        return whole(count) // CHUNK

    first_count = list_slots(rows_first, cols_first, firsts, FIRSTS + 1)
    second_count = list_slots(rows_both, cols_both, seconds, 1)

    def run(parts, count):
        for n in range(count):
            for part in parts[len(parts) * n // count : len(parts) * (n + 1) // count]:
                part()
            yield

    parts = [functools.partial(prepare_lead, j) for j in range(SNODE_BLOCKS, LEAD)]
    parts += [functools.partial(prepare, slot) for slot in range(lead_base)]
    parts += [functools.partial(prepare_col, k) for k in range(col_count)]

    def couple_beside(step, part):
        n = 2 * step + part
        for unit in range(2):
            for j in range(SNODE_BLOCKS):
                couple(2 * n + unit, j)

    factor_diagonal(diagonal, x_full, work, run(parts, 20), 2, couple_beside)
    x_high[...], x_low[...] = split(x_full[...])

    def couple_more(step, carry):
        for n in range(4):
            for j in range(SNODE_BLOCKS):
                couple(UNITS + 4 * step + n, j)
        return carry

    lax.fori_loop(0, (jnp.maximum(count - UNITS, 0) + 3) // 4, couple_more, 0)
    rounded = (cols_first + 1) // 2 * 2, (cols_both + 1) // 2 * 2
    for base, ends, stops in (
        (0, (rows_first, rows_both), (jnp.minimum(whole(rows_first), real_rows), jnp.minimum(whole(rows_both), real_rows))),
        (col_base, (cols_first, cols_both), rounded),
    ):
        for half in range(PANELS):

            def clear(slot, carry, half=half):
                for ref in (high, low):
                    ref[block_rows(slot), half * WIDTH : (half + 1) * WIDTH] = jnp.zeros((BLOCK, WIDTH), bf16)
                return carry

            lax.fori_loop(base + ends[half], base + stops[half], clear, 0)
    for i in range(lead_rows):
        at = slice((real_rows + i) * BLOCK, (real_rows + i + 1) * BLOCK)
        lanes = pl.ds(pl.multiple_of((i * rows_n + prow_at) * BLOCK, BLOCK), BLOCK)
        panel[at, lanes] = panel[at, lanes] + eye(BLOCK)

    middle = WIDTH // 2

    def gather(ref, chunk, lanes):
        return jnp.concatenate([ref[block_rows(slot), lanes] for slot in chunk], 0)

    def solve(chunk, first):
        a_high, a_low = split(gather(panel, chunk, slice(first, first + WIDTH)))
        for begin, end in ((0, middle), (middle, WIDTH)):
            part = mm3(a_high[:, :end], a_low[:, :end], x_high[begin:end, :end], x_low[begin:end, :end], NT)
            lanes = slice(first + begin, first + end)
            for q, slot in enumerate(chunk):
                rows = part[q * BLOCK : (q + 1) * BLOCK]
                panel[block_rows(slot), lanes] = rows
                high[block_rows(slot), lanes], low[block_rows(slot), lanes] = split(rows)

    next_chunk = tuple(range(next_base, lead_base))
    solve(next_chunk, 0)

    def subtract(chunk, out_ref):
        a_high, a_low = gather(high, chunk, slice(0, WIDTH)), gather(low, chunk, slice(0, WIDTH))
        for lanes in (slice(0, middle), slice(middle, WIDTH)):
            rows = slice(next_base * BLOCK + lanes.start, next_base * BLOCK + lanes.stop)
            done = mm3(a_high, a_low, high[rows, :WIDTH], low[rows, :WIDTH], NT)
            from_at = slice(WIDTH + lanes.start, WIDTH + lanes.stop)
            for q, slot in enumerate(chunk):
                rest = panel[block_rows(slot), from_at] - done[q * BLOCK : (q + 1) * BLOCK]
                if out_ref is panel:
                    panel[block_rows(slot), from_at] = rest
                else:
                    out_ref[q * BLOCK : (q + 1) * BLOCK, lanes] = rest

    subtract(next_chunk, diagonal)
    for j in range(SNODE_BLOCKS):
        at = slice(j * BLOCK, (j + 1) * BLOCK)
        diagonal[at, at] = diagonal[at, at] + eye(BLOCK)

    def chunk_of(slots_ref, n):
        return tuple(slots_ref[CHUNK * n + q] for q in range(CHUNK))

    def first_solve(n):
        solve(chunk_of(firsts, n), 0)

    def first_subtract(n):
        subtract(chunk_of(firsts, n), panel)

    def first_beside(step, part):
        if part == 0:
            first_solve(step)
        if part == 2:
            first_subtract(step)

    factor_diagonal(diagonal, x_full, work, iter(()), 4, first_beside)

    def first_more(n, carry):
        first_solve(n)
        first_subtract(n)
        return carry

    lax.fori_loop(FIRSTS, first_count, first_more, 0)
    x_high[...], x_low[...] = split(x_full[...])
    def second(n, carry):
        solve(chunk_of(seconds, n), WIDTH)
        return carry

    lax.fori_loop(0, second_count, second, 0)
    for i in range(lead_rows):
        if i * rows_n < SNODE_BLOCKS:

            @pl.when(i * rows_n + prow_at < SNODE_BLOCKS)
            def _(i=i):
                panel[(real_rows + i) * BLOCK : (real_rows + i + 1) * BLOCK, WIDTH:] = jnp.zeros((BLOCK, WIDTH), f32)

    per_slot = BLOCK * col_count
    row_live = whole(rows_both) // CHUNK
    row_two = whole(rows_first) // CHUNK
    col_live = (cols_both + 1) // 2
    col_two = (cols_first + 1) // 2

    def copies_out(step, half):
        made = []
        for q in range(CHUNK):
            at = pl.multiple_of(place[CHUNK * step + q] * per_slot, per_slot)
            made.append(
                pltpu.make_async_copy(stage.at[half, pl.ds(q * per_slot, per_slot), :], out.at[pl.ds(at, per_slot), :], sems.at[half, q])
            )
        return made

    steps = row_count // CHUNK

    def trail(step, carry):
        half = step % 2

        @pl.when(step >= 2)
        def _():
            for copy in copies_out(step - 2, half):
                copy.wait()

        def spots(q, k):
            return pl.ds(q * per_slot + k, BLOCK, stride=col_count)

        def tiles(c, carry):
            live = (step < row_live) & (c < col_live)
            two = (step < row_two) & (c < col_two)
            row_at = chunk_rows(CHUNK * step)
            col_at = pair_rows(col_base + 2 * c)

            def body(first):
                tiles = []
                for q in range(CHUNK):
                    slot = CHUNK * step + q
                    value = wendland(mm(left[slot], right_cols[c], TN), shape)
                    for e in range(2):
                        spot = col_base + 2 * c + e
                        factor = scale_cols[pl.ds(2 * c + e, 1), :] * (weight(table[slot], table[spot], pattern) * shape["gain"])
                        tiles.append(value[:, e * BLOCK : (e + 1) * BLOCK] * scale_rows[slot] * factor)
                update = mm3(high[row_at, first:], low[row_at, first:], high[col_at, first:], low[col_at, first:], NT)
                for q in range(CHUNK):
                    for e in range(2):
                        spot = col_base + 2 * c + e
                        tile = tiles[2 * q + e] - update[q * BLOCK : (q + 1) * BLOCK, e * BLOCK : (e + 1) * BLOCK]
                        stage[half, spots(q, place[spot]), :] = tile

            @pl.when(live & two)
            def _():
                body(0)

            @pl.when(live & jnp.logical_not(two))
            def _():
                body(WIDTH)

            @pl.when(jnp.logical_not(live))
            def _():
                for q in range(CHUNK):
                    for e in range(2):
                        stage[half, spots(q, place[col_base + 2 * c + e]), :] = jnp.zeros((BLOCK, BLOCK), f32)

            return carry

        lax.fori_loop(0, col_count // 2, tiles, 0)

        @pl.when(step == steps - 1)
        def _():
            for q in range(CHUNK - lead_rows, CHUNK):
                for k in range(col_count):
                    stage[half, spots(q, k), :] = jnp.zeros((BLOCK, BLOCK), f32)

        for q in range(CHUNK):
            slot = CHUNK * step + q
            g = table[slot]
            k_same = g // cols_n
            here = (k_same * cols_n + pcol_at == g) & (g >= LEAD)
            same = spots(q, k_same)

            @pl.when(here & (slot >= rows_both))
            def _(slot=slot, g=g, same=same):
                m = inverse[g]
                value = wendland(mm(left[slot], right_features(points[m]), TN), shape)
                factor = scale_gain * lax.rsqrt(1.0 + totals[pl.ds(m, 1), :]) * (weight(g, g, pattern) * shape["gain"])
                stage[half, same, :] = value * scale_rows[slot] * factor

            @pl.when(here)
            def _(same=same):
                stage[half, same, :] = stage[half, same, :] + eye(BLOCK)

            for k in range(col_count):
                if k * cols_n < LEAD:
                    j = k * cols_n + pcol_at

                    filled = (slot < jnp.where(j < SNODE_BLOCKS, rows_first, rows_both)) | (slot >= real_rows)

                    @pl.when((j < LEAD) & filled)
                    def _(k=k, j=j, q=q, slot=slot):
                        where = pl.ds(pl.multiple_of(j * BLOCK, BLOCK), BLOCK)
                        stage[half, spots(q, k), :] = panel[block_rows(slot), where]

                    @pl.when((j < LEAD) & jnp.logical_not(filled))
                    def _(k=k, q=q):
                        stage[half, spots(q, k), :] = jnp.zeros((BLOCK, BLOCK), f32)

        for copy in copies_out(step, half):
            copy.start()
        return carry

    lax.fori_loop(0, steps, trail, 0)
    for step in range(max(steps - 2, 0), steps):
        for copy in copies_out(step, step % 2):
            copy.wait()


def local(coords, block_map, pattern):
    rows_n = lax.axis_size("prow")
    cols_n = lax.axis_size("pcol")
    devices = rows_n * cols_n
    nblocks = block_map.shape[0]
    per = nblocks // devices
    row_count = nblocks // rows_n
    col_count = nblocks // cols_n
    radius = (spread_factor / (nblocks * BLOCK)) ** (1.0 / 3.0)
    slots = row_count + col_count + LEAD
    rows_kept = (slots - SNODE_BLOCKS + CHUNK) * BLOCK
    axes = ("prow", "pcol")
    smem = pl.BlockSpec(memory_space=pltpu.SMEM)
    vmem = pl.BlockSpec(memory_space=pltpu.VMEM)
    params = pltpu.CompilerParams(vmem_limit_bytes=VMEM_BYTES)
    shape = shape_of(radius)
    mine = pl.pallas_call(
        functools.partial(spread_kernel, per),
        out_shape=jax.ShapeDtypeStruct((devices, per, 4, BLOCK), jnp.int32),
        in_specs=[vmem],
        out_specs=vmem,
        name="spread",
    )(coords)
    points = lax.all_to_all(mine, axes, 0, 0, tiled=True).reshape(nblocks, 4, BLOCK)
    sums = pl.pallas_call(
        functools.partial(sums_kernel, shape, per),
        out_shape=jax.ShapeDtypeStruct((devices, per, BLOCK), f32),
        in_specs=[smem, smem, vmem],
        out_specs=vmem,
        scratch_shapes=[
            pltpu.VMEM((nblocks, FEATURES, BLOCK), bf16),
            pltpu.SMEM((per, nblocks + GROUP), jnp.int32),
            pltpu.SMEM((per, nblocks + GROUP), f32),
        ],
        compiler_params=params,
        name="sums",
    )(block_map, pattern, points)
    totals = lax.all_to_all(sums, axes, 0, 0, tiled=True).reshape(nblocks, BLOCK)
    out = pl.pallas_call(
        functools.partial(panels_kernel, shape, rows_n, cols_n),
        out_shape=jax.ShapeDtypeStruct((row_count * BLOCK * col_count, BLOCK), f32),
        in_specs=[smem, smem, vmem, vmem],
        out_specs=pl.BlockSpec(memory_space=pl.ANY),
        scratch_shapes=[
            pltpu.SMEM((nblocks,), jnp.int32),
            pltpu.SMEM((slots,), jnp.int32),
            pltpu.SMEM((slots,), jnp.int32),
            pltpu.SMEM((2 * slots + UNITS,), jnp.int32),
            pltpu.SMEM((slots + CHUNK * (FIRSTS + 1),), jnp.int32),
            pltpu.SMEM((slots + CHUNK,), jnp.int32),
            pltpu.VMEM((rows_kept, PANELS * WIDTH), f32),
            pltpu.VMEM((rows_kept, PANELS * WIDTH), bf16),
            pltpu.VMEM((rows_kept, PANELS * WIDTH), bf16),
            pltpu.VMEM((slots, FEATURES, BLOCK), bf16),
            pltpu.VMEM((LEAD, FEATURES, BLOCK), bf16),
            pltpu.VMEM((col_count // 2, FEATURES, 2 * BLOCK), bf16),
            pltpu.VMEM((slots, BLOCK, BLOCK), f32),
            pltpu.VMEM((PANELS, SNODE_BLOCKS, BLOCK), f32),
            pltpu.VMEM((col_count, BLOCK), f32),
            pltpu.VMEM((WIDTH, WIDTH), f32),
            pltpu.VMEM((WIDTH, WIDTH), bf16),
            pltpu.VMEM((WIDTH, WIDTH), bf16),
            pltpu.VMEM((WIDTH, WIDTH), f32),
            pltpu.VMEM((2, CHUNK * BLOCK * col_count, BLOCK), f32),
            pltpu.SemaphoreType.DMA((2, CHUNK)),
        ]
        + [pltpu.VMEM((BLOCK, 2 * BLOCK), f32)] * 4,
        compiler_params=params,
        name="panels",
    )(block_map, pattern, points, totals)
    return out.reshape(row_count, 1, BLOCK, col_count, 1, BLOCK)


def solution(mesh):
    placed = (P(None, ("prow", "pcol")), P(), P())
    return jax.shard_map(
        local,
        mesh=mesh,
        in_specs=placed,
        out_specs=P(None, "prow", None, None, "pcol", None),
        check_vma=False,
    )
```

```python
import functools

import jax
import jax.numpy as jnp
from jax import lax
from jax.experimental import pallas as pl
from jax.experimental.pallas import tpu as pltpu
from jax.sharding import PartitionSpec as P

BLOCK = 128
SNODE_BLOCKS = 4
PANELS = 2
LEAD = PANELS * SNODE_BLOCKS
WIDTH = SNODE_BLOCKS * BLOCK

spread_factor = 89.0
scale_gain = 8.0
grid_step = 1024.0

LOW, HIGH = 0.98, 66.0

f32 = jnp.float32
bf16 = jnp.bfloat16
NN = (((1,), (0,)), ((), ()))
NT = (((1,), (1,)), ((), ()))
TN = (((0,), (0,)), ((), ()))
FEATURES = 32
VMEM_BYTES = 60 * 1024 * 1024


def mm(a, b, dims):
    return lax.dot_general(a, b, dims, preferred_element_type=f32)


def split(a):
    high = a.astype(bf16)
    low = (a - high.astype(f32)).astype(bf16)
    return high, low


def dot1(a, b, dims=NN):
    return mm(a.astype(bf16), b.astype(bf16), dims)


def mm3(a_high, a_low, b_high, b_low, dims):
    rows = a_high.shape[0]
    both = mm(jnp.concatenate([a_high, a_low], 0), b_high, dims)
    return (both[:rows] + both[rows:]) + mm(a_high, b_low, dims)


def dot3(a, b, dims=NN):
    a_high, a_low = split(a)
    b_high, b_low = split(b)
    return mm3(a_high, a_low, b_high, b_low, dims)


def eye(n):
    return (lax.broadcasted_iota(jnp.int32, (n, n), 0) == lax.broadcasted_iota(jnp.int32, (n, n), 1)).astype(f32)


def newton(blocks, n, beside):
    first = 2 / (LOW + HIGH)
    rho = (HIGH - LOW) / (HIGH + LOW)
    one = eye(n)
    step = 2 / (2 - rho * rho)
    rho = rho * rho / (2 - rho * rho)
    found = [(2 * step * first) * one - (step * first * first) * a for a in blocks]
    for at in range(5):
        dot = dot1 if at < 2 else dot3
        step = 2 / (2 - rho * rho) if at < 4 else 1.0
        rho = rho * rho / (2 - rho * rho)
        rest = [(2 * one) - dot(a, x) for a, x in zip(blocks, found)]
        next(beside, None)
        found = [step * dot(x, e) for x, e in zip(found, rest)]
        next(beside, None)
    return found


def chains(work, count, per_step, beside):
    sub = lax.broadcasted_iota(jnp.int32, (8, BLOCK), 0)
    lane = lax.broadcasted_iota(jnp.int32, (8, BLOCK), 1)
    zero = jnp.zeros((8, BLOCK), f32)

    def strip(step, part):
        n = step * per_step + part
        at = n * 8
        rows = pl.ds(pl.multiple_of(at, 8), 8)
        beside(step, part)
        state = []
        for b in range(count):
            r = work[b][rows, 0:BLOCK]
            y = work[b][rows, BLOCK : 2 * BLOCK]
            turned = pltpu.roll(r, lax.rem(BLOCK - at, BLOCK), 1)
            c = [jnp.broadcast_to(turned[:, k : k + 1], (8, BLOCK)) for k in range(8)]
            state.append([r, y, c])
        for k in range(8):
            for b in range(count):
                r, y, c = state[b]
                inv = lax.rsqrt(c[k][k : k + 1, :])
                column = c[k] * inv
                below = jnp.where(sub > k, column, 0.0)
                r_row = r[k : k + 1] * inv
                y_row = y[k : k + 1] * inv
                r = jnp.where(sub == k, r_row, r - below * r_row)
                y = jnp.where(sub == k, y_row, y - below * y_row)
                for m in range(k + 1, 8):
                    c[m] = c[m] - below * column[m : m + 1, :]
                state[b] = [r, y, c]
        later = lane >= at + 8
        for b in range(count):
            r, y, _ = state[b]
            work[b][rows, 0:BLOCK] = r
            work[b][rows, BLOCK : 2 * BLOCK] = y
            r_high = r.astype(bf16).astype(f32)
            y_high = y.astype(bf16).astype(f32)
            high = jnp.concatenate([r_high, y_high], 1)
            low = jnp.concatenate([r - r_high, y - y_high], 1)
            left_high = jnp.where(later, r_high, 0.0)
            left_low = jnp.where(later, r - r_high, 0.0)
            left = jnp.concatenate([left_high, left_high, left_low, zero], 0).astype(bf16)
            right = jnp.concatenate([high, low, high, jnp.concatenate([zero, zero], 1)], 0).astype(bf16)
            work[b][...] = work[b][...] - mm(left, right, TN)

    def strips(step, carry):
        for n in range(per_step):
            strip(step, n)
        return carry

    lax.fori_loop(0, BLOCK // 8 // per_step, strips, 0)


def factor_diagonal(a_ref, x_ref, work, beside_newton, per_step, beside_strip):
    half = 2 * BLOCK
    rows = lax.broadcasted_iota(jnp.int32, (BLOCK, BLOCK), 0)
    cols = lax.broadcasted_iota(jnp.int32, (BLOCK, BLOCK), 1)
    lower = cols <= rows
    a11 = a_ref[0:half, 0:half]
    a21 = a_ref[half:, 0:half]
    s2 = a_ref[half:, half:] - dot3(dot3(a21, newton([a11], half, beside_newton)[0]), a21, NT)
    corner = [a11[0:BLOCK, 0:BLOCK], s2[0:BLOCK, 0:BLOCK]]
    side = [a11[BLOCK:, 0:BLOCK], s2[BLOCK:, 0:BLOCK]]
    last = [a11[BLOCK:, BLOCK:], s2[BLOCK:, BLOCK:]]
    inverse = newton(corner, BLOCK, beside_newton)
    for i in range(2):
        work[2 * i][:, 0:BLOCK] = corner[i]
        work[2 * i + 1][:, 0:BLOCK] = last[i] - dot3(dot3(side[i], inverse[i]), side[i], NT)
    for b in range(4):
        work[b][:, BLOCK:] = eye(BLOCK)
    for _ in beside_newton:
        pass
    chains(work, 4, per_step, beside_strip)
    for i in range(2):
        at = half * i
        xa = jnp.where(lower, work[2 * i][:, BLOCK:], 0.0)
        xb = jnp.where(lower, work[2 * i + 1][:, BLOCK:], 0.0)
        l21 = dot3(side[i], xa, NT)
        x_ref[at : at + BLOCK, at : at + BLOCK] = xa
        x_ref[at : at + BLOCK, at + BLOCK : at + half] = jnp.zeros((BLOCK, BLOCK), f32)
        x_ref[at + BLOCK : at + half, at : at + BLOCK] = -dot3(xb, dot3(l21, xa))
        x_ref[at + BLOCK : at + half, at + BLOCK : at + half] = xb
    x11 = x_ref[0:half, 0:half]
    x22 = x_ref[half:, half:]
    l21 = dot3(a21, x11, NT)
    x_ref[half:, 0:half] = -dot3(x22, dot3(l21, x11))
    x_ref[0:half, half:] = jnp.zeros((half, half), f32)


def pieces(point):
    low = (point & 255).astype(f32)
    mid = ((point >> 8) & 255).astype(f32)
    top = (point >> 16).astype(f32)
    return low, mid, top


def left_features(point):
    low, mid, top = pieces(point)
    norm = lax.broadcasted_iota(jnp.int32, point.shape, 0) == 3
    one = jnp.ones_like(low)
    zero = jnp.zeros_like(low)
    return jnp.concatenate(
        [low, jnp.where(norm, one, low), mid, jnp.where(norm, one, mid), top, jnp.where(norm, one, zero), zero, zero], 0
    ).astype(bf16)


def right_features(point):
    low, mid, top = pieces(point)
    norm = lax.broadcasted_iota(jnp.int32, point.shape, 0) == 3
    one = jnp.ones_like(low)
    zero = jnp.zeros_like(low)
    return jnp.concatenate(
        [
            jnp.where(norm, one, -2.0 * low),
            jnp.where(norm, low, -512.0 * mid),
            jnp.where(norm, 256.0 * one, -512.0 * low),
            jnp.where(norm, 256.0 * mid, -131072.0 * mid),
            jnp.where(norm, 65536.0 * one, zero),
            jnp.where(norm, 65536.0 * top, zero),
            zero,
            zero,
        ],
        0,
    ).astype(bf16)


def shape_of(radius):
    unit = 1.0 / (grid_step * radius)
    shift = 9.0 / (35.0 * unit)
    return {"reach": 1.0 / unit, "shift": shift, "bias": 3.0 / (35.0 * unit * unit) - shift * shift, "gain": 35.0 / 3.0 * unit**8}


def wendland(dist_sq, shape):
    dist = dist_sq * lax.rsqrt(jnp.maximum(dist_sq, 1.0))
    rest = jnp.maximum(shape["reach"] - dist, 0.0)
    rest_sq = rest * rest
    moved = dist + shape["shift"]
    return (rest_sq * rest_sq) * (rest_sq * (moved * moved + shape["bias"]))


def member(panel_at, block, pattern):
    first = panel_at * SNODE_BLOCKS
    own = (block >= first) & (block < first + SNODE_BLOCKS)
    return jnp.where(own, 1, jnp.where(block < first, 0, pattern[panel_at, block]))


def weight(row, col, pattern):
    value = (row == col).astype(jnp.int32)
    for panel_at in range(PANELS):
        value = value + member(panel_at, row, pattern) * member(panel_at, col, pattern)
    return value.astype(f32)


SCAN = 4
GROUP = 16
UNITS_BESIDE = 3
UNITS = 16 * UNITS_BESIDE
FIRSTS = 4
CHUNK = 4


def sums_kernel(shape, per, block_map, pattern, points, out, left, lists, weights):
    nblocks = points.shape[0]
    me = lax.axis_index("prow") * lax.axis_size("pcol") + lax.axis_index("pcol")
    own = [block_map[me * per + b] for b in range(per)]
    own_members = [[member(n, g, pattern) for n in range(PANELS)] for g in own]
    right = [right_features(points[me * per + b]) for b in range(per)]

    def scan_block(m, counts):
        left[m] = left_features(points[m])
        other = block_map[m]
        members = [member(n, other, pattern) for n in range(PANELS)]
        after = []
        for b in range(per):
            value = (own[b] == other).astype(jnp.int32)
            for n in range(PANELS):
                value = value + own_members[b][n] * members[n]
            lists[b, counts[b]] = m
            weights[b, counts[b]] = value.astype(f32) * shape["gain"]
            after.append(counts[b] + (value > 0).astype(jnp.int32))
        return tuple(after)

    def scan_blocks(step, counts):
        for n in range(SCAN):
            counts = scan_block(step * SCAN + n, counts)
        return counts

    counts = lax.fori_loop(0, nblocks // SCAN, scan_blocks, (0,) * per)
    for b in range(per):
        for g in range(GROUP):
            lists[b, counts[b] + g] = 0
            weights[b, counts[b] + g] = 0.0

    for b in range(per):

        def group(step, total):
            parts = []
            for g in range(GROUP):
                at = step * GROUP + g
                value = wendland(mm(left[lists[b, at]], right[b], TN), shape)
                parts.append(jnp.sum(value.reshape(BLOCK // 8, 8, BLOCK), axis=0) * weights[b, at])
            return total + functools.reduce(lambda x, y: x + y, parts)

        total = lax.fori_loop(0, (counts[b] + GROUP - 1) // GROUP, group, jnp.zeros((8, BLOCK), f32))
        row = jnp.sum(total, axis=0, keepdims=True)
        for d in range(out.shape[0]):
            out[d, b : b + 1, :] = row


def spread_kernel(per, coords, out):
    for b in range(per):
        point = coords[:, b * BLOCK : (b + 1) * BLOCK]
        norm = jnp.sum(point * point, axis=0, keepdims=True)
        point = jnp.concatenate([point, norm], 0)
        for d in range(out.shape[0]):
            out[d, b] = point


def panels_kernel(
    shape, rows_n, cols_n, block_map, pattern, points, totals, out,
    inverse, table, place, units, firsts, seconds, panel, high, low, left, right_lead, right_cols, scale_rows, scale_lead, scale_cols,
    diagonal, x_high, x_low, x_full, stage, sems, *work,
):
    nblocks = points.shape[0]
    row_count = nblocks // rows_n
    col_count = nblocks // cols_n
    prow_at = lax.axis_index("prow")
    pcol_at = lax.axis_index("pcol")
    col_base = row_count
    next_base = row_count + col_count
    lead_base = next_base + SNODE_BLOCKS
    slots = lead_base + SNODE_BLOCKS
    lead_rows = LEAD // rows_n

    def invert(m, carry):
        inverse[block_map[m]] = m
        return carry

    lax.fori_loop(0, nblocks, invert, 0)

    def block_rows(slot):
        if isinstance(slot, int):
            return slice(slot * BLOCK, (slot + 1) * BLOCK)
        return pl.ds(pl.multiple_of(slot * BLOCK, BLOCK), BLOCK)

    def pair_rows(slot):
        return pl.ds(pl.multiple_of(slot * BLOCK, 2 * BLOCK), 2 * BLOCK)

    def chunk_rows(slot):
        return pl.ds(pl.multiple_of(slot * BLOCK, CHUNK * BLOCK), CHUNK * BLOCK)

    def scale_of(m):
        return scale_gain * lax.rsqrt(1.0 + totals[pl.ds(m, 1), :])

    def prepare(slot):
        m = inverse[table[slot]]
        left[slot] = left_features(points[m])
        scale_rows[slot] = jnp.broadcast_to(scale_of(m), (BLOCK, BLOCK)).T

    def prepare_lead(j):
        m = inverse[j]
        half, at = divmod(j, SNODE_BLOCKS)
        right_lead[j] = right_features(points[m])
        scale_lead[half, at : at + 1, :] = scale_of(m)

    def prepare_col(k):
        m = inverse[table[col_base + k]]
        right_cols[k // 2, :, k % 2 * BLOCK : (k % 2 + 1) * BLOCK] = right_features(points[m])
        scale_cols[k : k + 1, :] = scale_of(m)

    def coupled(slot, half, j):
        value = wendland(mm(left[slot], right_lead[half * SNODE_BLOCKS + j], TN), shape)
        scale = scale_lead[half, j : j + 1, :] * (weight(table[slot], half * SNODE_BLOCKS + j, pattern) * shape["gain"])
        return value * scale_rows[slot] * scale

    def couple(at, j):
        unit = units[at]
        slot = unit // 2
        half = unit % 2
        lanes = pl.ds(pl.multiple_of(half * WIDTH + j * BLOCK, BLOCK), BLOCK)
        panel[block_rows(slot), lanes] = coupled(slot, half, j)

    for j in range(SNODE_BLOCKS):
        table[next_base + j] = SNODE_BLOCKS + j
        table[lead_base + j] = j
    for j in range(SNODE_BLOCKS):
        prepare(lead_base + j)
        prepare_lead(j)
    for i in range(SNODE_BLOCKS):
        for j in range(SNODE_BLOCKS):
            if i < SNODE_BLOCKS // 2 <= j:
                continue
            value = coupled(lead_base + i, 0, j)
            diagonal[i * BLOCK : (i + 1) * BLOCK, j * BLOCK : (j + 1) * BLOCK] = value + eye(BLOCK) if i == j else value

    def sort(base, blocks):
        kinds = []
        first = second = jnp.int32(0)
        for g, at in blocks:
            in_first = member(0, g, pattern) > 0
            in_second = member(1, g, pattern) > 0
            dead = g < LEAD
            kind = jnp.where(dead, 2, jnp.where(in_first, 0, jnp.where(in_second, 1, 2)))
            kinds.append(kind)
            first = first + (kind == 0).astype(jnp.int32)
            second = second + (kind == 1).astype(jnp.int32)
        spots = [base, base + first, base + first + second]
        for (g, at), kind in zip(blocks, kinds):
            spot = jnp.where(kind == 0, spots[0], jnp.where(kind == 1, spots[1], spots[2]))
            table[spot] = g
            place[spot] = at
            for n in range(3):
                spots[n] = spots[n] + (kind == n).astype(jnp.int32)
        return first, first + second

    real_rows = row_count - lead_rows
    for i in range(lead_rows):
        table[real_rows + i] = i * rows_n + prow_at
        place[real_rows + i] = i
    rows_first, rows_both = sort(0, [(i * rows_n + prow_at, i) for i in range(lead_rows, row_count)])
    cols_first, cols_both = sort(col_base, [(k * cols_n + pcol_at, k) for k in range(col_count)])
    def whole(n):
        return (n + CHUNK - 1) // CHUNK * CHUNK

    count = jnp.int32(0)
    for base, size, ends in ((next_base, SNODE_BLOCKS, (SNODE_BLOCKS,) * PANELS), (0, row_count, (rows_first, rows_both)), (col_base, col_count, (cols_first, cols_both))):
        for at in range(size):
            for half in range(PANELS):
                units[count] = 2 * (base + at) + half
                used = jnp.int32(at < ends[half]) if base or at < real_rows else 1
                count = count + used
    for n in range(UNITS):
        units[count + n] = 2 * lead_base + 1

    def list_slots(rows, cols, out, chunks):
        count = jnp.int32(0)
        for base, size, end in ((0, row_count, rows), (col_base, col_count, cols)):
            for at in range(size):
                out[count] = base + at
                count = count + (1 if not base and at >= real_rows else (at < end).astype(jnp.int32))
        for n in range(CHUNK * chunks):
            out[count + n] = lead_base + n % CHUNK
        return whole(count) // CHUNK

    first_count = list_slots(rows_first, cols_first, firsts, FIRSTS + 1)
    second_count = list_slots(rows_both, cols_both, seconds, 1)

    def run(parts, count):
        for n in range(count):
            for part in parts[len(parts) * n // count : len(parts) * (n + 1) // count]:
                part()
            yield

    parts = [functools.partial(prepare_lead, j) for j in range(SNODE_BLOCKS, LEAD)]
    parts += [functools.partial(prepare, slot) for slot in range(lead_base)]
    parts += [functools.partial(prepare_col, k) for k in range(col_count)]

    def couple_beside(step, part):
        n = 2 * step + part
        for unit in range(UNITS_BESIDE):
            for j in range(SNODE_BLOCKS):
                couple(UNITS_BESIDE * n + unit, j)

    factor_diagonal(diagonal, x_full, work, run(parts, 20), 2, couple_beside)
    x_high[...], x_low[...] = split(x_full[...])

    def couple_more(step, carry):
        for n in range(4):
            for j in range(SNODE_BLOCKS):
                couple(UNITS + 4 * step + n, j)
        return carry

    lax.fori_loop(0, (jnp.maximum(count - UNITS, 0) + 3) // 4, couple_more, 0)
    rounded = (cols_first + 1) // 2 * 2, (cols_both + 1) // 2 * 2
    for base, ends, stops in (
        (0, (rows_first, rows_both), (jnp.minimum(whole(rows_first), real_rows), jnp.minimum(whole(rows_both), real_rows))),
        (col_base, (cols_first, cols_both), rounded),
    ):
        for half in range(PANELS):

            def clear(slot, carry, half=half):
                for ref in (high, low):
                    ref[block_rows(slot), half * WIDTH : (half + 1) * WIDTH] = jnp.zeros((BLOCK, WIDTH), bf16)
                return carry

            lax.fori_loop(base + ends[half], base + stops[half], clear, 0)
    for i in range(lead_rows):
        at = slice((real_rows + i) * BLOCK, (real_rows + i + 1) * BLOCK)
        lanes = pl.ds(pl.multiple_of((i * rows_n + prow_at) * BLOCK, BLOCK), BLOCK)
        panel[at, lanes] = panel[at, lanes] + eye(BLOCK)

    middle = WIDTH // 2

    def gather(ref, chunk, lanes):
        return jnp.concatenate([ref[block_rows(slot), lanes] for slot in chunk], 0)

    def solve(chunk, first):
        a_high, a_low = split(gather(panel, chunk, slice(first, first + WIDTH)))
        for begin, end in ((0, middle), (middle, WIDTH)):
            part = mm3(a_high[:, :end], a_low[:, :end], x_high[begin:end, :end], x_low[begin:end, :end], NT)
            lanes = slice(first + begin, first + end)
            for q, slot in enumerate(chunk):
                rows = part[q * BLOCK : (q + 1) * BLOCK]
                panel[block_rows(slot), lanes] = rows
                high[block_rows(slot), lanes], low[block_rows(slot), lanes] = split(rows)

    next_chunk = tuple(range(next_base, lead_base))
    solve(next_chunk, 0)

    def subtract(chunk, out_ref):
        a_high, a_low = gather(high, chunk, slice(0, WIDTH)), gather(low, chunk, slice(0, WIDTH))
        for lanes in (slice(0, middle), slice(middle, WIDTH)):
            rows = slice(next_base * BLOCK + lanes.start, next_base * BLOCK + lanes.stop)
            done = mm3(a_high, a_low, high[rows, :WIDTH], low[rows, :WIDTH], NT)
            from_at = slice(WIDTH + lanes.start, WIDTH + lanes.stop)
            for q, slot in enumerate(chunk):
                rest = panel[block_rows(slot), from_at] - done[q * BLOCK : (q + 1) * BLOCK]
                if out_ref is panel:
                    panel[block_rows(slot), from_at] = rest
                else:
                    out_ref[q * BLOCK : (q + 1) * BLOCK, lanes] = rest

    subtract(next_chunk, diagonal)
    for j in range(SNODE_BLOCKS):
        at = slice(j * BLOCK, (j + 1) * BLOCK)
        diagonal[at, at] = diagonal[at, at] + eye(BLOCK)

    def chunk_of(slots_ref, n):
        return tuple(slots_ref[CHUNK * n + q] for q in range(CHUNK))

    def first_solve(n):
        solve(chunk_of(firsts, n), 0)

    def first_subtract(n):
        subtract(chunk_of(firsts, n), panel)

    def first_beside(step, part):
        if part == 0:
            first_solve(step)
        if part == 2:
            first_subtract(step)

    factor_diagonal(diagonal, x_full, work, iter(()), 4, first_beside)

    def first_more(n, carry):
        first_solve(n)
        first_subtract(n)
        return carry

    lax.fori_loop(FIRSTS, first_count, first_more, 0)
    x_high[...], x_low[...] = split(x_full[...])
    def second(n, carry):
        solve(chunk_of(seconds, n), WIDTH)
        return carry

    lax.fori_loop(0, second_count, second, 0)
    for i in range(lead_rows):
        if i * rows_n < SNODE_BLOCKS:

            @pl.when(i * rows_n + prow_at < SNODE_BLOCKS)
            def _(i=i):
                panel[(real_rows + i) * BLOCK : (real_rows + i + 1) * BLOCK, WIDTH:] = jnp.zeros((BLOCK, WIDTH), f32)

    per_slot = BLOCK * col_count
    row_live = whole(rows_both) // CHUNK
    row_two = whole(rows_first) // CHUNK
    col_live = (cols_both + 1) // 2
    col_two = (cols_first + 1) // 2

    def copies_out(step, half):
        made = []
        for q in range(CHUNK):
            at = pl.multiple_of(place[CHUNK * step + q] * per_slot, per_slot)
            made.append(
                pltpu.make_async_copy(stage.at[half, pl.ds(q * per_slot, per_slot), :], out.at[pl.ds(at, per_slot), :], sems.at[half, q])
            )
        return made

    steps = row_count // CHUNK

    def trail(step, carry):
        half = step % 2

        @pl.when(step >= 2)
        def _():
            for copy in copies_out(step - 2, half):
                copy.wait()

        def spots(q, k):
            return pl.ds(q * per_slot + k, BLOCK, stride=col_count)

        def tiles(c, carry):
            live = (step < row_live) & (c < col_live)
            two = (step < row_two) & (c < col_two)
            row_at = chunk_rows(CHUNK * step)
            col_at = pair_rows(col_base + 2 * c)

            def body(first):
                tiles = []
                for q in range(CHUNK):
                    slot = CHUNK * step + q
                    value = wendland(mm(left[slot], right_cols[c], TN), shape)
                    for e in range(2):
                        spot = col_base + 2 * c + e
                        factor = scale_cols[pl.ds(2 * c + e, 1), :] * (weight(table[slot], table[spot], pattern) * shape["gain"])
                        tiles.append(value[:, e * BLOCK : (e + 1) * BLOCK] * scale_rows[slot] * factor)
                update = mm3(high[row_at, first:], low[row_at, first:], high[col_at, first:], low[col_at, first:], NT)
                for q in range(CHUNK):
                    for e in range(2):
                        spot = col_base + 2 * c + e
                        tile = tiles[2 * q + e] - update[q * BLOCK : (q + 1) * BLOCK, e * BLOCK : (e + 1) * BLOCK]
                        stage[half, spots(q, place[spot]), :] = tile

            @pl.when(live & two)
            def _():
                body(0)

            @pl.when(live & jnp.logical_not(two))
            def _():
                body(WIDTH)

            @pl.when(jnp.logical_not(live))
            def _():
                for q in range(CHUNK):
                    for e in range(2):
                        stage[half, spots(q, place[col_base + 2 * c + e]), :] = jnp.zeros((BLOCK, BLOCK), f32)

            return carry

        lax.fori_loop(0, col_count // 2, tiles, 0)

        @pl.when(step == steps - 1)
        def _():
            for q in range(CHUNK - lead_rows, CHUNK):
                for k in range(col_count):
                    stage[half, spots(q, k), :] = jnp.zeros((BLOCK, BLOCK), f32)

        for q in range(CHUNK):
            slot = CHUNK * step + q
            g = table[slot]
            k_same = g // cols_n
            here = (k_same * cols_n + pcol_at == g) & (g >= LEAD)
            same = spots(q, k_same)

            @pl.when(here & (slot >= rows_both))
            def _(slot=slot, g=g, same=same):
                m = inverse[g]
                value = wendland(mm(left[slot], right_features(points[m]), TN), shape)
                factor = scale_gain * lax.rsqrt(1.0 + totals[pl.ds(m, 1), :]) * (weight(g, g, pattern) * shape["gain"])
                stage[half, same, :] = value * scale_rows[slot] * factor

            @pl.when(here)
            def _(same=same):
                stage[half, same, :] = stage[half, same, :] + eye(BLOCK)

            for k in range(col_count):
                if k * cols_n < LEAD:
                    j = k * cols_n + pcol_at

                    filled = (slot < jnp.where(j < SNODE_BLOCKS, rows_first, rows_both)) | (slot >= real_rows)

                    @pl.when((j < LEAD) & filled)
                    def _(k=k, j=j, q=q, slot=slot):
                        where = pl.ds(pl.multiple_of(j * BLOCK, BLOCK), BLOCK)
                        stage[half, spots(q, k), :] = panel[block_rows(slot), where]

                    @pl.when((j < LEAD) & jnp.logical_not(filled))
                    def _(k=k, q=q):
                        stage[half, spots(q, k), :] = jnp.zeros((BLOCK, BLOCK), f32)

        for copy in copies_out(step, half):
            copy.start()
        return carry

    lax.fori_loop(0, steps, trail, 0)
    for step in range(max(steps - 2, 0), steps):
        for copy in copies_out(step, step % 2):
            copy.wait()


def local(coords, block_map, pattern):
    rows_n = lax.axis_size("prow")
    cols_n = lax.axis_size("pcol")
    devices = rows_n * cols_n
    nblocks = block_map.shape[0]
    per = nblocks // devices
    row_count = nblocks // rows_n
    col_count = nblocks // cols_n
    radius = (spread_factor / (nblocks * BLOCK)) ** (1.0 / 3.0)
    slots = row_count + col_count + LEAD
    rows_kept = (slots - SNODE_BLOCKS + CHUNK) * BLOCK
    axes = ("prow", "pcol")
    smem = pl.BlockSpec(memory_space=pltpu.SMEM)
    vmem = pl.BlockSpec(memory_space=pltpu.VMEM)
    params = pltpu.CompilerParams(vmem_limit_bytes=VMEM_BYTES)
    shape = shape_of(radius)
    mine = pl.pallas_call(
        functools.partial(spread_kernel, per),
        out_shape=jax.ShapeDtypeStruct((devices, per, 4, BLOCK), jnp.int32),
        in_specs=[vmem],
        out_specs=vmem,
        name="spread",
    )(coords)
    points = lax.all_to_all(mine, axes, 0, 0, tiled=True).reshape(nblocks, 4, BLOCK)
    sums = pl.pallas_call(
        functools.partial(sums_kernel, shape, per),
        out_shape=jax.ShapeDtypeStruct((devices, per, BLOCK), f32),
        in_specs=[smem, smem, vmem],
        out_specs=vmem,
        scratch_shapes=[
            pltpu.VMEM((nblocks, FEATURES, BLOCK), bf16),
            pltpu.SMEM((per, nblocks + GROUP), jnp.int32),
            pltpu.SMEM((per, nblocks + GROUP), f32),
        ],
        compiler_params=params,
        name="sums",
    )(block_map, pattern, points)
    totals = lax.all_to_all(sums, axes, 0, 0, tiled=True).reshape(nblocks, BLOCK)
    out = pl.pallas_call(
        functools.partial(panels_kernel, shape, rows_n, cols_n),
        out_shape=jax.ShapeDtypeStruct((row_count * BLOCK * col_count, BLOCK), f32),
        in_specs=[smem, smem, vmem, vmem],
        out_specs=pl.BlockSpec(memory_space=pl.ANY),
        scratch_shapes=[
            pltpu.SMEM((nblocks,), jnp.int32),
            pltpu.SMEM((slots,), jnp.int32),
            pltpu.SMEM((slots,), jnp.int32),
            pltpu.SMEM((2 * slots + UNITS,), jnp.int32),
            pltpu.SMEM((slots + CHUNK * (FIRSTS + 1),), jnp.int32),
            pltpu.SMEM((slots + CHUNK,), jnp.int32),
            pltpu.VMEM((rows_kept, PANELS * WIDTH), f32),
            pltpu.VMEM((rows_kept, PANELS * WIDTH), bf16),
            pltpu.VMEM((rows_kept, PANELS * WIDTH), bf16),
            pltpu.VMEM((slots, FEATURES, BLOCK), bf16),
            pltpu.VMEM((LEAD, FEATURES, BLOCK), bf16),
            pltpu.VMEM((col_count // 2, FEATURES, 2 * BLOCK), bf16),
            pltpu.VMEM((slots, BLOCK, BLOCK), f32),
            pltpu.VMEM((PANELS, SNODE_BLOCKS, BLOCK), f32),
            pltpu.VMEM((col_count, BLOCK), f32),
            pltpu.VMEM((WIDTH, WIDTH), f32),
            pltpu.VMEM((WIDTH, WIDTH), bf16),
            pltpu.VMEM((WIDTH, WIDTH), bf16),
            pltpu.VMEM((WIDTH, WIDTH), f32),
            pltpu.VMEM((2, CHUNK * BLOCK * col_count, BLOCK), f32),
            pltpu.SemaphoreType.DMA((2, CHUNK)),
        ]
        + [pltpu.VMEM((BLOCK, 2 * BLOCK), f32)] * 4,
        compiler_params=params,
        name="panels",
    )(block_map, pattern, points, totals)
    return out.reshape(row_count, 1, BLOCK, col_count, 1, BLOCK)


def solution(mesh):
    placed = (P(None, ("prow", "pcol")), P(), P())
    return jax.shard_map(
        local,
        mesh=mesh,
        in_specs=placed,
        out_specs=P(None, "prow", None, None, "pcol", None),
        check_vma=False,
    )
```

```python
import functools

import jax
import jax.numpy as jnp
from jax import lax
from jax.experimental import pallas as pl
from jax.experimental.pallas import tpu as pltpu
from jax.sharding import PartitionSpec as P

BLOCK = 128
SNODE_BLOCKS = 4
PANELS = 2
LEAD = PANELS * SNODE_BLOCKS
WIDTH = SNODE_BLOCKS * BLOCK

spread_factor = 89.0
scale_gain = 8.0
grid_step = 1024.0

LOW, HIGH = 0.98, 66.0

f32 = jnp.float32
bf16 = jnp.bfloat16
NN = (((1,), (0,)), ((), ()))
NT = (((1,), (1,)), ((), ()))
TN = (((0,), (0,)), ((), ()))
FEATURES = 32
VMEM_BYTES = 60 * 1024 * 1024


def mm(a, b, dims):
    return lax.dot_general(a, b, dims, preferred_element_type=f32)


def split(a):
    high = a.astype(bf16)
    low = (a - high.astype(f32)).astype(bf16)
    return high, low


def dot1(a, b, dims=NN):
    return mm(a.astype(bf16), b.astype(bf16), dims)


def mm3(a_high, a_low, b_high, b_low, dims):
    rows = a_high.shape[0]
    both = mm(jnp.concatenate([a_high, a_low], 0), b_high, dims)
    return (both[:rows] + both[rows:]) + mm(a_high, b_low, dims)


def dot3(a, b, dims=NN):
    a_high, a_low = split(a)
    b_high, b_low = split(b)
    return mm3(a_high, a_low, b_high, b_low, dims)


def eye(n):
    return (lax.broadcasted_iota(jnp.int32, (n, n), 0) == lax.broadcasted_iota(jnp.int32, (n, n), 1)).astype(f32)


def newton(blocks, n, beside):
    first = 2 / (LOW + HIGH)
    rho = (HIGH - LOW) / (HIGH + LOW)
    one = eye(n)
    step = 2 / (2 - rho * rho)
    rho = rho * rho / (2 - rho * rho)
    found = [(2 * step * first) * one - (step * first * first) * a for a in blocks]
    for at in range(5):
        dot = dot1 if at < 2 else dot3
        step = 2 / (2 - rho * rho) if at < 4 else 1.0
        rho = rho * rho / (2 - rho * rho)
        rest = [(2 * one) - dot(a, x) for a, x in zip(blocks, found)]
        next(beside, None)
        found = [step * dot(x, e) for x, e in zip(found, rest)]
        next(beside, None)
    return found


def chains(work, count, per_step, beside):
    sub = lax.broadcasted_iota(jnp.int32, (8, BLOCK), 0)
    lane = lax.broadcasted_iota(jnp.int32, (8, BLOCK), 1)
    zero = jnp.zeros((8, BLOCK), f32)

    def strip(step, part):
        n = step * per_step + part
        at = n * 8
        rows = pl.ds(pl.multiple_of(at, 8), 8)
        beside(step, part)
        state = []
        for b in range(count):
            r = work[b][rows, 0:BLOCK]
            y = work[b][rows, BLOCK : 2 * BLOCK]
            turned = pltpu.roll(r, lax.rem(BLOCK - at, BLOCK), 1)
            c = [jnp.broadcast_to(turned[:, k : k + 1], (8, BLOCK)) for k in range(8)]
            state.append([r, y, c])
        for k in range(8):
            for b in range(count):
                r, y, c = state[b]
                inv = lax.rsqrt(c[k][k : k + 1, :])
                column = c[k] * inv
                below = jnp.where(sub > k, column, 0.0)
                r_row = r[k : k + 1] * inv
                y_row = y[k : k + 1] * inv
                r = jnp.where(sub == k, r_row, r - below * r_row)
                y = jnp.where(sub == k, y_row, y - below * y_row)
                for m in range(k + 1, 8):
                    c[m] = c[m] - below * column[m : m + 1, :]
                state[b] = [r, y, c]
        later = lane >= at + 8
        for b in range(count):
            r, y, _ = state[b]
            work[b][rows, 0:BLOCK] = r
            work[b][rows, BLOCK : 2 * BLOCK] = y
            r_high = r.astype(bf16).astype(f32)
            y_high = y.astype(bf16).astype(f32)
            high = jnp.concatenate([r_high, y_high], 1)
            low = jnp.concatenate([r - r_high, y - y_high], 1)
            left_high = jnp.where(later, r_high, 0.0)
            left_low = jnp.where(later, r - r_high, 0.0)
            left = jnp.concatenate([left_high, left_high, left_low, zero], 0).astype(bf16)
            right = jnp.concatenate([high, low, high, jnp.concatenate([zero, zero], 1)], 0).astype(bf16)
            work[b][...] = work[b][...] - mm(left, right, TN)

    def strips(step, carry):
        for n in range(per_step):
            strip(step, n)
        return carry

    lax.fori_loop(0, BLOCK // 8 // per_step, strips, 0)


def factor_diagonal(a_ref, x_ref, work, beside_newton, per_step, beside_strip):
    half = 2 * BLOCK
    rows = lax.broadcasted_iota(jnp.int32, (BLOCK, BLOCK), 0)
    cols = lax.broadcasted_iota(jnp.int32, (BLOCK, BLOCK), 1)
    lower = cols <= rows
    a11 = a_ref[0:half, 0:half]
    a21 = a_ref[half:, 0:half]
    s2 = a_ref[half:, half:] - dot3(dot3(a21, newton([a11], half, beside_newton)[0]), a21, NT)
    corner = [a11[0:BLOCK, 0:BLOCK], s2[0:BLOCK, 0:BLOCK]]
    side = [a11[BLOCK:, 0:BLOCK], s2[BLOCK:, 0:BLOCK]]
    last = [a11[BLOCK:, BLOCK:], s2[BLOCK:, BLOCK:]]
    inverse = newton(corner, BLOCK, beside_newton)
    for i in range(2):
        work[2 * i][:, 0:BLOCK] = corner[i]
        work[2 * i + 1][:, 0:BLOCK] = last[i] - dot3(dot3(side[i], inverse[i]), side[i], NT)
    for b in range(4):
        work[b][:, BLOCK:] = eye(BLOCK)
    for _ in beside_newton:
        pass
    chains(work, 4, per_step, beside_strip)
    for i in range(2):
        at = half * i
        xa = jnp.where(lower, work[2 * i][:, BLOCK:], 0.0)
        xb = jnp.where(lower, work[2 * i + 1][:, BLOCK:], 0.0)
        l21 = dot3(side[i], xa, NT)
        x_ref[at : at + BLOCK, at : at + BLOCK] = xa
        x_ref[at : at + BLOCK, at + BLOCK : at + half] = jnp.zeros((BLOCK, BLOCK), f32)
        x_ref[at + BLOCK : at + half, at : at + BLOCK] = -dot3(xb, dot3(l21, xa))
        x_ref[at + BLOCK : at + half, at + BLOCK : at + half] = xb
    x11 = x_ref[0:half, 0:half]
    x22 = x_ref[half:, half:]
    l21 = dot3(a21, x11, NT)
    x_ref[half:, 0:half] = -dot3(x22, dot3(l21, x11))
    x_ref[0:half, half:] = jnp.zeros((half, half), f32)


def pieces(point):
    low = (point & 255).astype(f32)
    mid = ((point >> 8) & 255).astype(f32)
    top = (point >> 16).astype(f32)
    return low, mid, top


def left_features(point):
    low, mid, top = pieces(point)
    norm = lax.broadcasted_iota(jnp.int32, point.shape, 0) == 3
    one = jnp.ones_like(low)
    zero = jnp.zeros_like(low)
    return jnp.concatenate(
        [low, jnp.where(norm, one, low), mid, jnp.where(norm, one, mid), top, jnp.where(norm, one, zero), zero, zero], 0
    ).astype(bf16)


def right_features(point):
    low, mid, top = pieces(point)
    norm = lax.broadcasted_iota(jnp.int32, point.shape, 0) == 3
    one = jnp.ones_like(low)
    zero = jnp.zeros_like(low)
    return jnp.concatenate(
        [
            jnp.where(norm, one, -2.0 * low),
            jnp.where(norm, low, -512.0 * mid),
            jnp.where(norm, 256.0 * one, -512.0 * low),
            jnp.where(norm, 256.0 * mid, -131072.0 * mid),
            jnp.where(norm, 65536.0 * one, zero),
            jnp.where(norm, 65536.0 * top, zero),
            zero,
            zero,
        ],
        0,
    ).astype(bf16)


def shape_of(radius):
    unit = 1.0 / (grid_step * radius)
    shift = 9.0 / (35.0 * unit)
    return {"reach": 1.0 / unit, "shift": shift, "bias": 3.0 / (35.0 * unit * unit) - shift * shift, "gain": 35.0 / 3.0 * unit**8}


def wendland(dist_sq, shape):
    dist = dist_sq * lax.rsqrt(jnp.maximum(dist_sq, 1.0))
    rest = jnp.maximum(shape["reach"] - dist, 0.0)
    rest_sq = rest * rest
    moved = dist + shape["shift"]
    return (rest_sq * rest_sq) * (rest_sq * (moved * moved + shape["bias"]))


def member(panel_at, block, pattern):
    first = panel_at * SNODE_BLOCKS
    own = (block >= first) & (block < first + SNODE_BLOCKS)
    return jnp.where(own, 1, jnp.where(block < first, 0, pattern[panel_at, block]))


def weight(row, col, pattern):
    value = (row == col).astype(jnp.int32)
    for panel_at in range(PANELS):
        value = value + member(panel_at, row, pattern) * member(panel_at, col, pattern)
    return value.astype(f32)


SCAN = 8
GROUP = 16
UNITS_BESIDE = 3
UNITS = 16 * UNITS_BESIDE
FIRSTS = 4
CHUNK = 4


def sums_kernel(shape, per, block_map, pattern, points, out, left, lists, weights):
    nblocks = points.shape[0]
    me = lax.axis_index("prow") * lax.axis_size("pcol") + lax.axis_index("pcol")
    own = [block_map[me * per + b] for b in range(per)]
    own_members = [[member(n, g, pattern) for n in range(PANELS)] for g in own]
    right = [right_features(points[me * per + b]) for b in range(per)]

    def scan_block(m, counts):
        left[m] = left_features(points[m])
        other = block_map[m]
        members = [member(n, other, pattern) for n in range(PANELS)]
        after = []
        for b in range(per):
            value = (own[b] == other).astype(jnp.int32)
            for n in range(PANELS):
                value = value + own_members[b][n] * members[n]
            lists[b, counts[b]] = m
            weights[b, counts[b]] = value.astype(f32) * shape["gain"]
            after.append(counts[b] + (value > 0).astype(jnp.int32))
        return tuple(after)

    def scan_blocks(step, counts):
        for n in range(SCAN):
            counts = scan_block(step * SCAN + n, counts)
        return counts

    counts = lax.fori_loop(0, nblocks // SCAN, scan_blocks, (0,) * per)
    for b in range(per):
        for g in range(GROUP):
            lists[b, counts[b] + g] = 0
            weights[b, counts[b] + g] = 0.0

    for b in range(per):

        def group(step, total):
            parts = []
            for g in range(GROUP):
                at = step * GROUP + g
                value = wendland(mm(left[lists[b, at]], right[b], TN), shape)
                parts.append(jnp.sum(value.reshape(BLOCK // 8, 8, BLOCK), axis=0) * weights[b, at])
            return total + functools.reduce(lambda x, y: x + y, parts)

        total = lax.fori_loop(0, (counts[b] + GROUP - 1) // GROUP, group, jnp.zeros((8, BLOCK), f32))
        row = jnp.sum(total, axis=0, keepdims=True)
        for d in range(out.shape[0]):
            out[d, b : b + 1, :] = row


def spread_kernel(per, coords, out):
    for b in range(per):
        point = coords[:, b * BLOCK : (b + 1) * BLOCK]
        norm = jnp.sum(point * point, axis=0, keepdims=True)
        point = jnp.concatenate([point, norm], 0)
        for d in range(out.shape[0]):
            out[d, b] = point


def panels_kernel(
    shape, rows_n, cols_n, block_map, pattern, points, totals, out,
    inverse, table, place, units, firsts, seconds, panel, high, low, left, right_lead, right_cols, scale_rows, scale_lead, scale_cols,
    diagonal, x_high, x_low, x_full, stage, sems, *work,
):
    nblocks = points.shape[0]
    row_count = nblocks // rows_n
    col_count = nblocks // cols_n
    prow_at = lax.axis_index("prow")
    pcol_at = lax.axis_index("pcol")
    col_base = row_count
    next_base = row_count + col_count
    lead_base = next_base + SNODE_BLOCKS
    slots = lead_base + SNODE_BLOCKS
    lead_rows = LEAD // rows_n

    def invert(step, carry):
        for n in range(SCAN):
            m = step * SCAN + n
            inverse[block_map[m]] = m
        return carry

    lax.fori_loop(0, nblocks // SCAN, invert, 0)

    def block_rows(slot):
        if isinstance(slot, int):
            return slice(slot * BLOCK, (slot + 1) * BLOCK)
        return pl.ds(pl.multiple_of(slot * BLOCK, BLOCK), BLOCK)

    def pair_rows(slot):
        return pl.ds(pl.multiple_of(slot * BLOCK, 2 * BLOCK), 2 * BLOCK)

    def chunk_rows(slot):
        return pl.ds(pl.multiple_of(slot * BLOCK, CHUNK * BLOCK), CHUNK * BLOCK)

    def scale_of(m):
        return scale_gain * lax.rsqrt(1.0 + totals[pl.ds(m, 1), :])

    def prepare(slot):
        m = inverse[table[slot]]
        left[slot] = left_features(points[m])
        scale_rows[slot] = jnp.broadcast_to(scale_of(m), (BLOCK, BLOCK)).T

    def prepare_lead(j):
        m = inverse[j]
        half, at = divmod(j, SNODE_BLOCKS)
        right_lead[j] = right_features(points[m])
        scale_lead[half, at : at + 1, :] = scale_of(m)

    def prepare_col(k):
        m = inverse[table[col_base + k]]
        right_cols[k // 2, :, k % 2 * BLOCK : (k % 2 + 1) * BLOCK] = right_features(points[m])
        scale_cols[k : k + 1, :] = scale_of(m)

    def coupled(slot, half, j):
        value = wendland(mm(left[slot], right_lead[half * SNODE_BLOCKS + j], TN), shape)
        scale = scale_lead[half, j : j + 1, :] * (weight(table[slot], half * SNODE_BLOCKS + j, pattern) * shape["gain"])
        return value * scale_rows[slot] * scale

    def couple(at, j):
        unit = units[at]
        slot = unit // 2
        half = unit % 2
        lanes = pl.ds(pl.multiple_of(half * WIDTH + j * BLOCK, BLOCK), BLOCK)
        panel[block_rows(slot), lanes] = coupled(slot, half, j)

    for j in range(SNODE_BLOCKS):
        table[next_base + j] = SNODE_BLOCKS + j
        table[lead_base + j] = j
    for j in range(SNODE_BLOCKS):
        prepare(lead_base + j)
        prepare_lead(j)
    for i in range(SNODE_BLOCKS):
        for j in range(SNODE_BLOCKS):
            if i < SNODE_BLOCKS // 2 <= j:
                continue
            value = coupled(lead_base + i, 0, j)
            diagonal[i * BLOCK : (i + 1) * BLOCK, j * BLOCK : (j + 1) * BLOCK] = value + eye(BLOCK) if i == j else value

    def sort(base, blocks):
        kinds = []
        first = second = jnp.int32(0)
        for g, at in blocks:
            in_first = member(0, g, pattern) > 0
            in_second = member(1, g, pattern) > 0
            dead = g < LEAD
            kind = jnp.where(dead, 2, jnp.where(in_first, 0, jnp.where(in_second, 1, 2)))
            kinds.append(kind)
            first = first + (kind == 0).astype(jnp.int32)
            second = second + (kind == 1).astype(jnp.int32)
        spots = [base, base + first, base + first + second]
        for (g, at), kind in zip(blocks, kinds):
            spot = jnp.where(kind == 0, spots[0], jnp.where(kind == 1, spots[1], spots[2]))
            table[spot] = g
            place[spot] = at
            for n in range(3):
                spots[n] = spots[n] + (kind == n).astype(jnp.int32)
        return first, first + second

    real_rows = row_count - lead_rows
    for i in range(lead_rows):
        table[real_rows + i] = i * rows_n + prow_at
        place[real_rows + i] = i
    rows_first, rows_both = sort(0, [(i * rows_n + prow_at, i) for i in range(lead_rows, row_count)])
    cols_first, cols_both = sort(col_base, [(k * cols_n + pcol_at, k) for k in range(col_count)])
    def whole(n):
        return (n + CHUNK - 1) // CHUNK * CHUNK

    count = jnp.int32(0)
    for base, size, ends in ((next_base, SNODE_BLOCKS, (SNODE_BLOCKS,) * PANELS), (0, row_count, (rows_first, rows_both)), (col_base, col_count, (cols_first, cols_both))):
        for at in range(size):
            for half in range(PANELS):
                units[count] = 2 * (base + at) + half
                used = jnp.int32(at < ends[half]) if base or at < real_rows else 1
                count = count + used
    for n in range(UNITS):
        units[count + n] = 2 * lead_base + 1

    def list_slots(rows, cols, out, chunks):
        count = jnp.int32(0)
        for base, size, end in ((0, row_count, rows), (col_base, col_count, cols)):
            for at in range(size):
                out[count] = base + at
                count = count + (1 if not base and at >= real_rows else (at < end).astype(jnp.int32))
        for n in range(CHUNK * chunks):
            out[count + n] = lead_base + n % CHUNK
        return whole(count) // CHUNK

    first_count = list_slots(rows_first, cols_first, firsts, FIRSTS + 1)
    second_count = list_slots(rows_both, cols_both, seconds, 1)

    def run(parts, count):
        for n in range(count):
            for part in parts[len(parts) * n // count : len(parts) * (n + 1) // count]:
                part()
            yield

    parts = [functools.partial(prepare_lead, j) for j in range(SNODE_BLOCKS, LEAD)]
    parts += [functools.partial(prepare, slot) for slot in range(lead_base)]
    parts += [functools.partial(prepare_col, k) for k in range(col_count)]

    def couple_beside(step, part):
        n = 2 * step + part
        for unit in range(UNITS_BESIDE):
            for j in range(SNODE_BLOCKS):
                couple(UNITS_BESIDE * n + unit, j)

    factor_diagonal(diagonal, x_full, work, run(parts, 20), 2, couple_beside)
    x_high[...], x_low[...] = split(x_full[...])

    def couple_more(step, carry):
        for n in range(4):
            for j in range(SNODE_BLOCKS):
                couple(UNITS + 4 * step + n, j)
        return carry

    lax.fori_loop(0, (jnp.maximum(count - UNITS, 0) + 3) // 4, couple_more, 0)
    rounded = (cols_first + 1) // 2 * 2, (cols_both + 1) // 2 * 2
    for base, ends, stops in (
        (0, (rows_first, rows_both), (jnp.minimum(whole(rows_first), real_rows), jnp.minimum(whole(rows_both), real_rows))),
        (col_base, (cols_first, cols_both), rounded),
    ):
        for half in range(PANELS):

            def clear(slot, carry, half=half):
                for ref in (high, low):
                    ref[block_rows(slot), half * WIDTH : (half + 1) * WIDTH] = jnp.zeros((BLOCK, WIDTH), bf16)
                return carry

            lax.fori_loop(base + ends[half], base + stops[half], clear, 0)
    for i in range(lead_rows):
        at = slice((real_rows + i) * BLOCK, (real_rows + i + 1) * BLOCK)
        lanes = pl.ds(pl.multiple_of((i * rows_n + prow_at) * BLOCK, BLOCK), BLOCK)
        panel[at, lanes] = panel[at, lanes] + eye(BLOCK)

    middle = WIDTH // 2

    def gather(ref, chunk, lanes):
        return jnp.concatenate([ref[block_rows(slot), lanes] for slot in chunk], 0)

    def solve(chunk, first):
        a_high, a_low = split(gather(panel, chunk, slice(first, first + WIDTH)))
        for begin, end in ((0, middle), (middle, WIDTH)):
            part = mm3(a_high[:, :end], a_low[:, :end], x_high[begin:end, :end], x_low[begin:end, :end], NT)
            lanes = slice(first + begin, first + end)
            for q, slot in enumerate(chunk):
                rows = part[q * BLOCK : (q + 1) * BLOCK]
                panel[block_rows(slot), lanes] = rows
                high[block_rows(slot), lanes], low[block_rows(slot), lanes] = split(rows)

    next_chunk = tuple(range(next_base, lead_base))
    solve(next_chunk, 0)

    def subtract(chunk, out_ref):
        a_high, a_low = gather(high, chunk, slice(0, WIDTH)), gather(low, chunk, slice(0, WIDTH))
        for lanes in (slice(0, middle), slice(middle, WIDTH)):
            rows = slice(next_base * BLOCK + lanes.start, next_base * BLOCK + lanes.stop)
            done = mm3(a_high, a_low, high[rows, :WIDTH], low[rows, :WIDTH], NT)
            from_at = slice(WIDTH + lanes.start, WIDTH + lanes.stop)
            for q, slot in enumerate(chunk):
                rest = panel[block_rows(slot), from_at] - done[q * BLOCK : (q + 1) * BLOCK]
                if out_ref is panel:
                    panel[block_rows(slot), from_at] = rest
                else:
                    out_ref[q * BLOCK : (q + 1) * BLOCK, lanes] = rest

    subtract(next_chunk, diagonal)
    for j in range(SNODE_BLOCKS):
        at = slice(j * BLOCK, (j + 1) * BLOCK)
        diagonal[at, at] = diagonal[at, at] + eye(BLOCK)

    def chunk_of(slots_ref, n):
        return tuple(slots_ref[CHUNK * n + q] for q in range(CHUNK))

    def first_solve(n):
        solve(chunk_of(firsts, n), 0)

    def first_subtract(n):
        subtract(chunk_of(firsts, n), panel)

    def first_beside(step, part):
        if part == 0:
            first_solve(step)
        if part == 2:
            first_subtract(step)

    factor_diagonal(diagonal, x_full, work, iter(()), 4, first_beside)

    def first_more(n, carry):
        first_solve(n)
        first_subtract(n)
        return carry

    lax.fori_loop(FIRSTS, first_count, first_more, 0)
    x_high[...], x_low[...] = split(x_full[...])
    def second(n, carry):
        solve(chunk_of(seconds, n), WIDTH)
        return carry

    lax.fori_loop(0, second_count, second, 0)
    for i in range(lead_rows):
        if i * rows_n < SNODE_BLOCKS:

            @pl.when(i * rows_n + prow_at < SNODE_BLOCKS)
            def _(i=i):
                panel[(real_rows + i) * BLOCK : (real_rows + i + 1) * BLOCK, WIDTH:] = jnp.zeros((BLOCK, WIDTH), f32)

    per_slot = BLOCK * col_count
    row_live = whole(rows_both) // CHUNK
    row_two = whole(rows_first) // CHUNK
    col_live = (cols_both + 1) // 2
    col_two = (cols_first + 1) // 2

    def copies_out(step, half):
        made = []
        for q in range(CHUNK):
            at = pl.multiple_of(place[CHUNK * step + q] * per_slot, per_slot)
            made.append(
                pltpu.make_async_copy(stage.at[half, pl.ds(q * per_slot, per_slot), :], out.at[pl.ds(at, per_slot), :], sems.at[half, q])
            )
        return made

    steps = row_count // CHUNK

    def trail(step, carry):
        half = step % 2

        @pl.when(step >= 2)
        def _():
            for copy in copies_out(step - 2, half):
                copy.wait()

        def spots(q, k):
            return pl.ds(q * per_slot + k, BLOCK, stride=col_count)

        def tiles(c, carry):
            live = (step < row_live) & (c < col_live)
            two = (step < row_two) & (c < col_two)
            row_at = chunk_rows(CHUNK * step)
            col_at = pair_rows(col_base + 2 * c)

            def body(first):
                tiles = []
                for q in range(CHUNK):
                    slot = CHUNK * step + q
                    value = wendland(mm(left[slot], right_cols[c], TN), shape)
                    for e in range(2):
                        spot = col_base + 2 * c + e
                        factor = scale_cols[pl.ds(2 * c + e, 1), :] * (weight(table[slot], table[spot], pattern) * shape["gain"])
                        tiles.append(value[:, e * BLOCK : (e + 1) * BLOCK] * scale_rows[slot] * factor)
                update = mm3(high[row_at, first:], low[row_at, first:], high[col_at, first:], low[col_at, first:], NT)
                for q in range(CHUNK):
                    for e in range(2):
                        spot = col_base + 2 * c + e
                        tile = tiles[2 * q + e] - update[q * BLOCK : (q + 1) * BLOCK, e * BLOCK : (e + 1) * BLOCK]
                        stage[half, spots(q, place[spot]), :] = tile

            @pl.when(live & two)
            def _():
                body(0)

            @pl.when(live & jnp.logical_not(two))
            def _():
                body(WIDTH)

            @pl.when(jnp.logical_not(live))
            def _():
                for q in range(CHUNK):
                    for e in range(2):
                        stage[half, spots(q, place[col_base + 2 * c + e]), :] = jnp.zeros((BLOCK, BLOCK), f32)

            return carry

        lax.fori_loop(0, col_count // 2, tiles, 0)

        @pl.when(step == steps - 1)
        def _():
            for q in range(CHUNK - lead_rows, CHUNK):
                for k in range(col_count):
                    stage[half, spots(q, k), :] = jnp.zeros((BLOCK, BLOCK), f32)

        for q in range(CHUNK):
            slot = CHUNK * step + q
            g = table[slot]
            k_same = g // cols_n
            here = (k_same * cols_n + pcol_at == g) & (g >= LEAD)
            same = spots(q, k_same)

            @pl.when(here & (slot >= rows_both))
            def _(slot=slot, g=g, same=same):
                m = inverse[g]
                value = wendland(mm(left[slot], right_features(points[m]), TN), shape)
                factor = scale_gain * lax.rsqrt(1.0 + totals[pl.ds(m, 1), :]) * (weight(g, g, pattern) * shape["gain"])
                stage[half, same, :] = value * scale_rows[slot] * factor

            @pl.when(here)
            def _(same=same):
                stage[half, same, :] = stage[half, same, :] + eye(BLOCK)

            for k in range(col_count):
                if k * cols_n < LEAD:
                    j = k * cols_n + pcol_at

                    filled = (slot < jnp.where(j < SNODE_BLOCKS, rows_first, rows_both)) | (slot >= real_rows)

                    @pl.when((j < LEAD) & filled)
                    def _(k=k, j=j, q=q, slot=slot):
                        where = pl.ds(pl.multiple_of(j * BLOCK, BLOCK), BLOCK)
                        stage[half, spots(q, k), :] = panel[block_rows(slot), where]

                    @pl.when((j < LEAD) & jnp.logical_not(filled))
                    def _(k=k, q=q):
                        stage[half, spots(q, k), :] = jnp.zeros((BLOCK, BLOCK), f32)

        for copy in copies_out(step, half):
            copy.start()
        return carry

    lax.fori_loop(0, steps, trail, 0)
    for step in range(max(steps - 2, 0), steps):
        for copy in copies_out(step, step % 2):
            copy.wait()


def local(coords, block_map, pattern):
    rows_n = lax.axis_size("prow")
    cols_n = lax.axis_size("pcol")
    devices = rows_n * cols_n
    nblocks = block_map.shape[0]
    per = nblocks // devices
    row_count = nblocks // rows_n
    col_count = nblocks // cols_n
    radius = (spread_factor / (nblocks * BLOCK)) ** (1.0 / 3.0)
    slots = row_count + col_count + LEAD
    rows_kept = (slots - SNODE_BLOCKS + CHUNK) * BLOCK
    axes = ("prow", "pcol")
    smem = pl.BlockSpec(memory_space=pltpu.SMEM)
    vmem = pl.BlockSpec(memory_space=pltpu.VMEM)
    params = pltpu.CompilerParams(vmem_limit_bytes=VMEM_BYTES)
    shape = shape_of(radius)
    mine = pl.pallas_call(
        functools.partial(spread_kernel, per),
        out_shape=jax.ShapeDtypeStruct((devices, per, 4, BLOCK), jnp.int32),
        in_specs=[vmem],
        out_specs=vmem,
        name="spread",
    )(coords)
    points = lax.all_to_all(mine, axes, 0, 0, tiled=True).reshape(nblocks, 4, BLOCK)
    sums = pl.pallas_call(
        functools.partial(sums_kernel, shape, per),
        out_shape=jax.ShapeDtypeStruct((devices, per, BLOCK), f32),
        in_specs=[smem, smem, vmem],
        out_specs=vmem,
        scratch_shapes=[
            pltpu.VMEM((nblocks, FEATURES, BLOCK), bf16),
            pltpu.SMEM((per, nblocks + GROUP), jnp.int32),
            pltpu.SMEM((per, nblocks + GROUP), f32),
        ],
        compiler_params=params,
        name="sums",
    )(block_map, pattern, points)
    totals = lax.all_to_all(sums, axes, 0, 0, tiled=True).reshape(nblocks, BLOCK)
    out = pl.pallas_call(
        functools.partial(panels_kernel, shape, rows_n, cols_n),
        out_shape=jax.ShapeDtypeStruct((row_count * BLOCK * col_count, BLOCK), f32),
        in_specs=[smem, smem, vmem, vmem],
        out_specs=pl.BlockSpec(memory_space=pl.ANY),
        scratch_shapes=[
            pltpu.SMEM((nblocks,), jnp.int32),
            pltpu.SMEM((slots,), jnp.int32),
            pltpu.SMEM((slots,), jnp.int32),
            pltpu.SMEM((2 * slots + UNITS,), jnp.int32),
            pltpu.SMEM((slots + CHUNK * (FIRSTS + 1),), jnp.int32),
            pltpu.SMEM((slots + CHUNK,), jnp.int32),
            pltpu.VMEM((rows_kept, PANELS * WIDTH), f32),
            pltpu.VMEM((rows_kept, PANELS * WIDTH), bf16),
            pltpu.VMEM((rows_kept, PANELS * WIDTH), bf16),
            pltpu.VMEM((slots, FEATURES, BLOCK), bf16),
            pltpu.VMEM((LEAD, FEATURES, BLOCK), bf16),
            pltpu.VMEM((col_count // 2, FEATURES, 2 * BLOCK), bf16),
            pltpu.VMEM((slots, BLOCK, BLOCK), f32),
            pltpu.VMEM((PANELS, SNODE_BLOCKS, BLOCK), f32),
            pltpu.VMEM((col_count, BLOCK), f32),
            pltpu.VMEM((WIDTH, WIDTH), f32),
            pltpu.VMEM((WIDTH, WIDTH), bf16),
            pltpu.VMEM((WIDTH, WIDTH), bf16),
            pltpu.VMEM((WIDTH, WIDTH), f32),
            pltpu.VMEM((2, CHUNK * BLOCK * col_count, BLOCK), f32),
            pltpu.SemaphoreType.DMA((2, CHUNK)),
        ]
        + [pltpu.VMEM((BLOCK, 2 * BLOCK), f32)] * 4,
        compiler_params=params,
        name="panels",
    )(block_map, pattern, points, totals)
    return out.reshape(row_count, 1, BLOCK, col_count, 1, BLOCK)


def solution(mesh):
    placed = (P(None, ("prow", "pcol")), P(), P())
    return jax.shard_map(
        local,
        mesh=mesh,
        in_specs=placed,
        out_specs=P(None, "prow", None, None, "pcol", None),
        check_vma=False,
    )
```
